32 devices in a mesh: dp: 8 (over y, x, core), tensor: 4 (over z).
Axes of the slice: x: 2, y: 2, z: 4, core: 2. Of those that a mesh axis runs over, the one named last changes fastest.
Arguments:
- tokens: bfloat16 [8192, 768], P(('dp', 'tensor')), may hold values from -6 to 6
- lengths: int32 [8, 7], P('dp'), may hold values from 0 to 896, as said below
- query_weight: bfloat16 [768, 768], P(None, 'tensor'), may hold values from -0.109375 to 0.109375
- query_bias: float32 [768], P('tensor'), may hold values from -3 to 3
- key_weight: bfloat16 [768, 768], P(None, 'tensor'), may hold values from -0.109375 to 0.109375
- key_bias: float32 [768], P('tensor'), may hold values from -3 to 3
- value_weight: bfloat16 [768, 768], P(None, 'tensor'), may hold values from -0.21875 to 0.21875
- value_bias: float32 [768], P('tensor'), may hold values from -3 to 3
- feature_proj: bfloat16 [12, 64, 256], P('tensor'), may hold values from -4 to 4
- mixer_weight: bfloat16 [768, 768], P('tensor'), may hold values from -0.875 to 0.875
- mixer_bias: float32 [768], replicated, may hold values from -3 to 3
- first_gain: float32 [768], replicated, may hold values from 0.5 to 1.5
- first_shift: float32 [768], replicated, may hold values from -3 to 3
- hidden_weight: bfloat16 [768, 3072], P(None, 'tensor'), may hold values from -0.21875 to 0.21875
- hidden_bias: float32 [3072], P('tensor'), may hold values from -3 to 3
- output_weight: bfloat16 [3072, 768], P('tensor'), may hold values from -0.109375 to 0.109375
- output_bias: float32 [768], replicated, may hold values from -3 to 3
- second_gain: float32 [768], replicated, may hold values from 0.5 to 1.5
- second_shift: float32 [768], replicated, may hold values from -3 to 3
- cotangent: bfloat16 [8192, 768], P(('dp', 'tensor')), may hold values from -6 to 6
Outputs:
- layer_out: bfloat16 [8192, 768], P(('dp', 'tensor'))
- tokens_grad: float32 [8192, 768], P(('dp', 'tensor'))
- grad_query_weight: float32 [768, 768], P('dp', 'tensor')
- grad_query_bias: float32 [768], replicated
- grad_key_weight: float32 [768, 768], P('dp', 'tensor')
- grad_key_bias: float32 [768], replicated
- grad_value_weight: float32 [768, 768], P('dp', 'tensor')
- grad_value_bias: float32 [768], replicated
- grad_mixer_weight: float32 [768, 768], P('tensor', 'dp')
- grad_mixer_bias: float32 [768], replicated
- grad_first_gain: float32 [768], replicated
- grad_first_shift: float32 [768], replicated
- grad_hidden_weight: float32 [768, 3072], P('dp', 'tensor')
- grad_hidden_bias: float32 [3072], replicated
- grad_output_weight: float32 [3072, 768], P('tensor', 'dp')
- grad_output_bias: float32 [768], replicated
- grad_second_gain: float32 [768], replicated
- grad_second_shift: float32 [768], replicated
The draws below stay inside these ranges and needn't reach their ends.
Inputs may be any that keep to these rules, and one draw needn't show every extreme that they name: lengths[r, 0] to lengths[r, 5] are the lengths of the sequences packed in order into row r (0 is an empty slot) and lengths[r, 6] the padding at the row's end; each row sums to 1024; some row holds a sequence of exactly 896 positions.
All inputs are finite; a program needn't handle non-finite values.
Results may differ from the reference program's by a relative error of at most 0.035.
Values may be sent and summed in bfloat16 or wider, within the bound.
No kernel may reach another device: no remote copies, remote signals or barrier semaphores. Data moves between devices by JAX's collectives and lax.ppermute only.
A program may use at most 192 MiB of HBM per device.

```python
import math
from functools import partial
import jax
import jax.numpy as jnp
from jax import lax

D = 768
HEADS = 12
HEAD_DIM = 64
FF = 3072
FEAT = 256
SEQS = 6
ROW = 1024
ROWS = 8
TOKENS = 8192
LMAX = 896


def draw_lengths(key, part):
    key_pad, key_expo, key_row = jax.random.split(key, 3)
    padding = jax.random.randint(key_pad, (ROWS,), 0, ROW // 4)
    live_count = ROW - padding
    expo = jax.random.randint(key_expo, (ROWS, SEQS), 0, 7)
    weights = jnp.left_shift(jnp.ones_like(expo), expo)
    weight_sum = jnp.sum(weights, axis=1, keepdims=True)
    shares = live_count[:, None] * weights // weight_sum
    shares = shares.at[:, 0].add(live_count - jnp.sum(shares, axis=1))
    shares = jnp.minimum(shares, LMAX - 1)
    rest = ROW - LMAX
    tail_weights = weights[0, 1:]
    tail = rest * tail_weights // jnp.sum(tail_weights)
    tail = tail.at[0].add(rest - jnp.sum(tail))
    long_row = jnp.concatenate([jnp.full((1,), LMAX, jnp.int32), tail.astype(jnp.int32)])
    chosen = jax.random.randint(key_row, (), 0, ROWS)
    is_long = (jnp.arange(ROWS, dtype=jnp.int32) == chosen)[:, None]
    seq_part = jnp.where(is_long, long_row[None, :], shares.astype(jnp.int32))
    pad_part = ROW - jnp.sum(seq_part, axis=1)
    return jnp.concatenate([seq_part, pad_part[:, None]], axis=1).astype(jnp.int32)


def spiked(entries, key, source, target, parts, factor):
    def block_of(position):
        return (jnp.arange(entries.shape[position]) // (entries.shape[position] // parts)).reshape((-1,) + (1,) * (entries.ndim - 1 - position))

    one_side = jax.random.permutation(key, parts)[block_of(target)]
    second = (block_of(target) + parts // 2) % parts
    return jnp.where((block_of(source) == one_side) | (block_of(source) == second), factor * entries, entries)


def block_scale(rng, dims, cuts, least, high):
    factor_of, own = 1.0, jax.random.fold_in(rng, 6)
    for axis_at, blocks in cuts:
        heights = jnp.exp(jax.random.uniform(jax.random.fold_in(own, axis_at), (blocks,), jnp.float32, least / len(cuts), high / len(cuts)))
        factor_of = factor_of * jnp.repeat(heights, dims[axis_at] // blocks).reshape([-1 if axis == axis_at else 1 for axis in range(len(dims))])
    return factor_of


def bell_draw(rng, shape, deviation, reach, cuts=(), kind=jnp.bfloat16):
    entries = deviation * jax.random.normal(rng, shape, jnp.float32)
    if cuts:
        entries = entries * block_scale(rng, shape, cuts, -0.22, 0.18)
    return jnp.clip(entries, -reach, reach).astype(kind)


def heavy_noise(own_key, shape, width, bound, cuts, heavy, kind=jnp.bfloat16):
    array = width * jax.random.normal(own_key, shape, jnp.float32)
    if cuts:
        array = array * block_scale(own_key, shape, cuts, -0.22, 0.18)
    return jnp.clip(spiked(array, jax.random.fold_in(own_key, 3), *heavy), -bound, bound).astype(kind)


def setup_inputs(seed: int = 0) -> dict:
    key_of = jax.random.split(jax.random.key(seed), 21)
    return {
        "tokens": heavy_noise(key_of[0], (TOKENS, D), 1.0, 6.0, ((0, 32),), (0, 1, 32, 2.75)),
        "lengths": draw_lengths(jax.random.fold_in(key_of[20], 71), 0),
        "query_weight": bell_draw(key_of[2], (D, D), (4 * D) ** -0.5, 0.109375, ((1, 4),)),
        "query_bias": bell_draw(key_of[3], (D,), 0.5, 3.0, ((0, 4),), jnp.float32),
        "key_weight": bell_draw(key_of[4], (D, D), (4 * D) ** -0.5, 0.109375, ((1, 4),)),
        "key_bias": bell_draw(key_of[5], (D,), 0.5, 3.0, ((0, 4),), jnp.float32),
        "value_weight": bell_draw(key_of[6], (D, D), D ** -0.5, 0.21875, ((1, 4),)),
        "value_bias": bell_draw(key_of[7], (D,), 0.5, 3.0, ((0, 4),), jnp.float32),
        "feature_proj": bell_draw(key_of[8], (HEADS, HEAD_DIM, FEAT), 1.0, 4.0, ((0, 4),)),
        "mixer_weight": bell_draw(key_of[9], (D, D), (D // 16) ** -0.5, 0.875, ((0, 4),)),
        "mixer_bias": bell_draw(key_of[10], (D,), 0.5, 3.0, (), jnp.float32),
        "first_gain": jnp.clip(1.0 + 0.1 * jax.random.normal(key_of[11], (D,), jnp.float32), 0.5, 1.5),
        "first_shift": bell_draw(key_of[12], (D,), 0.5, 3.0, (), jnp.float32),
        "hidden_weight": bell_draw(key_of[13], (D, FF), D ** -0.5, 0.21875, ((1, 4),)),
        "hidden_bias": bell_draw(key_of[14], (FF,), 0.5, 3.0, ((0, 4),), jnp.float32),
        "output_weight": bell_draw(key_of[15], (FF, D), FF ** -0.5, 0.109375, ((0, 4),)),
        "output_bias": bell_draw(key_of[16], (D,), 0.5, 3.0, (), jnp.float32),
        "second_gain": jnp.clip(1.0 + 0.1 * jax.random.normal(key_of[17], (D,), jnp.float32), 0.5, 1.5),
        "second_shift": bell_draw(key_of[18], (D,), 0.5, 3.0, (), jnp.float32),
        "cotangent": heavy_noise(key_of[19], (TOKENS, D), 1.0, 6.0, ((0, 32),), (0, 1, 32, 2.75)),
    }


HIGH = lax.Precision.HIGHEST
eps = 1e-06

@jax.custom_vjp
def low(v):
    return lax.optimization_barrier(v.astype(jnp.bfloat16)).astype(jnp.float32)

@jax.custom_vjp
def low_back(v):
    return v

def low_keep(v):
    return (low(v), None)

def low_pass(kept, grad):
    return (grad,)

def back_keep(v):
    return (v, None)

def back_low(kept, grad):
    return (low(grad),)
low.defvjp(low_keep, low_pass)
low_back.defvjp(back_keep, back_low)

def segment_table(row_lengths, row_count):
    seq_lengths = row_lengths[:-1].astype(jnp.int32)
    ends = jnp.cumsum(seq_lengths).astype(jnp.int32)
    starts = ends - seq_lengths
    places = jnp.arange(row_count, dtype=jnp.int32)[:, None]
    inside = (places >= starts[None, :]) & (places < ends[None, :])
    return inside.astype(jnp.float32)

def layer_norm(resid, gain, shift):
    center = resid - lax.optimization_barrier(jnp.mean(resid, axis=-1, keepdims=True))
    return center * lax.rsqrt(lax.optimization_barrier(jnp.mean(center * center, axis=-1, keepdims=True)) + eps) * gain + shift

def project(left, right):
    return jnp.dot(left, right, precision=HIGH, preferred_element_type=jnp.float32)

def feature_map(vectors, proj_w):
    scale = HEAD_DIM ** (-0.25)
    proj = low_back(scale * jnp.einsum('rhd,hdf->rhf', vectors, proj_w, precision=HIGH))
    square = 0.5 * scale * scale * lax.optimization_barrier(jnp.sum(vectors * vectors, axis=-1, keepdims=True))
    return low(jnp.exp(proj - square) / math.sqrt(FEAT))

def head_attend(inputs, table, live):
    q_feat, k_feat, values = inputs
    state = low_back(low(jnp.einsum('ts,tf,td->sfd', table, k_feat, values, precision=HIGH)))
    key_sum = jnp.einsum('ts,tf->sf', table, k_feat, precision=HIGH)
    numer = low_back(jnp.einsum('ts,tf,sfd->td', table, q_feat, state, precision=HIGH))
    denom = jnp.einsum('ts,tf,sf->t', table, q_feat, key_sum, precision=HIGH) + (1.0 - live)
    return numer / denom[:, None]

def row_forward(inputs, params, proj_w):
    row_tokens, table = inputs
    w_query, b_query, w_key, b_key, w_value, b_value, w_mixer, b_mixer, g_first, s_first, w_hidden, b_hidden, w_output, b_output, g_second, s_second = params
    row_count = row_tokens.shape[0]
    queries = low_back(low(project(row_tokens, w_query) + b_query)).reshape(row_count, HEADS, HEAD_DIM)
    keys = low_back(low(project(row_tokens, w_key) + b_key)).reshape(row_count, HEADS, HEAD_DIM)
    values = low_back(low(project(row_tokens, w_value) + b_value)).reshape(row_count, HEADS, HEAD_DIM)
    q_feat = feature_map(queries, proj_w)
    k_feat = feature_map(keys, proj_w)
    live = lax.optimization_barrier(jnp.sum(table, axis=1))
    attend = jax.checkpoint(partial(head_attend, table=table, live=live))
    heads_out = lax.map(attend, (q_feat.transpose(1, 0, 2), k_feat.transpose(1, 0, 2), values.transpose(1, 0, 2)))
    mixed = low_back(low(heads_out.transpose(1, 0, 2).reshape(row_count, D)))
    branch = low_back(project(mixed, w_mixer) + b_mixer)
    first = layer_norm(row_tokens + branch, g_first, s_first)
    first_low = low(first)
    hidden_pre = low_back(project(first_low, w_hidden) + b_hidden)
    hidden_act = low(jax.nn.gelu(hidden_pre, approximate=False))
    ffn = low_back(project(hidden_act, w_output) + b_output)
    return layer_norm(first + ffn, g_second, s_second)

def reference(tokens, lengths, query_weight, query_bias, key_weight, key_bias, value_weight, value_bias, feature_proj, mixer_weight, mixer_bias, first_gain, first_shift, hidden_weight, hidden_bias, output_weight, output_bias, second_gain, second_shift, cotangent):
    params = tuple((a.astype(jnp.float32) for a in (query_weight, query_bias, key_weight, key_bias, value_weight, value_bias, mixer_weight, mixer_bias, first_gain, first_shift, hidden_weight, hidden_bias, output_weight, output_bias, second_gain, second_shift)))
    proj_w = feature_proj.astype(jnp.float32)
    tables = jax.vmap(partial(segment_table, row_count=ROW))(lengths)

    def forward(token_vals, *weights):
        shaped = token_vals.reshape(ROWS, ROW, D)
        step_fn = jax.checkpoint(partial(row_forward, params=weights, proj_w=proj_w))
        result = lax.map(step_fn, (shaped, tables))
        return result.reshape(ROWS * ROW, D)
    result, pull = jax.vjp(forward, tokens.astype(jnp.float32), *params)
    grads = pull(cotangent.astype(jnp.float32))
    return (result.astype(jnp.bfloat16), grads[0], grads[1], grads[2], grads[3], grads[4], grads[5], grads[6], grads[7], grads[8], grads[9], grads[10], grads[11], grads[12], grads[13], grads[14], grads[15], grads[16])
```

```python
import math

import jax
import jax.numpy as jnp
from jax import lax
from jax.sharding import PartitionSpec as P

D = 768
HEAD_DIM = 64
FF = 3072
FEAT = 256
PLANE = 8

eps = 1e-06
contract_rows = (((0,), (0,)), ((), ()))
contract_cols = (((1,), (1,)), ((), ()))
bf16 = jnp.bfloat16
f32 = jnp.float32


def dot(left, right):
    return jnp.dot(left, right, preferred_element_type=f32)


def dot_rows(left, right):
    return lax.dot_general(left, right, contract_rows, preferred_element_type=f32)


def dot_cols(left, right):
    return lax.dot_general(left, right, contract_cols, preferred_element_type=f32)


def split(wide):
    high = wide.astype(bf16)
    return high, (wide - high.astype(f32)).astype(bf16)


def swap(values, mask):
    size = lax.axis_size("dp")
    return lax.ppermute(values, "dp", [(i, i ^ mask) for i in range(size)])


def shift(values, step):
    size = lax.axis_size("tensor")
    return lax.ppermute(values, "tensor", [(i, (i + step) % size) for i in range(size)])


def segment_table(row_lengths, row_count):
    seq_lengths = row_lengths[:-1]
    count = seq_lengths.shape[0]
    order = jnp.arange(count, dtype=jnp.int32)
    ends = jnp.sum(
        jnp.where(order[None, :] <= order[:, None], seq_lengths[None, :], 0), axis=1
    )
    starts = ends - seq_lengths
    places = jnp.arange(row_count, dtype=jnp.int32)[:, None]
    inside = (places >= starts[None, :]) & (places < ends[None, :])
    return inside.astype(f32)


def layer_norm(resid, gain, shift_by):
    center = resid - jnp.mean(resid, axis=-1, keepdims=True)
    inverse = lax.rsqrt(jnp.mean(center * center, axis=-1, keepdims=True) + eps)
    normed = center * inverse
    return (normed * gain + shift_by, normed, inverse)


def norm_back(grad_out, normed, inverse, gain):
    scaled = grad_out * gain
    return inverse * (
        scaled
        - jnp.mean(scaled, axis=-1, keepdims=True)
        - normed * jnp.mean(scaled * normed, axis=-1, keepdims=True)
    )


def spread(table_low, entries):
    outer = table_low[:, :, None] * entries[:, None, :]
    return outer.reshape(entries.shape[0], -1)


def collect(table, wide):
    shaped = wide.reshape(table.shape[0], table.shape[1], -1)
    return jnp.sum(shaped * table[:, :, None], axis=1)


def feature_map(vectors, proj_w):
    scale = HEAD_DIM ** (-0.25)
    widened = vectors.astype(f32)
    square = 0.5 * scale * scale * jnp.sum(widened * widened, axis=-1, keepdims=True)
    full_feat = jnp.exp(scale * dot(vectors, proj_w) - square) / math.sqrt(FEAT)
    return full_feat.astype(bf16)


def feature_back(grad_feat, feat, vectors, proj_w):
    scale = HEAD_DIM ** (-0.25)
    grad_proj = grad_feat * feat.astype(f32)
    pulled = scale * dot_cols(grad_proj.astype(bf16), proj_w)
    return pulled - scale * scale * vectors.astype(f32) * jnp.sum(
        grad_proj, axis=1, keepdims=True
    )


def head_forward(query, key, value, proj_w, table, table_low, dead):
    q_feat = feature_map(query, proj_w)
    k_feat = feature_map(key, proj_w)
    state = dot_rows(k_feat, spread(table_low, value)).astype(bf16)
    key_high, key_low = split(dot_rows(k_feat, table_low))
    numer = collect(table, dot(q_feat, state))
    scores = dot(q_feat, key_high) + dot(q_feat, key_low)
    denom = jnp.sum(table * scores, axis=1, keepdims=True) + dead
    return numer / denom, (q_feat, k_feat, state, key_high, key_low, denom)


def head_backward(grad_head, out_head, query, key, value, proj_w, saved, table, table_low):
    q_feat, k_feat, state, key_high, key_low, denom = saved
    grad_wide = grad_head.astype(f32)
    grad_numer = spread(table_low, (grad_wide / denom).astype(bf16))
    grad_denom = table * (-jnp.sum(grad_wide * out_head, axis=1, keepdims=True) / denom)
    den_high, den_low = split(grad_denom)
    grad_state = dot_rows(q_feat, grad_numer).astype(bf16)
    sum_high, sum_low = split(dot_rows(q_feat, den_high) + dot_rows(q_feat, den_low))
    grad_qfeat = (
        dot_cols(grad_numer, state)
        + dot_cols(den_high, key_high)
        + dot_cols(den_low, key_high)
        + dot_cols(den_high, key_low)
    )
    grad_kfeat = (
        dot_cols(spread(table_low, value), grad_state)
        + dot_cols(table_low, sum_high)
        + dot_cols(table_low, sum_low)
    )
    grad_value = collect(table, dot(k_feat, grad_state))
    return (
        feature_back(grad_qfeat, q_feat, query, proj_w),
        feature_back(grad_kfeat, k_feat, key, proj_w),
        grad_value,
    )


def gather_weights(parts):
    own = lax.axis_index("dp") % PLANE
    slices = [
        lax.dynamic_slice_in_dim(part, own * (part.shape[0] // PLANE), part.shape[0] // PLANE, 0)
        for part in parts
    ]
    payload = jnp.concatenate(slices, axis=0)
    shards = lax.axis_size("tensor")
    stack = jnp.stack([payload] + [shift(payload, s) for s in range(1, shards)])
    held = {0: stack}
    for mask in (2, 4, 6):
        held[mask] = swap(stack, mask)
    for mask in (0, 2, 4, 6):
        held[mask + 1] = swap(held[mask], 1)
    whole = []
    begin = 0
    for part in slices:
        height, width = part.shape
        buffer = jnp.zeros((shards, PLANE, height, width), part.dtype)
        for mask in range(PLANE):
            buffer = lax.dynamic_update_slice(
                buffer, held[mask][:, None, begin : begin + height], (0, own ^ mask, 0, 0)
            )
        whole.append(buffer.reshape(shards, PLANE * height, width))
        begin += height
    return whole


def scatter_plane(grads):
    size = lax.axis_size("dp")
    axis = grads.ndim - 2
    if size != PLANE:
        return lax.psum_scatter(grads, "dp", scatter_dimension=axis, tiled=True)
    own = lax.axis_index("dp")
    height = grads.shape[axis] // size

    def block(mask):
        return lax.dynamic_slice_in_dim(grads, (own ^ mask) * height, height, axis)

    far = swap(jnp.stack([block(mask + 1) for mask in (0, 2, 4, 6)]), 1)
    near = [(block(mask).astype(f32) + far[mask // 2].astype(f32)).astype(bf16) for mask in (0, 2, 4, 6)]
    total = near[0].astype(f32)
    for mask in (2, 4, 6):
        total = total + swap(near[mask // 2], mask).astype(f32)
    return total.astype(bf16)


def scatter_shards(grads):
    total = grads[0].astype(f32)
    for s in range(1, grads.shape[0]):
        total = total + shift(grads[s], -s).astype(f32)
    return total


def small_sum(values):
    size = lax.axis_size("dp")
    if size != PLANE:
        return lax.psum(values, ("dp", "tensor"))
    values = values + swap(values, 1)
    values = values + swap(values, 2) + swap(values, 4) + swap(values, 6)
    total = values
    for s in range(1, lax.axis_size("tensor")):
        total = total + shift(values, s)
    return total


def body(
    tokens,
    lengths,
    query_weight,
    query_bias,
    key_weight,
    key_bias,
    value_weight,
    value_bias,
    feature_proj,
    mixer_weight,
    mixer_bias,
    first_gain,
    first_shift,
    hidden_weight,
    hidden_bias,
    output_weight,
    output_bias,
    second_gain,
    second_shift,
    cotangent,
):
    local_rows = tokens.shape[0]
    shards = lax.axis_size("tensor")
    place = lax.axis_index("tensor")
    all_rows = local_rows * shards
    width = query_weight.shape[1]
    head_count = width // HEAD_DIM
    table = segment_table(lengths[0], all_rows)
    table_low = table.astype(bf16)
    dead = 1.0 - jnp.sum(table, axis=1, keepdims=True)

    gathered = lax.all_gather(tokens, "tensor", axis=0, tiled=True)
    all_bias = lax.all_gather(hidden_bias, "tensor", axis=0, tiled=False)
    mixer_all, hidden_all = gather_weights([mixer_weight, hidden_weight])
    (output_all,) = gather_weights([output_weight])

    qkv_weight = jnp.concatenate([query_weight, key_weight, value_weight], axis=1)
    qkv_bias = jnp.concatenate([query_bias, key_bias, value_bias])
    qkv = (dot(gathered, qkv_weight) + qkv_bias).astype(bf16)

    def head_of(array, kind, h):
        begin = kind * width + h * HEAD_DIM
        return array[:, begin : begin + HEAD_DIM]

    kept = [
        head_forward(
            head_of(qkv, 0, h), head_of(qkv, 1, h), head_of(qkv, 2, h), feature_proj[h], table, table_low, dead
        )
        for h in range(head_count)
    ]
    mixed = jnp.concatenate([entry[0] for entry in kept], axis=1)
    mixed_low = mixed.astype(bf16)

    def rows_of(array, owner):
        return lax.dynamic_slice_in_dim(array, owner * local_rows, local_rows, 0)

    pieces = [rows_of(mixed_low, place)] + [
        shift(rows_of(mixed_low, (place + s) % shards), s) for s in range(1, shards)
    ]
    branch = mixer_bias + sum(dot(pieces[s], mixer_all[s]) for s in range(shards))
    first, normed_one, inverse_one = layer_norm(tokens.astype(f32) + branch, first_gain, first_shift)
    first_low = first.astype(bf16)
    acts = []
    slopes = []
    ffn = output_bias
    for s in range(shards):
        bias = lax.dynamic_index_in_dim(all_bias, (place - s) % shards, 0, keepdims=False)
        pre = dot(first_low, hidden_all[s]) + bias
        phi = 0.5 * (1.0 + lax.erf(pre * math.sqrt(0.5)))
        slopes.append(phi + pre * jnp.exp(-0.5 * pre * pre) * (1.0 / math.sqrt(2.0 * math.pi)))
        acts.append((pre * phi).astype(bf16))
        ffn = ffn + dot(acts[s], output_all[s])
    layer, normed_two, inverse_two = layer_norm(first + ffn, second_gain, second_shift)
    layer_out = layer.astype(bf16)
    grad_out = cotangent.astype(f32)
    grad_second_gain = jnp.sum(grad_out * normed_two, axis=0)
    grad_second_shift = jnp.sum(grad_out, axis=0)
    grad_resid_two = norm_back(grad_out, normed_two, inverse_two, second_gain)
    grad_ffn = grad_resid_two.astype(bf16)
    grad_output_bias = jnp.sum(grad_ffn.astype(f32), axis=0)
    grad_output = scatter_plane(
        jnp.stack([dot_rows(grad_ffn, acts[s]).astype(bf16) for s in range(shards)])
    )
    grad_pre = [
        (dot_cols(grad_ffn, output_all[s]) * slopes[s]).astype(bf16) for s in range(shards)
    ]
    grad_hidden_bias = jnp.stack([jnp.sum(entry.astype(f32), axis=0) for entry in grad_pre])
    grad_first = grad_resid_two + sum(dot_cols(grad_pre[s], hidden_all[s]) for s in range(shards))
    grad_hidden = scatter_plane(
        jnp.stack([dot_rows(first_low, grad_pre[s]).astype(bf16) for s in range(shards)])
    )
    grad_first_gain = jnp.sum(grad_first * normed_one, axis=0)
    grad_first_shift = jnp.sum(grad_first, axis=0)
    grad_resid_one = norm_back(grad_first, normed_one, inverse_one, first_gain)
    grad_branch = grad_resid_one.astype(bf16)
    grad_mixer_bias = jnp.sum(grad_branch.astype(f32), axis=0)
    grad_mixer = scatter_plane(
        jnp.stack([dot_rows(grad_branch, pieces[s]).astype(bf16) for s in range(shards)])
    )
    back = [dot_cols(grad_branch, mixer_all[s]).astype(bf16) for s in range(shards)]
    back = [back[0]] + [shift(back[s], -s) for s in range(1, shards)]
    back = jnp.concatenate(back + back[:-1], axis=0)
    grad_heads = lax.dynamic_slice_in_dim(back, ((shards - place) % shards) * local_rows, all_rows, 0)

    grads = [
        head_backward(
            head_of(grad_heads, 0, h),
            kept[h][0],
            head_of(qkv, 0, h),
            head_of(qkv, 1, h),
            head_of(qkv, 2, h),
            feature_proj[h],
            kept[h][1],
            table,
            table_low,
        )
        for h in range(head_count)
    ]
    grad_qkv = jnp.concatenate(
        [grads[h][kind] for kind in range(3) for h in range(head_count)], axis=1
    ).astype(bf16)
    grad_qkv_bias = jnp.sum(grad_qkv.astype(f32), axis=0)
    through = lax.psum_scatter(
        dot_cols(grad_qkv, qkv_weight).astype(bf16), "tensor", scatter_dimension=0, tiled=True
    )
    tokens_grad = grad_resid_one + through.astype(f32)
    grad_qkv_weight = scatter_plane(dot_rows(gathered, grad_qkv).astype(bf16)).astype(f32)

    def placed(local_part, total_width):
        return lax.dynamic_update_slice_in_dim(
            jnp.zeros((total_width,), f32), local_part, place * local_part.shape[0], 0
        )

    full = jnp.concatenate([grad_hidden_bias, grad_hidden_bias[:-1]], axis=0)[::-1]
    natural = lax.dynamic_slice_in_dim(full, (2 * shards - 2 - place) % shards, shards, 0)
    smalls = [
        placed(grad_qkv_bias[:width], D),
        placed(grad_qkv_bias[width : 2 * width], D),
        placed(grad_qkv_bias[2 * width :], D),
        natural.reshape(-1),
        grad_mixer_bias,
        grad_output_bias,
        grad_first_gain,
        grad_first_shift,
        grad_second_gain,
        grad_second_shift,
    ]
    small = small_sum(jnp.concatenate(smalls))
    parts = []
    begin = 0
    for entry in smalls:
        parts.append(small[begin : begin + entry.shape[0]])
        begin += entry.shape[0]
    grad_hidden = scatter_shards(grad_hidden)
    grad_output = scatter_shards(grad_output).T
    grad_mixer = scatter_shards(grad_mixer).T
    return (
        layer_out,
        tokens_grad,
        grad_qkv_weight[:, :width],
        parts[0],
        grad_qkv_weight[:, width : 2 * width],
        parts[1],
        grad_qkv_weight[:, 2 * width :],
        parts[2],
        grad_mixer,
        parts[4],
        parts[6],
        parts[7],
        grad_hidden,
        parts[3],
        grad_output,
        parts[5],
        parts[8],
        parts[9],
    )


def solution(mesh):
    placed = (
        P(("dp", "tensor"), None),
        P("dp", None),
        P(None, "tensor"),
        P("tensor"),
        P(None, "tensor"),
        P("tensor"),
        P(None, "tensor"),
        P("tensor"),
        P("tensor", None, None),
        P("tensor", None),
        P(),
        P(),
        P(),
        P(None, "tensor"),
        P("tensor"),
        P("tensor", None),
        P(),
        P(),
        P(),
        P(("dp", "tensor"), None),
    )
    return jax.shard_map(
        body,
        mesh=mesh,
        in_specs=placed,
        out_specs=(
            P(("dp", "tensor"), None),
            P(("dp", "tensor"), None),
            P("dp", "tensor"),
            P(),
            P("dp", "tensor"),
            P(),
            P("dp", "tensor"),
            P(),
            P("tensor", "dp"),
            P(),
            P(),
            P(),
            P("dp", "tensor"),
            P(),
            P("tensor", "dp"),
            P(),
            P(),
            P(),
        ),
        check_vma=False,
    )
```

```python
import functools
import math

import jax
import jax.numpy as jnp
from jax import lax
from jax.experimental import pallas as pl
from jax.experimental.pallas import tpu as pltpu
from jax.sharding import PartitionSpec as P

HEAD_DIM = 64
FEAT = 256
PLANE = 8
VMEM_LIMIT = 60 * 1024 * 1024
COST_RATE = 9e8

eps = 1e-06
bf16 = jnp.bfloat16
f32 = jnp.float32


def dot(left, right):
    return jnp.dot(left, right, preferred_element_type=f32)


def dot_rows(left, right):
    return lax.dot_general(left, right, (((0,), (0,)), ((), ())), preferred_element_type=f32)


def dot_cols(left, right):
    return lax.dot_general(left, right, (((1,), (1,)), ((), ())), preferred_element_type=f32)


def cost(micros):
    return pl.CostEstimate(flops=int(micros * COST_RATE), transcendentals=0, bytes_accessed=0)


def pack_kernel(
    own_ref, bias_ref, tokens_ref, hidden_ref, mixer_ref, output_ref, xt_ref, first_ref, second_ref, held_ref, sems
):
    rows, columns = second_ref.shape
    chip = lax.shift_right_logical(own_ref[0], 1)
    core = lax.bitwise_and(own_ref[0], 1)
    mixer_rows = mixer_ref.shape[0] // (PLANE // 2)

    def copy(source, height, target, sem):
        begin = pl.multiple_of(chip * height, 16)
        return pltpu.make_async_copy(
            source.at[pl.ds(begin, height), lanes(core, columns)], target, sem
        )

    copies = [
        copy(hidden_ref, rows, first_ref.at[0:rows], sems.at[0]),
        copy(mixer_ref, mixer_rows, first_ref.at[rows : rows + mixer_rows], sems.at[1]),
        copy(output_ref, rows, second_ref, sems.at[2]),
    ]
    fetch = pltpu.make_async_copy(tokens_ref, held_ref, sems.at[3])
    fetch.start()
    start_all([copies])
    wide = bias_ref[...]
    parts = []
    for _ in range(3):
        part = wide.astype(bf16).astype(f32)
        wide = wide - part
        parts += [part[:, :columns], part[:, columns:]]
    parts.append(jnp.zeros((10, columns), f32))
    first_ref[rows + mixer_rows :] = jnp.concatenate(parts, axis=0).astype(bf16)
    fetch.wait()
    xt_ref[...] = held_ref[...].T
    wait_all(copies)


def pack(own, tokens, hidden_bias, hidden_weight, mixer_weight, output_weight):
    local, depth = tokens.shape
    chips = PLANE // 2
    columns = depth // 2
    rows = depth // chips
    first_rows = rows + mixer_weight.shape[0] // chips + 16
    vmem = pl.BlockSpec(memory_space=pltpu.VMEM)
    return pl.pallas_call(
        pack_kernel,
        in_specs=[pl.BlockSpec(memory_space=pltpu.SMEM), vmem] + [pl.BlockSpec(memory_space=pltpu.HBM)] * 4,
        out_specs=[vmem] * 3,
        out_shape=[
            jax.ShapeDtypeStruct((depth, local), bf16),
            jax.ShapeDtypeStruct((first_rows, columns), bf16),
            jax.ShapeDtypeStruct((rows, columns), bf16),
        ],
        scratch_shapes=[pltpu.VMEM((local, depth), bf16), pltpu.SemaphoreType.DMA((4,))],
        compiler_params=pltpu.CompilerParams(vmem_limit_bytes=VMEM_LIMIT),
        cost_estimate=cost(3),
        name="pack",
    )(own, hidden_bias, tokens, hidden_weight, mixer_weight, output_weight)


def unpack_bias(entries):
    wide = entries.astype(f32)
    return jnp.concatenate([wide[0:1] + wide[2:3] + wide[4:5], wide[1:2] + wide[3:4] + wide[5:6]], axis=1)


def prepare_kernel(
    query_ref, key_ref, value_ref, query_bias_ref, key_bias_ref, value_bias_ref, proj_ref, joined_ref, turned_ref, bias_ref, proj_t_ref
):
    width = query_ref.shape[1]
    weights = [query_ref[...], key_ref[...], value_ref[...]]
    joined_ref[...] = jnp.concatenate(weights, axis=1)
    for kind, weight in enumerate(weights):
        turned_ref[kind * width : (kind + 1) * width] = weight.T
    for kind, bias in enumerate((query_bias_ref, key_bias_ref, value_bias_ref)):
        bias_ref[kind * width : (kind + 1) * width] = jnp.broadcast_to(bias[...], (8, width)).T
    for h in range(proj_ref.shape[0]):
        proj_t_ref[h] = proj_ref[h].T


def prepare(weights, biases, proj):
    depth, width = weights[0].shape
    heads, head_dim, feat = proj.shape
    vmem = pl.BlockSpec(memory_space=pltpu.VMEM)
    return pl.pallas_call(
        prepare_kernel,
        in_specs=[vmem] * 7,
        out_specs=[vmem] * 4,
        out_shape=[
            jax.ShapeDtypeStruct((depth, 3 * width), bf16),
            jax.ShapeDtypeStruct((3 * width, depth), bf16),
            jax.ShapeDtypeStruct((3 * width, 8), f32),
            jax.ShapeDtypeStruct((heads, feat, head_dim), bf16),
        ],
        compiler_params=pltpu.CompilerParams(vmem_limit_bytes=VMEM_LIMIT),
        cost_estimate=cost(4),
        name="prepare",
    )(*weights, *biases, proj)


def lanes(index, size):
    return pl.ds(pl.multiple_of(index * size, size), size)


def segments(lengths_ref, count, shape):
    places = lax.broadcasted_iota(jnp.int32, shape, len(shape) - 1)
    seg = jnp.zeros(shape, jnp.int32)
    end = jnp.int32(0)
    for s in range(count):
        end = end + lengths_ref[0, s]
        seg = seg + (places >= end).astype(jnp.int32)
    return seg


def masked_copies(seg, entries, count):
    zero = jnp.zeros_like(entries)
    return [jnp.where(seg == s, entries, zero) for s in range(count)]


def one_hot_rows(seg, count):
    rows = lax.broadcasted_iota(jnp.int32, (8, seg.shape[1]), 0)
    return jnp.where((rows == seg) & (rows < count), 1.0, 0.0).astype(f32)


def masked_sum(seg, wide, count):
    height = HEAD_DIM
    total = jnp.zeros((height, wide.shape[1]), f32)
    for s in range(count):
        total = total + jnp.where(seg == s, wide[s * height : (s + 1) * height], 0.0)
    return total


def feature_rows(vectors, proj_t):
    scale = HEAD_DIM ** (-0.25)
    widened = vectors.astype(f32)
    square = (0.5 * scale * scale) * jnp.sum(widened * widened, axis=0, keepdims=True)
    return (jnp.exp(scale * dot(proj_t, vectors) - square) * (1.0 / math.sqrt(FEAT))).astype(bf16)


def attend_kernel(
    count,
    lengths_ref,
    place_ref,
    xt_ref,
    wt_ref,
    bias_ref,
    proj_t_ref,
    qkv_ref,
    qf_ref,
    kf_ref,
    state_ref,
    out_ref,
    den_ref,
    p0_ref,
    p1_ref,
    p2_ref,
    p3_ref,
    mixed_ref,
):
    h = pl.program_id(0)
    shards, _, local = xt_ref.shape
    heads = pl.num_programs(0)
    width = wt_ref.shape[0] // 3
    spread_rows = count * HEAD_DIM

    @pl.when(h == 0)
    def _():
        for s in range(shards):
            qkv_ref[:, s * local : (s + 1) * local] = (
                dot(wt_ref[...], xt_ref[s]) + bias_ref[:, 0:1]
            ).astype(bf16)

    def rows(kind):
        begin = pl.multiple_of(kind * width + h * HEAD_DIM, HEAD_DIM)
        return qkv_ref[pl.ds(begin, HEAD_DIM), :]

    seg = segments(lengths_ref, count, (1, shards * local))
    hot = one_hot_rows(seg, count)
    proj_t = proj_t_ref[0]
    q_feat = feature_rows(rows(0), proj_t)
    k_feat = feature_rows(rows(1), proj_t)
    qf_ref[0] = q_feat
    kf_ref[0] = k_feat
    wide = jnp.concatenate(
        masked_copies(seg, rows(2), count) + [jnp.concatenate([hot, hot], axis=0).astype(bf16)], axis=0
    )
    state = dot_cols(wide, k_feat)
    sums = state[spread_rows : spread_rows + 8]
    high = sums.astype(bf16).astype(f32)
    state_ref[0, :spread_rows] = state[:spread_rows].astype(bf16)
    state_ref[0, spread_rows : spread_rows + 16] = jnp.concatenate([high, high], axis=0).astype(bf16)
    state_ref[0, spread_rows + 16 :] = jnp.concatenate(
        [sums - high, jnp.zeros_like(high)], axis=0
    ).astype(bf16)
    through = dot(state_ref[0], q_feat)
    scores = through[spread_rows : spread_rows + 8] + through[spread_rows + 16 : spread_rows + 24]
    den = jnp.sum(hot * scores, axis=0, keepdims=True) + (seg >= count).astype(f32)
    out = masked_sum(seg, through, count) / den
    out_ref[...] = out
    den_ref[0] = jnp.broadcast_to(den, den_ref.shape[1:])
    mixed_ref[pl.ds(pl.multiple_of(h * HEAD_DIM, HEAD_DIM), HEAD_DIM), :] = out.astype(bf16)

    @pl.when(h == heads - 1)
    def _():
        for s, piece in enumerate((p0_ref, p1_ref, p2_ref, p3_ref)):
            owner = lax.rem(place_ref[0] + s, shards)
            piece[...] = mixed_ref[:, lanes(owner, local)]


def attend(xt, wt, bias, proj_t, lengths, place):
    shards, depth, local = xt.shape
    heads, feat, head_dim = proj_t.shape
    total = shards * local
    count = lengths.shape[1] - 1
    width = heads * head_dim
    state_rows = count * head_dim + 32
    smem = pl.BlockSpec(memory_space=pltpu.SMEM)

    def whole(*shape):
        return pl.BlockSpec(shape, lambda h: (0,) * len(shape))

    def per_head(*shape):
        return pl.BlockSpec((1,) + shape, lambda h: (h,) + (0,) * len(shape))

    return pl.pallas_call(
        functools.partial(attend_kernel, count),
        grid=(heads,),
        in_specs=[
            smem,
            smem,
            whole(shards, depth, local),
            whole(3 * width, depth),
            whole(3 * width, 8),
            per_head(feat, head_dim),
        ],
        out_specs=[
            whole(3 * width, total),
            per_head(feat, total),
            per_head(feat, total),
            per_head(state_rows, feat),
            pl.BlockSpec((head_dim, total), lambda h: (h, 0)),
            per_head(8, total),
        ]
        + [whole(width, local)] * shards,
        out_shape=[
            jax.ShapeDtypeStruct((3 * width, total), bf16),
            jax.ShapeDtypeStruct((heads, feat, total), bf16),
            jax.ShapeDtypeStruct((heads, feat, total), bf16),
            jax.ShapeDtypeStruct((heads, state_rows, feat), bf16),
            jax.ShapeDtypeStruct((width, total), f32),
            jax.ShapeDtypeStruct((heads, 8, total), f32),
        ]
        + [jax.ShapeDtypeStruct((width, local), bf16)] * shards,
        scratch_shapes=[pltpu.VMEM((width, total), bf16)],
        compiler_params=pltpu.CompilerParams(vmem_limit_bytes=VMEM_LIMIT),
        cost_estimate=cost(8),
        name="attend",
    )(lengths, place, xt, wt, bias, proj_t)


def feature_back_rows(grad_feat, feat, vectors, proj_w):
    scale = HEAD_DIM ** (-0.25)
    grad_proj = grad_feat * feat.astype(f32)
    pulled = scale * dot(proj_w, grad_proj.astype(bf16))
    return pulled - (scale * scale) * vectors.astype(f32) * jnp.sum(grad_proj, axis=0, keepdims=True)


def attend_back_kernel(
    count,
    lengths_ref,
    place_ref,
    qkv_ref,
    qf_ref,
    kf_ref,
    state_ref,
    out_ref,
    den_ref,
    g0_ref,
    g1_ref,
    g2_ref,
    g3_ref,
    proj_ref,
    weight_ref,
    sums_ref,
    grad_ref,
    total_ref,
    small_ref,
    heads_ref,
):
    h = pl.program_id(0)
    shards = total_ref.shape[0]
    width, local = g0_ref.shape
    heads = pl.num_programs(0)
    spread_rows = count * HEAD_DIM

    @pl.when(h == 0)
    def _():
        for s, piece in enumerate((g0_ref, g1_ref, g2_ref, g3_ref)):
            owner = lax.rem(place_ref[0] + s, shards)
            heads_ref[:, lanes(owner, local)] = piece[...]

    def at(kind):
        return pl.ds(pl.multiple_of(kind * width + h * HEAD_DIM, HEAD_DIM), HEAD_DIM)

    seg = segments(lengths_ref, count, (1, shards * local))
    hot = one_hot_rows(seg, count)
    query, key, value = qkv_ref[at(0), :], qkv_ref[at(1), :], qkv_ref[at(2), :]
    q_feat, k_feat = qf_ref[0], kf_ref[0]
    grad_head = heads_ref[pl.ds(pl.multiple_of(h * HEAD_DIM, HEAD_DIM), HEAD_DIM), :].astype(f32)
    den = den_ref[0, 0:1, :]
    grad_numer = (grad_head / den).astype(bf16)
    grad_den = -jnp.sum(grad_head * out_ref[...], axis=0, keepdims=True) / den
    marked = hot * grad_den
    high = marked.astype(bf16).astype(f32)
    low = marked - high
    numer_wide = jnp.concatenate(
        masked_copies(seg, grad_numer, count)
        + [
            jnp.concatenate([high, low], axis=0).astype(bf16),
            jnp.concatenate([high, jnp.zeros_like(high)], axis=0).astype(bf16),
        ],
        axis=0,
    )
    grad_state = dot_cols(numer_wide[: spread_rows + 16], q_feat)
    sums = grad_state[spread_rows : spread_rows + 8] + grad_state[spread_rows + 8 : spread_rows + 16]
    sums_high = sums.astype(bf16).astype(f32)
    grad_state = jnp.concatenate(
        [
            grad_state[:spread_rows].astype(bf16),
            jnp.concatenate([sums_high, sums - sums_high], axis=0).astype(bf16),
        ],
        axis=0,
    )
    value_wide = jnp.concatenate(
        masked_copies(seg, value, count) + [jnp.concatenate([hot, hot], axis=0).astype(bf16)], axis=0
    )
    proj_w = proj_ref[0]
    grad_qfeat = dot_rows(state_ref[0], numer_wide)
    grad_ref[at(0), :] = feature_back_rows(grad_qfeat, q_feat, query, proj_w).astype(bf16)
    grad_kfeat = dot_rows(grad_state, value_wide)
    grad_ref[at(1), :] = feature_back_rows(grad_kfeat, k_feat, key, proj_w).astype(bf16)
    grad_ref[at(2), :] = masked_sum(seg, dot(grad_state[:spread_rows], k_feat), count).astype(bf16)

    @pl.when(h == heads - 1)
    def _():
        for d in range(shards):
            total_ref[d] = dot(weight_ref[...], grad_ref[:, d * local : (d + 1) * local]).astype(bf16)
        rows = sums_ref.shape[0]
        small_ref[:rows] = sums_ref[...]
        small_ref[rows:] = jnp.zeros_like(small_ref[rows:])
        ones = jnp.ones((8, shards * local), bf16)
        totals = dot_cols(ones, grad_ref[...])
        for t in range(shards):

            @pl.when(place_ref[0] == t)
            def _():
                for kind in range(3):
                    small_ref[rows + kind : rows + kind + 1, t * width : (t + 1) * width] = totals[
                        0:1, kind * width : (kind + 1) * width
                    ]


def attend_back(saved, pieces, proj, weight, sums, lengths, place):
    qkv, qf, kf, state, out, den = saved
    heads, feat, total = qf.shape
    width, local = pieces[0].shape
    shards = total // local
    depth = weight.shape[0]
    count = lengths.shape[1] - 1
    state_rows = state.shape[1]
    smem = pl.BlockSpec(memory_space=pltpu.SMEM)

    def whole(*shape):
        return pl.BlockSpec(shape, lambda h: (0,) * len(shape))

    def per_head(*shape):
        return pl.BlockSpec((1,) + shape, lambda h: (h,) + (0,) * len(shape))

    return pl.pallas_call(
        functools.partial(attend_back_kernel, count),
        grid=(heads,),
        in_specs=[
            smem,
            smem,
            whole(3 * width, total),
            per_head(feat, total),
            per_head(feat, total),
            per_head(state_rows, feat),
            pl.BlockSpec((HEAD_DIM, total), lambda h: (h, 0)),
            per_head(8, total),
        ]
        + [whole(width, local)] * shards
        + [per_head(HEAD_DIM, feat), whole(depth, 3 * width), whole(*sums.shape)],
        out_specs=[
            whole(3 * width, total),
            whole(shards, depth, local),
            whole(sums.shape[0] + 8, depth),
        ],
        out_shape=[
            jax.ShapeDtypeStruct((3 * width, total), bf16),
            jax.ShapeDtypeStruct((shards, depth, local), bf16),
            jax.ShapeDtypeStruct((sums.shape[0] + 8, depth), f32),
        ],
        scratch_shapes=[pltpu.VMEM((width, total), bf16)],
        compiler_params=pltpu.CompilerParams(vmem_limit_bytes=VMEM_LIMIT),
        cost_estimate=cost(9),
        name="attend_back",
    )(lengths, place, qkv, qf, kf, state, out, den, *pieces, proj, weight, sums)


def write_blocks(grads, hold_ref, begin=0):
    slots, height, _ = hold_ref.shape
    count = grads.shape[1]
    hold_ref[:, :, begin : begin + count] = grads.astype(bf16).reshape(slots, height, count)


def slot_place(slot, half):
    k = slot // 2
    if half == 0:
        return 1 - k % 2, k // 2
    return 1 - k // 2, k % 2


def emit_blocks(own, hold_ref, even_ref, odd_ref, half):
    for slot in range(hold_ref.shape[0]):
        target = odd_ref if slot % 2 else even_ref
        target[(0,) + slot_place(slot, half) + (0,)] = hold_ref[lax.bitwise_xor(own, slot)]


def emit_half(own, hold_ref, even_ref, odd_ref, second):
    for half in range(2):

        @pl.when(second == half)
        def _():
            emit_blocks(own, hold_ref, even_ref, odd_ref, half)


def output_grad_kernel(own_ref, grad_ffn_ref, act_ref, even_ref, odd_ref, hold_ref):
    write_blocks(dot_rows(grad_ffn_ref[...], act_ref[0]), hold_ref)
    emit_half(own_ref[0], hold_ref, even_ref, odd_ref, pl.program_id(0) // 2)


def block_outputs(slots, shards, height, count):
    spec = pl.BlockSpec((1, 2, 2, 1, height, count), lambda s: (s // 2, 0, 0, s % 2, 0, 0))
    shape = jax.ShapeDtypeStruct((2, 2, slots // 4, shards // 2, height, count), bf16)
    return [spec, spec], [shape, shape]


def output_grad(own, slots, grad_ffn, acts):
    shards, rows, hidden = acts.shape
    depth = grad_ffn.shape[1]
    specs, shapes = block_outputs(slots, shards, depth // slots, hidden)
    return pl.pallas_call(
        output_grad_kernel,
        grid=(shards,),
        in_specs=[
            pl.BlockSpec(memory_space=pltpu.SMEM),
            pl.BlockSpec((rows, depth), lambda s: (0, 0)),
            pl.BlockSpec((1, rows, hidden), lambda s: (s, 0, 0)),
        ],
        out_specs=specs,
        out_shape=shapes,
        scratch_shapes=[pltpu.VMEM((slots, depth // slots, hidden), bf16)],
        compiler_params=pltpu.CompilerParams(vmem_limit_bytes=VMEM_LIMIT),
        cost_estimate=cost(4),
        name="output_grad",
    )(own, grad_ffn, acts)


def hidden_grad_kernel(
    own_ref, first_ref, grad_pre_ref, grad_branch_ref, p0_ref, p1_ref, p2_ref, p3_ref, even_ref, odd_ref, hold_ref
):
    s = pl.program_id(0)
    hidden = grad_pre_ref.shape[2]
    write_blocks(dot_rows(first_ref[...], grad_pre_ref[0]), hold_ref)
    for index, piece in enumerate((p0_ref, p1_ref, p2_ref, p3_ref)):

        @pl.when(s == index)
        def _():
            grads = lax.dot_general(
                grad_branch_ref[...], piece[...], (((0,), (1,)), ((), ())), preferred_element_type=f32
            )
            write_blocks(grads, hold_ref, hidden)

    emit_half(own_ref[0], hold_ref, even_ref, odd_ref, s // 2)


def hidden_grad(own, slots, first_low, grad_pre, grad_branch, pieces):
    shards, rows, hidden = grad_pre.shape
    depth = first_low.shape[1]
    width = pieces[0].shape[0]
    specs, shapes = block_outputs(slots, shards, depth // slots, hidden + width)
    return pl.pallas_call(
        hidden_grad_kernel,
        grid=(shards,),
        in_specs=[
            pl.BlockSpec(memory_space=pltpu.SMEM),
            pl.BlockSpec((rows, depth), lambda s: (0, 0)),
            pl.BlockSpec((1, rows, hidden), lambda s: (s, 0, 0)),
            pl.BlockSpec((rows, depth), lambda s: (0, 0)),
        ]
        + [pl.BlockSpec((width, rows), lambda s: (0, 0))] * shards,
        out_specs=specs,
        out_shape=shapes,
        scratch_shapes=[pltpu.VMEM((slots, depth // slots, hidden + width), bf16)],
        compiler_params=pltpu.CompilerParams(vmem_limit_bytes=VMEM_LIMIT),
        cost_estimate=cost(5),
        name="hidden_grad",
    )(own, first_low, grad_pre, grad_branch, *pieces)


def qkv_grad_kernel(own_ref, xt_ref, grad_ref, even_ref, odd_ref, hold_ref):
    shards, _, local = xt_ref.shape
    grads = sum(
        dot_cols(xt_ref[d], grad_ref[:, d * local : (d + 1) * local]) for d in range(shards)
    )
    write_blocks(grads, hold_ref)
    rows = even_ref.shape[4]
    for slot in range(hold_ref.shape[0]):
        target = odd_ref if slot % 2 else even_ref
        block = hold_ref[lax.bitwise_xor(own_ref[0], slot)]
        for half in range(2):
            target[(half,) + slot_place(slot, half) + (0,)] = block[half * rows : (half + 1) * rows]


def qkv_grad(own, slots, xt, grads):
    shards, depth, local = xt.shape
    count = grads.shape[0]
    vmem = pl.BlockSpec(memory_space=pltpu.VMEM)
    shape = jax.ShapeDtypeStruct((2, 2, slots // 4, 1, depth // slots // 2, count), bf16)
    return pl.pallas_call(
        qkv_grad_kernel,
        in_specs=[pl.BlockSpec(memory_space=pltpu.SMEM), vmem, vmem],
        out_specs=[vmem, vmem],
        out_shape=[shape, shape],
        scratch_shapes=[pltpu.VMEM((slots, depth // slots, count), bf16)],
        compiler_params=pltpu.CompilerParams(vmem_limit_bytes=VMEM_LIMIT),
        cost_estimate=cost(2),
        name="qkv_grad",
    )(own, xt, grads)


def norm_rows(resid):
    center = resid - jnp.mean(resid, axis=-1, keepdims=True)
    inverse = lax.rsqrt(jnp.mean(center * center, axis=-1, keepdims=True) + eps)
    return center * inverse, inverse


HELD = [((0, 2), 0), ((4, 6), 0), ((0, 4), 2), ((2, 6), 2)]
HELD = HELD + [((low ^ 1, high ^ 1), shard) for (low, high), shard in HELD]


def place_copies(own, held, begin, rows, target, sems):
    columns = held[0].shape[2]
    copies = [[] for _ in range(target.shape[0])]
    for piece, (masks, shard) in zip(held, HELD):
        for index in range(4):
            mask, s = masks[index // 2], shard + index % 2
            source = lax.bitwise_xor(own, mask)
            chip = lax.shift_right_logical(source, 1)
            core = lax.bitwise_and(source, 1)
            copies[s].append(
                pltpu.make_async_copy(
                    piece.at[index, pl.ds(begin, rows), :],
                    target.at[s, chip, :, lanes(core, columns)],
                    sems.at[s, mask],
                )
            )
    return copies


def start_all(copies):
    for entries in copies:
        for copy in entries:
            copy.start()


def wait_all(entries):
    for copy in entries:
        copy.wait()


def ffn_up_kernel(
    own_ref,
    tokens_ref,
    p0_ref,
    p1_ref,
    p2_ref,
    p3_ref,
    mixer_bias_ref,
    gain_ref,
    shift_ref,
    hidden_bias_ref,
    *refs,
):
    held = refs[:PLANE]
    normed_ref, inverse_ref, first_ref, act_ref, slope_ref, mixer_ref, hidden_ref, mixer_sem, hidden_sem = refs[PLANE:]
    own = own_ref[0]
    shards, chips, mixer_rows, depth = mixer_ref.shape
    hidden_rows = hidden_ref.shape[2]
    mixer_copies = place_copies(own, held, hidden_rows, mixer_rows, mixer_ref, mixer_sem)
    hidden_copies = place_copies(own, held, 0, hidden_rows, hidden_ref, hidden_sem)
    start_all(mixer_copies)
    start_all(hidden_copies)
    resid = tokens_ref[...].astype(f32) + mixer_bias_ref[...]
    for s, piece in enumerate((p0_ref, p1_ref, p2_ref, p3_ref)):
        wait_all(mixer_copies[s])
        resid = resid + dot_rows(piece[...], mixer_ref[s].reshape(chips * mixer_rows, depth))
    normed, inverse = norm_rows(resid)
    normed_ref[...] = normed
    inverse_ref[...] = jnp.broadcast_to(inverse, inverse_ref.shape)
    first_low = (normed * gain_ref[...] + shift_ref[...]).astype(bf16)
    first_ref[...] = first_low
    for s in range(shards):
        wait_all(hidden_copies[s])
        bias = unpack_bias(hidden_bias_ref[s])
        pre = dot(first_low, hidden_ref[s].reshape(chips * hidden_rows, hidden_ref.shape[3])) + bias
        phi = 0.5 * (1.0 + lax.erf(pre * math.sqrt(0.5)))
        act_ref[s] = (pre * phi).astype(bf16)
        slope_ref[s] = (
            phi + pre * jnp.exp(-0.5 * pre * pre) * (1.0 / math.sqrt(2.0 * math.pi))
        ).astype(bf16)


def ffn_up(own, tokens, pieces, mixer_bias, gain, shift_by, hidden_bias, held, mixer_rows):
    rows, depth = tokens.shape
    shards = len(pieces)
    chips = PLANE // 2
    hidden = 2 * hidden_bias.shape[-1]
    hidden_rows = held[0].shape[1] - mixer_rows
    vmem = pl.BlockSpec(memory_space=pltpu.VMEM)
    return pl.pallas_call(
        ffn_up_kernel,
        in_specs=[pl.BlockSpec(memory_space=pltpu.SMEM)]
        + [vmem] * (1 + shards + 4)
        + [pl.BlockSpec(memory_space=pltpu.HBM)] * PLANE,
        out_specs=[vmem] * 5,
        out_shape=[
            jax.ShapeDtypeStruct((rows, depth), f32),
            jax.ShapeDtypeStruct((rows, 128), f32),
            jax.ShapeDtypeStruct((rows, depth), bf16),
            jax.ShapeDtypeStruct((shards, rows, hidden), bf16),
            jax.ShapeDtypeStruct((shards, rows, hidden), bf16),
        ],
        scratch_shapes=[
            pltpu.VMEM((shards, chips, mixer_rows, depth), bf16),
            pltpu.VMEM((shards, chips, hidden_rows, hidden), bf16),
            pltpu.SemaphoreType.DMA((shards, PLANE)),
            pltpu.SemaphoreType.DMA((shards, PLANE)),
        ],
        compiler_params=pltpu.CompilerParams(vmem_limit_bytes=VMEM_LIMIT),
        cost_estimate=cost(8),
        name="ffn_up",
    )(own, tokens, *pieces, mixer_bias, gain, shift_by, hidden_bias, *held)


def norm_rows_back(scaled, normed, inverse):
    return inverse * (
        scaled
        - jnp.mean(scaled, axis=-1, keepdims=True)
        - normed * jnp.mean(scaled * normed, axis=-1, keepdims=True)
    )


def column_sum(entries):
    return jnp.sum(entries, axis=0, keepdims=True)


def ffn_down_kernel(
    own_ref,
    normed_ref,
    inverse_ref,
    act_ref,
    slope_ref,
    cotangent_ref,
    first_gain_ref,
    first_shift_ref,
    output_bias_ref,
    gain_ref,
    shift_ref,
    *refs,
):
    held, refs = refs[:PLANE], refs[PLANE:]
    held_out, refs = refs[:PLANE], refs[PLANE:]
    (
        layer_ref,
        resid_ref,
        b0_ref,
        b1_ref,
        b2_ref,
        b3_ref,
        grad_ffn_ref,
        grad_pre_ref,
        grad_branch_ref,
        sums_ref,
        mixer_ref,
        hidden_ref,
        output_ref,
        mixer_sem,
        hidden_sem,
        output_sem,
    ) = refs
    own, place = own_ref[0], own_ref[1]
    shards, chips, mixer_rows, depth = mixer_ref.shape
    hidden_rows = hidden_ref.shape[2]
    hidden = hidden_ref.shape[3]
    output_copies = place_copies(own, held_out, 0, output_ref.shape[2], output_ref, output_sem)
    hidden_copies = place_copies(own, held, 0, hidden_rows, hidden_ref, hidden_sem)
    mixer_copies = place_copies(own, held, hidden_rows, mixer_rows, mixer_ref, mixer_sem)
    start_all(output_copies)
    start_all(hidden_copies)
    start_all(mixer_copies)
    normed_one = normed_ref[...]
    resid = normed_one * first_gain_ref[...] + first_shift_ref[...] + output_bias_ref[...]
    for s in range(shards):
        wait_all(output_copies[s])
        resid = resid + dot(act_ref[s], output_ref[s].reshape(hidden, depth))
    normed, inverse = norm_rows(resid)
    layer_ref[...] = (normed * gain_ref[...] + shift_ref[...]).astype(bf16)
    grad_out = cotangent_ref[...].astype(f32)
    sums_ref[0:1] = column_sum(grad_out * normed)
    sums_ref[1:2] = column_sum(grad_out)
    grad_two = norm_rows_back(grad_out * gain_ref[...], normed, inverse)
    grad_ffn = grad_two.astype(bf16)
    grad_ffn_ref[...] = grad_ffn
    sums_ref[2:3] = column_sum(grad_ffn.astype(f32))
    grad_first = grad_two
    for s in range(shards):
        grad_pre = (
            dot_cols(grad_ffn, output_ref[s].reshape(hidden, depth)) * slope_ref[s].astype(f32)
        ).astype(bf16)
        grad_pre_ref[s] = grad_pre
        sums_ref[pl.ds(8 + lax.rem(place - s + shards, shards), 1)] = column_sum(grad_pre.astype(f32))
        wait_all(hidden_copies[s])
        grad_first = grad_first + dot_cols(grad_pre, hidden_ref[s].reshape(depth, hidden))
    sums_ref[3:4] = column_sum(grad_first * normed_one)
    sums_ref[4:5] = column_sum(grad_first)
    grad_one = norm_rows_back(grad_first * first_gain_ref[...], normed_one, inverse_ref[:, 0:1])
    resid_ref[...] = grad_one
    grad_branch = grad_one.astype(bf16)
    grad_branch_ref[...] = grad_branch
    sums_ref[5:6] = column_sum(grad_branch.astype(f32))
    sums_ref[6:8] = jnp.zeros((2, depth), f32)
    sums_ref[8 + shards :] = jnp.zeros((8 - shards, depth), f32)
    for s, back in enumerate((b0_ref, b1_ref, b2_ref, b3_ref)):
        wait_all(mixer_copies[s])
        back[...] = dot_cols(mixer_ref[s].reshape(chips * mixer_rows, depth), grad_branch).astype(bf16)


def ffn_down(own, normed, inverse, acts, slopes, cotangent, vectors, held, held_out, mixer_rows):
    rows, depth = normed.shape
    shards, _, hidden = acts.shape
    chips = PLANE // 2
    hidden_rows = held[0].shape[1] - mixer_rows
    output_rows = held_out[0].shape[1]
    vmem = pl.BlockSpec(memory_space=pltpu.VMEM)
    width = chips * mixer_rows
    return pl.pallas_call(
        ffn_down_kernel,
        in_specs=[pl.BlockSpec(memory_space=pltpu.SMEM)]
        + [vmem] * 10
        + [pl.BlockSpec(memory_space=pltpu.HBM)] * (2 * PLANE),
        out_specs=[vmem] * (6 + shards),
        out_shape=[
            jax.ShapeDtypeStruct((rows, depth), bf16),
            jax.ShapeDtypeStruct((rows, depth), f32),
        ]
        + [jax.ShapeDtypeStruct((width, rows), bf16)] * shards
        + [
            jax.ShapeDtypeStruct((rows, depth), bf16),
            jax.ShapeDtypeStruct((shards, rows, hidden), bf16),
            jax.ShapeDtypeStruct((rows, depth), bf16),
            jax.ShapeDtypeStruct((16, depth), f32),
        ],
        scratch_shapes=[
            pltpu.VMEM((shards, chips, mixer_rows, depth), bf16),
            pltpu.VMEM((shards, chips, hidden_rows, hidden), bf16),
            pltpu.VMEM((shards, chips, output_rows, depth), bf16),
            pltpu.SemaphoreType.DMA((shards, PLANE)),
            pltpu.SemaphoreType.DMA((shards, PLANE)),
            pltpu.SemaphoreType.DMA((shards, PLANE)),
        ],
        compiler_params=pltpu.CompilerParams(vmem_limit_bytes=VMEM_LIMIT),
        cost_estimate=cost(15),
        name="ffn_down",
    )(own, normed, inverse, acts, slopes, cotangent, *vectors, *held, *held_out)


def swap(values, mask):
    size = lax.axis_size("dp")
    return lax.ppermute(values, "dp", [(i, i ^ mask) for i in range(size)])


def shift(values, step):
    size = lax.axis_size("tensor")
    return lax.ppermute(values, "tensor", [(i, (i + step) % size) for i in range(size)])


def after(values, *others):
    return lax.optimization_barrier((values, others))[0]


def spread_shards(payload):
    return [payload] + [shift(payload, s) for s in range(1, lax.axis_size("tensor"))]


def spread_plane(parts, before=(), between=()):
    low, high = after((jnp.stack(parts[:2]), jnp.stack(parts[2:])), *before)
    low_far, high_far = after((swap(low, 2), swap(high, 4)), *between)
    low = jnp.concatenate([low, low_far])
    high = jnp.concatenate([high, high_far])
    return low, swap(low, 4), high, swap(high, 2)


def both_cores(held):
    return list(held) + [swap(entry, 1) for entry in held]


def add_low(*entries):
    return sum(entry.astype(f32) for entry in entries).astype(bf16)


def sum_cores(even, odd):
    far = swap(odd, 1)
    return [[add_low(even[half, part], far[half, part]) for part in range(2)] for half in range(2)]


def sum_first(near, *before):
    (send_low, keep_low), (send_high, keep_high) = near
    send_low, send_high = after((send_low, send_high), *before)
    low, high = swap(send_low, 2), swap(send_high, 4)
    return (
        [add_low(keep_low[0], low[0]), add_low(keep_high[0], high[0])],
        [add_low(keep_low[1], low[1]), add_low(keep_high[1], high[1])],
    )


def sum_second(stay, send):
    low, high = swap(send[0], 4), swap(send[1], 2)
    return [add_low(stay[0], low), add_low(stay[1], high)]


def scatter_all(even, odd):
    order = [[(half, slot) for slot in range(PLANE)] for half in range(2)]
    halves = []
    for half in range(2):
        blocks = [
            (odd if slot % 2 else even)[(half,) + slot_place(slot, half)] for half, slot in order[half]
        ]
        halves.append(jnp.stack(blocks, axis=1))
    return halves


def scatter_shards(grads):
    total = grads[0].astype(f32)
    for s in range(1, len(grads)):
        total = total + shift(grads[s], -s).astype(f32)
    return total


def small_sum(values):
    size = lax.axis_size("dp")
    if size != PLANE:
        return lax.psum(values, ("dp", "tensor"))
    values = values + swap(values, 1)
    values = values + swap(values, 2) + swap(values, 4) + swap(values, 6)
    total = values
    for s in range(1, lax.axis_size("tensor")):
        total = total + shift(values, s)
    return total


def body(
    tokens,
    lengths,
    query_weight,
    query_bias,
    key_weight,
    key_bias,
    value_weight,
    value_bias,
    feature_proj,
    mixer_weight,
    mixer_bias,
    first_gain,
    first_shift,
    hidden_weight,
    hidden_bias,
    output_weight,
    output_bias,
    second_gain,
    second_shift,
    cotangent,
):
    depth = tokens.shape[1]
    shards = lax.axis_size("tensor")
    place = lax.axis_index("tensor").astype(jnp.int32)
    plane = (lax.axis_index("dp") % PLANE).astype(jnp.int32)
    width = query_weight.shape[1]
    hidden = hidden_weight.shape[1]
    mixer_rows = mixer_weight.shape[0] // (PLANE // 2)
    own = jnp.stack([plane, place])
    slot_of = plane[None] if lax.axis_size("dp") == PLANE else jnp.zeros((1,), jnp.int32)

    def row(vector):
        return vector.reshape(1, -1)

    own_xt, payload, payload_out = pack(
        own, tokens, row(hidden_bias), hidden_weight, mixer_weight, output_weight
    )
    parts = spread_shards(payload)
    weights = after((query_weight, key_weight, value_weight), payload)
    qkv_weight, qkv_turned, qkv_bias, proj_t = prepare(
        weights, [row(query_bias), row(key_bias), row(value_bias)], feature_proj
    )
    xt = lax.all_gather(after(own_xt, qkv_bias), "tensor", axis=0, tiled=False)
    rows = payload.shape[0] - 16
    around = spread_plane([part[:rows] for part in parts])
    all_bias = jnp.stack([part[rows:] for part in parts])
    parts_out = spread_shards(after(payload_out, *parts))
    held = both_cores(around)
    *saved, p0, p1, p2, p3 = attend(
        after(xt, *around), qkv_turned, qkv_bias, proj_t, lengths, place[None]
    )
    around_out = spread_plane(parts_out, around, (p0,))
    held_out = both_cores(around_out)
    pieces = [p0] + [shift(p, s) for s, p in ((1, p1), (2, p2), (3, p3))]
    normed, inverse, first_low, acts, slopes = ffn_up(
        own, tokens, pieces, row(mixer_bias), row(first_gain), row(first_shift), all_bias, held, mixer_rows
    )
    vectors = [row(v) for v in (first_gain, first_shift, output_bias, second_gain, second_shift)]
    layer_out, grad_resid, b0, b1, b2, b3, grad_ffn, grad_pre, grad_branch, sums = ffn_down(
        own, normed, inverse, acts, slopes, cotangent, vectors, held, held_out, mixer_rows
    )
    back = [b0] + [shift(b, -s) for s, b in ((1, b1), (2, b2), (3, b3))]
    output_blocks = output_grad(slot_of, PLANE, grad_ffn, acts)
    hidden_blocks = hidden_grad(slot_of, PLANE, first_low, grad_pre, grad_branch, pieces)
    fast = lax.axis_size("dp") == PLANE
    if fast:
        near_output = sum_cores(*output_blocks)
        stay_output, send_output = sum_first(near_output)
        back = after(back, near_output)
    grad_qkv, total, small = attend_back(
        saved, back, feature_proj, qkv_weight, sums, lengths, place[None]
    )
    through = lax.psum_scatter(total, "tensor", scatter_dimension=0, tiled=True)
    tokens_grad = grad_resid + through[0].T.astype(f32)
    if fast:
        near_hidden = sum_cores(*hidden_blocks)
        grad_qkv = after(grad_qkv, send_output, near_hidden)
    qkv_blocks = qkv_grad(slot_of, PLANE, xt, grad_qkv)
    if fast:
        near_qkv = sum_cores(*qkv_blocks)
        grad_output = sum_second(stay_output, send_output)
        stay_hidden, send_hidden = sum_first(near_hidden, send_output)
        grad_hidden = sum_second(stay_hidden, send_hidden)
        stay_qkv, send_qkv = sum_first(near_qkv, send_hidden)
        grad_weight = jnp.concatenate([half[0] for half in sum_second(stay_qkv, send_qkv)])
    else:

        def scatter(halves, axis, dim):
            blocks = jnp.concatenate(halves, axis=axis)
            blocks = blocks.reshape(blocks.shape[:1] + (-1,) + blocks.shape[-1:])
            return lax.psum_scatter(blocks, "dp", scatter_dimension=1, tiled=True)

        grad_output = [scatter(scatter_all(*output_blocks), 0, 0)]
        grad_hidden = [scatter(scatter_all(*hidden_blocks), 0, 0)]
        grad_weight = scatter(scatter_all(*qkv_blocks), 2, 0)[0]
    grad_weight = grad_weight.astype(f32)
    small = small_sum(small)
    grad_output = scatter_shards([entry[s] for entry in grad_output for s in range(entry.shape[0])]).T
    grad_hidden = scatter_shards([entry[s] for entry in grad_hidden for s in range(entry.shape[0])])
    return (
        layer_out,
        tokens_grad,
        grad_weight[:, :width],
        small[16],
        grad_weight[:, width : 2 * width],
        small[17],
        grad_weight[:, 2 * width :],
        small[18],
        grad_hidden[:, hidden:].T,
        small[5],
        small[3],
        small[4],
        grad_hidden[:, :hidden],
        small[8 : 8 + shards].reshape(-1),
        grad_output,
        small[2],
        small[0],
        small[1],
    )


def solution(mesh):
    placed = (
        P(("dp", "tensor"), None),
        P("dp", None),
        P(None, "tensor"),
        P("tensor"),
        P(None, "tensor"),
        P("tensor"),
        P(None, "tensor"),
        P("tensor"),
        P("tensor", None, None),
        P("tensor", None),
        P(),
        P(),
        P(),
        P(None, "tensor"),
        P("tensor"),
        P("tensor", None),
        P(),
        P(),
        P(),
        P(("dp", "tensor"), None),
    )
    return jax.shard_map(
        body,
        mesh=mesh,
        in_specs=placed,
        out_specs=(
            P(("dp", "tensor"), None),
            P(("dp", "tensor"), None),
            P("dp", "tensor"),
            P(),
            P("dp", "tensor"),
            P(),
            P("dp", "tensor"),
            P(),
            P("tensor", "dp"),
            P(),
            P(),
            P(),
            P("dp", "tensor"),
            P(),
            P("tensor", "dp"),
            P(),
            P(),
            P(),
        ),
        check_vma=False,
    )
```

```python
import functools
import math

import jax
import jax.numpy as jnp
from jax import lax
from jax.experimental import pallas as pl
from jax.experimental.pallas import tpu as pltpu
from jax.sharding import PartitionSpec as P

HEAD_DIM = 64
FEAT = 256
PLANE = 8
COST_RATE = 9e9

eps = 1e-06
bf16 = jnp.bfloat16
f32 = jnp.float32


def dot(left, right):
    return jnp.dot(left, right, preferred_element_type=f32)


def dot_rows(left, right):
    return lax.dot_general(left, right, (((0,), (0,)), ((), ())), preferred_element_type=f32)


def dot_cols(left, right):
    return lax.dot_general(left, right, (((1,), (1,)), ((), ())), preferred_element_type=f32)


def cost(micros):
    return pl.CostEstimate(flops=int(micros * COST_RATE), transcendentals=0, bytes_accessed=0)


def pack_kernel(
    own_ref, bias_ref, tokens_ref, hidden_ref, mixer_ref, output_ref, xt_ref, first_ref, second_ref, held_ref, sems
):
    rows, columns = second_ref.shape
    chip = lax.shift_right_logical(own_ref[0], 1)
    core = lax.bitwise_and(own_ref[0], 1)
    mixer_rows = mixer_ref.shape[0] // (PLANE // 2)

    def copy(source, height, target, sem):
        begin = pl.multiple_of(chip * height, 16)
        return pltpu.make_async_copy(
            source.at[pl.ds(begin, height), lanes(core, columns)], target, sem
        )

    copies = [
        copy(hidden_ref, rows, first_ref.at[0:rows], sems.at[0]),
        copy(mixer_ref, mixer_rows, first_ref.at[rows : rows + mixer_rows], sems.at[1]),
        copy(output_ref, rows, second_ref, sems.at[2]),
    ]
    fetch = pltpu.make_async_copy(tokens_ref, held_ref, sems.at[3])
    fetch.start()
    start_all([copies])
    wide = jnp.concatenate([bias_ref[...], jnp.zeros((16 - bias_ref.shape[0], 128), f32)], axis=0)
    for index in range(3):
        part = wide.astype(bf16)
        wide = wide - part.astype(f32)
        first_ref[rows + mixer_rows :, index * 128 : (index + 1) * 128] = part
    fetch.wait()
    xt_ref[...] = held_ref[...].T
    wait_all(copies)


def pack(own, tokens, hidden_bias, hidden_weight, mixer_weight, output_weight):
    local, depth = tokens.shape
    chips = PLANE // 2
    columns = depth // 2
    rows = depth // chips
    first_rows = rows + mixer_weight.shape[0] // chips + 16
    vmem = pl.BlockSpec(memory_space=pltpu.VMEM)
    return pl.pallas_call(
        pack_kernel,
        in_specs=[pl.BlockSpec(memory_space=pltpu.SMEM), vmem] + [pl.BlockSpec(memory_space=pltpu.HBM)] * 4,
        out_specs=[vmem] * 3,
        out_shape=[
            jax.ShapeDtypeStruct((depth, local), bf16),
            jax.ShapeDtypeStruct((first_rows, columns), bf16),
            jax.ShapeDtypeStruct((rows, columns), bf16),
        ],
        scratch_shapes=[pltpu.VMEM((local, depth), bf16), pltpu.SemaphoreType.DMA((4,))],
        compiler_params=pltpu.CompilerParams(vmem_limit_bytes=60 << 20),
        cost_estimate=cost(3),
        name="pack",
    )(own, hidden_bias, tokens, hidden_weight, mixer_weight, output_weight)


def unpack_bias(entries):
    wide = entries.astype(f32)
    wide = wide[:, :128] + wide[:, 128:256] + wide[:, 256:384]
    return jnp.concatenate([wide[index : index + 1] for index in range(6)], axis=1)


def prepare_kernel(query_ref, key_ref, value_ref, joined_ref):
    joined_ref[...] = jnp.concatenate([query_ref[...].T, key_ref[...].T, value_ref[...].T], axis=1)


def prepare(weights):
    width, depth = weights[0].shape
    vmem = pl.BlockSpec(memory_space=pltpu.VMEM)
    return pl.pallas_call(
        prepare_kernel,
        in_specs=[vmem] * 3,
        out_specs=vmem,
        out_shape=jax.ShapeDtypeStruct((depth, 3 * width), bf16),
        compiler_params=pltpu.CompilerParams(vmem_limit_bytes=60 << 20),
        cost_estimate=cost(4),
        name="prepare",
    )(*weights)


def lanes(index, size):
    return pl.ds(pl.multiple_of(index * size, size), size)


def segments(lengths_ref, count, shape):
    places = lax.broadcasted_iota(jnp.int32, shape, len(shape) - 1)
    seg = jnp.zeros(shape, jnp.int32)
    end = jnp.int32(0)
    for s in range(count):
        end = end + lengths_ref[0, s]
        seg = seg + (places >= end).astype(jnp.int32)
    return seg


def masked_copies(seg, entries, count):
    zero = jnp.zeros_like(entries)
    return [jnp.where(seg == s, entries, zero) for s in range(count)]


def one_hot_rows(seg, count):
    rows = lax.broadcasted_iota(jnp.int32, (8, seg.shape[1]), 0)
    return jnp.where((rows == seg) & (rows < count), 1.0, 0.0).astype(f32)


def masked_sum(seg, wide, count):
    height = HEAD_DIM
    total = jnp.zeros((height, wide.shape[1]), f32)
    for s in range(count):
        total = total + jnp.where(seg == s, wide[s * height : (s + 1) * height], 0.0)
    return total


def feature_rows(vectors, proj_t):
    scale = HEAD_DIM ** (-0.25)
    widened = vectors.astype(f32)
    square = (0.5 * scale * scale) * jnp.sum(widened * widened, axis=0, keepdims=True)
    return (jnp.exp(scale * dot(proj_t, vectors) - square) * (1.0 / math.sqrt(FEAT))).astype(bf16)


def attend_kernel(
    count,
    lengths_ref,
    place_ref,
    xt_ref,
    query_weight_ref,
    key_weight_ref,
    value_weight_ref,
    query_bias_ref,
    key_bias_ref,
    value_bias_ref,
    proj_ref,
    qkv_ref,
    qf_ref,
    kf_ref,
    state_ref,
    out_ref,
    den_ref,
    p0_ref,
    p1_ref,
    p2_ref,
    p3_ref,
    mixed_ref,
):
    h = pl.program_id(0)
    shards, _, local = xt_ref.shape
    heads = pl.num_programs(0)
    width = query_weight_ref.shape[0]
    spread_rows = count * HEAD_DIM

    @pl.when(h == 0)
    def _():
        for kind, (weight, bias) in enumerate(
            (
                (query_weight_ref, query_bias_ref),
                (key_weight_ref, key_bias_ref),
                (value_weight_ref, value_bias_ref),
            )
        ):
            column = jnp.broadcast_to(bias[...], (8, width)).T[:, 0:1]
            for s in range(shards):
                qkv_ref[kind * width : (kind + 1) * width, s * local : (s + 1) * local] = (
                    dot(weight[...], xt_ref[s]) + column
                ).astype(bf16)

    def rows(kind):
        begin = pl.multiple_of(kind * width + h * HEAD_DIM, HEAD_DIM)
        return qkv_ref[pl.ds(begin, HEAD_DIM), :]

    seg = segments(lengths_ref, count, (1, shards * local))
    hot = one_hot_rows(seg, count)
    proj_t = proj_ref[0].T
    q_feat = feature_rows(rows(0), proj_t)
    k_feat = feature_rows(rows(1), proj_t)
    qf_ref[0] = q_feat
    kf_ref[0] = k_feat
    wide = jnp.concatenate(
        masked_copies(seg, rows(2), count) + [jnp.concatenate([hot, hot], axis=0).astype(bf16)], axis=0
    )
    state = dot_cols(wide, k_feat)
    sums = state[spread_rows : spread_rows + 8]
    high = sums.astype(bf16).astype(f32)
    state_ref[0, :spread_rows] = state[:spread_rows].astype(bf16)
    state_ref[0, spread_rows : spread_rows + 16] = jnp.concatenate([high, high], axis=0).astype(bf16)
    state_ref[0, spread_rows + 16 :] = jnp.concatenate(
        [sums - high, jnp.zeros_like(high)], axis=0
    ).astype(bf16)
    through = dot(state_ref[0], q_feat)
    scores = through[spread_rows : spread_rows + 8] + through[spread_rows + 16 : spread_rows + 24]
    den = jnp.sum(hot * scores, axis=0, keepdims=True) + (seg >= count).astype(f32)
    out = masked_sum(seg, through, count) / den
    out_ref[...] = out
    den_ref[0] = jnp.broadcast_to(den, den_ref.shape[1:])
    mixed_ref[pl.ds(pl.multiple_of(h * HEAD_DIM, HEAD_DIM), HEAD_DIM), :] = out.astype(bf16)

    @pl.when(h == heads - 1)
    def _():
        for s, piece in enumerate((p0_ref, p1_ref, p2_ref, p3_ref)):
            piece[...] = mixed_ref[:, lanes(lax.bitwise_xor(place_ref[0], s), local)]


def attend(xt, weights, biases, proj, lengths, place):
    shards, depth, local = xt.shape
    heads, head_dim, feat = proj.shape
    total = shards * local
    count = lengths.shape[1] - 1
    width = heads * head_dim
    state_rows = count * head_dim + 32
    smem = pl.BlockSpec(memory_space=pltpu.SMEM)

    def whole(*shape):
        return pl.BlockSpec(shape, lambda h: (0,) * len(shape))

    def per_head(*shape):
        return pl.BlockSpec((1,) + shape, lambda h: (h,) + (0,) * len(shape))

    return pl.pallas_call(
        functools.partial(attend_kernel, count),
        grid=(heads,),
        in_specs=[
            smem,
            smem,
            whole(shards, depth, local),
        ]
        + [whole(width, depth)] * 3
        + [whole(1, width)] * 3
        + [per_head(head_dim, feat)],
        out_specs=[
            whole(3 * width, total),
            per_head(feat, total),
            per_head(feat, total),
            per_head(state_rows, feat),
            pl.BlockSpec((head_dim, total), lambda h: (h, 0)),
            per_head(8, total),
        ]
        + [whole(width, local)] * shards,
        out_shape=[
            jax.ShapeDtypeStruct((3 * width, total), bf16),
            jax.ShapeDtypeStruct((heads, feat, total), bf16),
            jax.ShapeDtypeStruct((heads, feat, total), bf16),
            jax.ShapeDtypeStruct((heads, state_rows, feat), bf16),
            jax.ShapeDtypeStruct((width, total), f32),
            jax.ShapeDtypeStruct((heads, 8, total), f32),
        ]
        + [jax.ShapeDtypeStruct((width, local), bf16)] * shards,
        scratch_shapes=[pltpu.VMEM((width, total), bf16)],
        compiler_params=pltpu.CompilerParams(vmem_limit_bytes=60 << 20),
        cost_estimate=cost(8),
        name="attend",
    )(lengths, place, xt, *weights, *biases, proj)


def feature_back_rows(grad_feat, feat, vectors, proj_w):
    scale = HEAD_DIM ** (-0.25)
    grad_proj = grad_feat * feat.astype(f32)
    pulled = scale * dot(proj_w, grad_proj.astype(bf16))
    return pulled - (scale * scale) * vectors.astype(f32) * jnp.sum(grad_proj, axis=0, keepdims=True)


def attend_back_kernel(
    count,
    lengths_ref,
    place_ref,
    qkv_ref,
    qf_ref,
    kf_ref,
    state_ref,
    out_ref,
    den_ref,
    g0_ref,
    g1_ref,
    g2_ref,
    g3_ref,
    proj_ref,
    weight_ref,
    sums_ref,
    grad_ref,
    send_ref,
    keep_ref,
    heads_ref,
    small_ref,
):
    h = pl.program_id(0)
    width, local = g0_ref.shape
    shards = grad_ref.shape[1] // local
    depth = weight_ref.shape[0]
    heads = pl.num_programs(0)
    spread_rows = count * HEAD_DIM

    @pl.when(h == 0)
    def _():
        for s, piece in enumerate((g0_ref, g1_ref, g2_ref, g3_ref)):
            heads_ref[:, lanes(lax.bitwise_xor(place_ref[0], s), local)] = piece[...]

    def at(kind):
        return pl.ds(pl.multiple_of(kind * width + h * HEAD_DIM, HEAD_DIM), HEAD_DIM)

    seg = segments(lengths_ref, count, (1, shards * local))
    hot = one_hot_rows(seg, count)
    query, key, value = qkv_ref[at(0), :], qkv_ref[at(1), :], qkv_ref[at(2), :]
    q_feat, k_feat = qf_ref[0], kf_ref[0]
    grad_head = heads_ref[pl.ds(pl.multiple_of(h * HEAD_DIM, HEAD_DIM), HEAD_DIM), :].astype(f32)
    den = den_ref[0, 0:1, :]
    grad_numer = (grad_head / den).astype(bf16)
    grad_den = -jnp.sum(grad_head * out_ref[...], axis=0, keepdims=True) / den
    marked = hot * grad_den
    high = marked.astype(bf16).astype(f32)
    low = marked - high
    numer_wide = jnp.concatenate(
        masked_copies(seg, grad_numer, count)
        + [
            jnp.concatenate([high, low], axis=0).astype(bf16),
            jnp.concatenate([high, jnp.zeros_like(high)], axis=0).astype(bf16),
        ],
        axis=0,
    )
    grad_state = dot_cols(numer_wide[: spread_rows + 16], q_feat)
    sums = grad_state[spread_rows : spread_rows + 8] + grad_state[spread_rows + 8 : spread_rows + 16]
    sums_high = sums.astype(bf16).astype(f32)
    grad_state = jnp.concatenate(
        [
            grad_state[:spread_rows].astype(bf16),
            jnp.concatenate([sums_high, sums - sums_high], axis=0).astype(bf16),
        ],
        axis=0,
    )
    value_wide = jnp.concatenate(
        masked_copies(seg, value, count) + [jnp.concatenate([hot, hot], axis=0).astype(bf16)], axis=0
    )
    proj_w = proj_ref[0]
    grad_qfeat = dot_rows(state_ref[0], numer_wide)
    grad_ref[at(0), :] = feature_back_rows(grad_qfeat, q_feat, query, proj_w).astype(bf16)
    grad_kfeat = dot_rows(grad_state, value_wide)
    grad_ref[at(1), :] = feature_back_rows(grad_kfeat, k_feat, key, proj_w).astype(bf16)
    grad_ref[at(2), :] = masked_sum(seg, dot(grad_state[:spread_rows], k_feat), count).astype(bf16)

    @pl.when(h == heads - 1)
    def _():
        small_ref[...] = sums_ref[...]
        totals = dot_cols(jnp.ones((8, shards * local), bf16), grad_ref[...])
        for t in range(shards):

            @pl.when(place_ref[0] == t)
            def _():
                for kind, row in enumerate(BIAS_ROWS):
                    small_ref[row : row + 1, t * width : (t + 1) * width] = totals[
                        0:1, kind * width : (kind + 1) * width
                    ]

        small = jnp.concatenate(
            [small_ref[:, begin : begin + local] for begin in range(0, depth, local)], axis=0
        )
        rows = small.shape[0]
        high = small.astype(bf16)
        low = (small - high.astype(f32)).astype(bf16)
        for s in range(shards):
            out = (keep_ref, send_ref)[s % 2].at[s // 2]
            out[:depth] = dot(
                weight_ref[...], grad_ref[:, lanes(lax.bitwise_xor(place_ref[0], s), local)]
            ).astype(bf16)
            out[depth : depth + rows] = high
            out[depth + rows :] = low


def attend_back(saved, pieces, proj, weight, sums, lengths, place):
    qkv, qf, kf, state, out, den = saved
    heads, feat, total = qf.shape
    width, local = pieces[0].shape
    shards = total // local
    depth = weight.shape[0]
    count = lengths.shape[1] - 1
    state_rows = state.shape[1]
    extra = 2 * sums.shape[0] * (depth // local)
    smem = pl.BlockSpec(memory_space=pltpu.SMEM)

    def whole(*shape):
        return pl.BlockSpec(shape, lambda h: (0,) * len(shape))

    def per_head(*shape):
        return pl.BlockSpec((1,) + shape, lambda h: (h,) + (0,) * len(shape))

    return pl.pallas_call(
        functools.partial(attend_back_kernel, count),
        grid=(heads,),
        in_specs=[
            smem,
            smem,
            whole(3 * width, total),
            per_head(feat, total),
            per_head(feat, total),
            per_head(state_rows, feat),
            pl.BlockSpec((HEAD_DIM, total), lambda h: (h, 0)),
            per_head(8, total),
        ]
        + [whole(width, local)] * shards
        + [per_head(HEAD_DIM, feat), whole(depth, 3 * width), whole(*sums.shape)],
        out_specs=[
            whole(3 * width, total),
            whole(shards // 2, depth + extra, local),
            whole(shards // 2, depth + extra, local),
        ],
        out_shape=[
            jax.ShapeDtypeStruct((3 * width, total), bf16),
            jax.ShapeDtypeStruct((shards // 2, depth + extra, local), bf16),
            jax.ShapeDtypeStruct((shards // 2, depth + extra, local), bf16),
        ],
        scratch_shapes=[pltpu.VMEM((width, total), bf16), pltpu.VMEM(sums.shape, f32)],
        compiler_params=pltpu.CompilerParams(vmem_limit_bytes=28 << 20),
        cost_estimate=cost(9),
        name="attend_back",
    )(lengths, place, qkv, qf, kf, state, out, den, *pieces, proj, weight, sums)


def slot_place(slot, half):
    k = slot // 2
    if half == 0:
        return 1 - k % 2, k // 2
    return 1 - k // 2, k % 2


def pick_blocks(own, turned_ref):
    slots = turned_ref.shape[0]
    return jnp.concatenate([turned_ref[lax.bitwise_xor(own, slot)] for slot in range(0, slots, 2)], axis=0)


def emit_slots(entries, outs, begin=0):
    height = outs[0].shape[2]
    count = entries.shape[1]
    for half in range(2):

        @pl.when(pl.program_id(0) // 2 == half)
        def _():
            for k in range(PLANE // 2):
                part, index = slot_place(2 * k, half)
                outs[2 * half + part][index, 0, :, begin : begin + count] = entries[k * height : (k + 1) * height]


def slot_outputs(shards, height, count):
    low = pl.BlockSpec((2, 1, height, count), lambda s: (0, jnp.minimum(s, 1), 0, 0))
    high = pl.BlockSpec((2, 1, height, count), lambda s: (0, jnp.maximum(s - 2, 0), 0, 0))
    shape = jax.ShapeDtypeStruct((2, shards // 2, height, count), bf16)
    return [low, low, high, high], [shape] * 4


def output_grad_kernel(own_ref, turned_ref, turned_far_ref, act_ref, act_far_ref, *outs):
    own = own_ref[0]
    grads = dot(pick_blocks(own, turned_ref), act_ref[0]) + dot(pick_blocks(own, turned_far_ref), act_far_ref[0])
    emit_slots(grads.astype(bf16), outs)


def output_grad(own, turned, turned_far, acts, acts_far):
    shards, rows, hidden = acts.shape
    slots, height, _ = turned.shape
    specs, shapes = slot_outputs(shards, height, hidden)
    whole = pl.BlockSpec((slots, height, rows), lambda s: (0, 0, 0))
    by_shard = pl.BlockSpec((1, rows, hidden), lambda s: (s, 0, 0))
    return pl.pallas_call(
        output_grad_kernel,
        grid=(shards,),
        in_specs=[pl.BlockSpec(memory_space=pltpu.SMEM), whole, whole, by_shard, by_shard],
        out_specs=specs,
        out_shape=shapes,
        compiler_params=pltpu.CompilerParams(vmem_limit_bytes=16 << 20),
        cost_estimate=cost(4),
        name="output_grad",
    )(own, turned, turned_far, acts, acts_far)


def hidden_grad_kernel(
    own_ref,
    first_ref,
    first_far_ref,
    grad_pre_ref,
    grad_pre_far_ref,
    branch_ref,
    branch_far_ref,
    mixed_ref,
    mixed_far_ref,
    *outs,
):
    own = own_ref[0]
    hidden = grad_pre_ref.shape[2]
    grads = dot(pick_blocks(own, first_ref), grad_pre_ref[0]) + dot(
        pick_blocks(own, first_far_ref), grad_pre_far_ref[0]
    )
    emit_slots(grads.astype(bf16), outs)
    grads = dot_cols(pick_blocks(own, branch_ref), mixed_ref[0]) + dot_cols(
        pick_blocks(own, branch_far_ref), mixed_far_ref[0]
    )
    emit_slots(grads.astype(bf16), outs, hidden)


def hidden_grad(own, first, first_far, grad_pre, grad_pre_far, branch, branch_far, mixed, mixed_far):
    shards, rows, hidden = grad_pre.shape
    slots, height, _ = first.shape
    width = mixed.shape[1]
    specs, shapes = slot_outputs(shards, height, hidden + width)
    whole = pl.BlockSpec((slots, height, rows), lambda s: (0, 0, 0))
    by_shard = pl.BlockSpec((1, rows, hidden), lambda s: (s, 0, 0))
    piece = pl.BlockSpec((1, width, rows), lambda s: (s, 0, 0))
    return pl.pallas_call(
        hidden_grad_kernel,
        grid=(shards,),
        in_specs=[
            pl.BlockSpec(memory_space=pltpu.SMEM),
            whole,
            whole,
            by_shard,
            by_shard,
            whole,
            whole,
            piece,
            piece,
        ],
        out_specs=specs,
        out_shape=shapes,
        compiler_params=pltpu.CompilerParams(vmem_limit_bytes=16 << 20),
        cost_estimate=cost(5),
        name="hidden_grad",
    )(own, first, first_far, grad_pre, grad_pre_far, branch, branch_far, mixed, mixed_far)


def qkv_grad_kernel(own_ref, xt_ref, grad_ref, even_ref, odd_ref, hold_ref):
    shards, _, local = xt_ref.shape
    grads = sum(
        dot_cols(xt_ref[d], grad_ref[:, d * local : (d + 1) * local]) for d in range(shards)
    )
    hold_ref[...] = grads.astype(bf16).reshape(hold_ref.shape)
    rows = even_ref.shape[4]
    for slot in range(hold_ref.shape[0]):
        target = odd_ref if slot % 2 else even_ref
        block = hold_ref[lax.bitwise_xor(own_ref[0], slot)]
        for half in range(2):
            target[(half,) + slot_place(slot, half) + (0,)] = block[half * rows : (half + 1) * rows]


def qkv_grad(own, slots, xt, grads):
    shards, depth, local = xt.shape
    count = grads.shape[0]
    vmem = pl.BlockSpec(memory_space=pltpu.VMEM)
    shape = jax.ShapeDtypeStruct((2, 2, slots // 4, 1, depth // slots // 2, count), bf16)
    return pl.pallas_call(
        qkv_grad_kernel,
        in_specs=[pl.BlockSpec(memory_space=pltpu.SMEM), vmem, vmem],
        out_specs=[vmem, vmem],
        out_shape=[shape, shape],
        scratch_shapes=[pltpu.VMEM((slots, depth // slots, count), bf16)],
        compiler_params=pltpu.CompilerParams(vmem_limit_bytes=16 << 20),
        cost_estimate=cost(2),
        name="qkv_grad",
    )(own, xt, grads)


def norm_rows(resid):
    center = resid - jnp.mean(resid, axis=-1, keepdims=True)
    inverse = lax.rsqrt(jnp.mean(center * center, axis=-1, keepdims=True) + eps)
    return center * inverse, inverse


HELD = [(0, (0, 1, 2, 3)), (2, (0, 1, 2, 3)), (4, (0, 1, 2, 3)), (6, (0, 1)), (6, (2, 3))]
HELD = HELD + [(mask ^ 1, shards) for mask, shards in HELD]


def place_copies(own, held, begin, rows, target, sems):
    columns = held[0].shape[2]
    copies = [[] for _ in range(target.shape[0])]
    for piece, (mask, shards) in zip(held, HELD):
        source = lax.bitwise_xor(own, mask)
        chip = lax.shift_right_logical(source, 1)
        core = lax.bitwise_and(source, 1)
        for index, s in enumerate(shards):
            copies[s].append(
                pltpu.make_async_copy(
                    piece.at[index, pl.ds(begin, rows), :],
                    target.at[s, chip, :, lanes(core, columns)],
                    sems.at[s, mask],
                )
            )
    return copies


def start_all(copies):
    for entries in copies:
        for copy in entries:
            copy.start()


def wait_all(entries):
    for copy in entries:
        copy.wait()


def ffn_up_kernel(
    own_ref,
    tokens_ref,
    p0_ref,
    p1_ref,
    p2_ref,
    p3_ref,
    mixer_bias_ref,
    gain_ref,
    shift_ref,
    *refs,
):
    held, refs = refs[: len(HELD)], refs[len(HELD) :]
    parts, refs = refs[:4], refs[4:]
    (
        normed_ref,
        inverse_ref,
        turned_ref,
        mixed_ref,
        act_ref,
        slope_ref,
        mixer_ref,
        hidden_ref,
        bias_ref,
        mixer_sem,
        hidden_sem,
        bias_sem,
    ) = refs
    own = own_ref[0]
    shards, chips, mixer_rows, depth = mixer_ref.shape
    hidden_rows = hidden_ref.shape[2]
    mixer_copies = place_copies(own, held, hidden_rows, mixer_rows, mixer_ref, mixer_sem)
    hidden_copies = place_copies(own, held, 0, hidden_rows, hidden_ref, hidden_sem)
    bias_rows = parts[0].shape[0] - 16
    bias_copies = [
        pltpu.make_async_copy(part.at[bias_rows : bias_rows + 16], bias_ref.at[s], bias_sem.at[s])
        for s, part in enumerate(parts)
    ]
    start_all(mixer_copies)
    start_all(hidden_copies)
    start_all([bias_copies])
    resid = tokens_ref[...].astype(f32) + mixer_bias_ref[...]
    for s, piece in enumerate((p0_ref, p1_ref, p2_ref, p3_ref)):
        mixed_ref[s] = piece[...]
        wait_all(mixer_copies[s])
        resid = resid + dot_rows(piece[...], mixer_ref[s].reshape(chips * mixer_rows, depth))
    normed, inverse = norm_rows(resid)
    normed_ref[...] = normed
    inverse_ref[...] = jnp.broadcast_to(inverse, inverse_ref.shape)
    first_low = (normed * gain_ref[...] + shift_ref[...]).astype(bf16)
    turned_ref[...] = first_low.T
    for s in range(shards):
        wait_all(hidden_copies[s] + [bias_copies[s]])
        bias = unpack_bias(bias_ref[s])
        pre = dot(first_low, hidden_ref[s].reshape(chips * hidden_rows, hidden_ref.shape[3])) + bias
        phi = 0.5 * (1.0 + lax.erf(pre * math.sqrt(0.5)))
        act_ref[s] = (pre * phi).astype(bf16)
        slope_ref[s] = (
            phi + pre * jnp.exp(-0.5 * pre * pre) * (1.0 / math.sqrt(2.0 * math.pi))
        ).astype(bf16)


def ffn_up(own, tokens, pieces, mixer_bias, gain, shift_by, parts, held, mixer_rows):
    rows, depth = tokens.shape
    shards = len(pieces)
    chips = PLANE // 2
    hidden = 2 * held[0].shape[2]
    hidden_rows = held[0].shape[1] - mixer_rows
    vmem = pl.BlockSpec(memory_space=pltpu.VMEM)
    return pl.pallas_call(
        ffn_up_kernel,
        in_specs=[pl.BlockSpec(memory_space=pltpu.SMEM)]
        + [vmem] * (1 + shards + 3)
        + [pl.BlockSpec(memory_space=pltpu.HBM)] * (len(HELD) + shards),
        out_specs=[vmem] * 6,
        out_shape=[
            jax.ShapeDtypeStruct((rows, depth), f32),
            jax.ShapeDtypeStruct((rows, 128), f32),
            jax.ShapeDtypeStruct((depth, rows), bf16),
            jax.ShapeDtypeStruct((shards,) + pieces[0].shape, bf16),
            jax.ShapeDtypeStruct((shards, rows, hidden), bf16),
            jax.ShapeDtypeStruct((shards, rows, hidden), bf16),
        ],
        scratch_shapes=[
            pltpu.VMEM((shards, chips, mixer_rows, depth), bf16),
            pltpu.VMEM((shards, chips, hidden_rows, hidden), bf16),
            pltpu.VMEM((shards, 16, held[0].shape[2]), bf16),
            pltpu.SemaphoreType.DMA((shards, PLANE)),
            pltpu.SemaphoreType.DMA((shards, PLANE)),
            pltpu.SemaphoreType.DMA((shards,)),
        ],
        compiler_params=pltpu.CompilerParams(vmem_limit_bytes=28 << 20),
        cost_estimate=cost(8),
        name="ffn_up",
    )(own, tokens, *pieces, mixer_bias, gain, shift_by, *held, *parts)


def norm_rows_back(scaled, normed, inverse):
    return inverse * (
        scaled
        - jnp.mean(scaled, axis=-1, keepdims=True)
        - normed * jnp.mean(scaled * normed, axis=-1, keepdims=True)
    )


def column_sum(entries):
    return jnp.sum(entries, axis=0, keepdims=True)


def ffn_down_kernel(
    own_ref,
    normed_ref,
    inverse_ref,
    act_ref,
    slope_ref,
    cotangent_ref,
    first_gain_ref,
    first_shift_ref,
    output_bias_ref,
    gain_ref,
    shift_ref,
    *refs,
):
    held, refs = refs[: len(HELD)], refs[len(HELD) :]
    held_out, refs = refs[: len(HELD)], refs[len(HELD) :]
    (
        layer_ref,
        resid_ref,
        b0_ref,
        b1_ref,
        b2_ref,
        b3_ref,
        grad_ffn_ref,
        grad_pre_ref,
        grad_branch_ref,
        sums_ref,
        mixer_ref,
        hidden_ref,
        output_ref,
        mixer_sem,
        hidden_sem,
        output_sem,
    ) = refs
    own, place = own_ref[0], own_ref[1]
    shards, chips, mixer_rows, depth = mixer_ref.shape
    hidden_rows = hidden_ref.shape[2]
    hidden = hidden_ref.shape[3]
    output_copies = place_copies(own, held_out, 0, output_ref.shape[2], output_ref, output_sem)
    hidden_copies = place_copies(own, held, 0, hidden_rows, hidden_ref, hidden_sem)
    mixer_copies = place_copies(own, held, hidden_rows, mixer_rows, mixer_ref, mixer_sem)
    start_all(output_copies)
    start_all(hidden_copies)
    start_all(mixer_copies)
    normed_one = normed_ref[...]
    resid = normed_one * first_gain_ref[...] + first_shift_ref[...] + output_bias_ref[...]
    for s in range(shards):
        wait_all(output_copies[s])
        resid = resid + dot(act_ref[s], output_ref[s].reshape(hidden, depth))
    normed, inverse = norm_rows(resid)
    layer_ref[...] = (normed * gain_ref[...] + shift_ref[...]).astype(bf16)
    grad_out = cotangent_ref[...].astype(f32)
    sums_ref[0:1] = column_sum(grad_out * normed)
    sums_ref[1:2] = column_sum(grad_out)
    grad_two = norm_rows_back(grad_out * gain_ref[...], normed, inverse)
    grad_ffn = grad_two.astype(bf16)
    grad_ffn_ref[...] = grad_ffn.T
    sums_ref[2:3] = column_sum(grad_ffn.astype(f32))
    grad_first = grad_two
    for s in range(shards):
        grad_pre = (
            dot_cols(grad_ffn, output_ref[s].reshape(hidden, depth)) * slope_ref[s].astype(f32)
        ).astype(bf16)
        grad_pre_ref[s] = grad_pre
        sums_ref[pl.ds(8 + lax.bitwise_xor(place, s), 1)] = column_sum(grad_pre.astype(f32))
        wait_all(hidden_copies[s])
        grad_first = grad_first + dot_cols(grad_pre, hidden_ref[s].reshape(depth, hidden))
    sums_ref[3:4] = column_sum(grad_first * normed_one)
    sums_ref[4:5] = column_sum(grad_first)
    grad_one = norm_rows_back(grad_first * first_gain_ref[...], normed_one, inverse_ref[:, 0:1])
    resid_ref[...] = grad_one
    grad_branch = grad_one.astype(bf16)
    branch_turned = grad_branch.T
    grad_branch_ref[...] = branch_turned
    sums_ref[5:6] = column_sum(grad_branch.astype(f32))
    sums_ref[6:8] = jnp.zeros((2, depth), f32)
    sums_ref[8 + shards :] = jnp.zeros((8 - shards, depth), f32)
    for s, back in enumerate((b0_ref, b1_ref, b2_ref, b3_ref)):
        wait_all(mixer_copies[s])
        back[...] = dot(mixer_ref[s].reshape(chips * mixer_rows, depth), branch_turned).astype(bf16)


def ffn_down(own, normed, inverse, acts, slopes, cotangent, vectors, held, held_out, mixer_rows):
    rows, depth = normed.shape
    shards, _, hidden = acts.shape
    chips = PLANE // 2
    hidden_rows = held[0].shape[1] - mixer_rows
    output_rows = held_out[0].shape[1]
    vmem = pl.BlockSpec(memory_space=pltpu.VMEM)
    width = chips * mixer_rows
    return pl.pallas_call(
        ffn_down_kernel,
        in_specs=[pl.BlockSpec(memory_space=pltpu.SMEM)]
        + [vmem] * 10
        + [pl.BlockSpec(memory_space=pltpu.HBM)] * (2 * len(HELD)),
        out_specs=[vmem] * (6 + shards),
        out_shape=[
            jax.ShapeDtypeStruct((rows, depth), bf16),
            jax.ShapeDtypeStruct((rows, depth), f32),
        ]
        + [jax.ShapeDtypeStruct((width, rows), bf16)] * shards
        + [
            jax.ShapeDtypeStruct((depth, rows), bf16),
            jax.ShapeDtypeStruct((shards, rows, hidden), bf16),
            jax.ShapeDtypeStruct((depth, rows), bf16),
            jax.ShapeDtypeStruct((16, depth), f32),
        ],
        scratch_shapes=[
            pltpu.VMEM((shards, chips, mixer_rows, depth), bf16),
            pltpu.VMEM((shards, chips, hidden_rows, hidden), bf16),
            pltpu.VMEM((shards, chips, output_rows, depth), bf16),
            pltpu.SemaphoreType.DMA((shards, PLANE)),
            pltpu.SemaphoreType.DMA((shards, PLANE)),
            pltpu.SemaphoreType.DMA((shards, PLANE)),
        ],
        compiler_params=pltpu.CompilerParams(vmem_limit_bytes=36 << 20),
        cost_estimate=cost(15),
        name="ffn_down",
    )(own, normed, inverse, acts, slopes, cotangent, *vectors, *held, *held_out)


def fold_kernel(depth, keep_ref, far_ref, mine_ref, other_ref):
    rows = (keep_ref.shape[1] - depth) // 2
    for s, out in enumerate((mine_ref, other_ref)):
        out[:depth] = (keep_ref[s, :depth].astype(f32) + far_ref[s, :depth].astype(f32)).astype(bf16)
        small = sum(
            ref[s, depth : depth + rows].astype(f32) + ref[s, depth + rows :].astype(f32) for ref in (keep_ref, far_ref)
        )
        high = small.astype(bf16)
        out[depth : depth + rows] = high
        out[depth + rows :] = (small - high.astype(f32)).astype(bf16)


def fold(depth, keep, far):
    vmem = pl.BlockSpec(memory_space=pltpu.VMEM)
    return pl.pallas_call(
        functools.partial(fold_kernel, depth),
        in_specs=[vmem] * 2,
        out_specs=[vmem] * 2,
        out_shape=[jax.ShapeDtypeStruct(keep.shape[1:], bf16)] * 2,
        compiler_params=pltpu.CompilerParams(vmem_limit_bytes=16 << 20),
        cost_estimate=cost(2),
        name="fold",
    )(keep, far)


def join_cores_kernel(near_ref, far_ref, *outs):
    for half in range(2):
        for part in range(2):
            outs[2 * half + part][...] = (
                near_ref[half, part].astype(f32) + far_ref[half, part].astype(f32)
            ).astype(bf16)


def join_cores(near, far):
    vmem = pl.BlockSpec(memory_space=pltpu.VMEM)
    return pl.pallas_call(
        join_cores_kernel,
        in_specs=[vmem] * 2,
        out_specs=[vmem] * 4,
        out_shape=[jax.ShapeDtypeStruct(near.shape[2:], bf16)] * 4,
        compiler_params=pltpu.CompilerParams(vmem_limit_bytes=16 << 20),
        cost_estimate=cost(2),
        name="join_cores",
    )(near, far)


def finish_tokens_kernel(resid_ref, mine_ref, far_ref, out_ref, small_ref):
    depth = resid_ref.shape[1]
    rows = small_ref.shape[0]
    total = mine_ref[:depth].astype(f32) + far_ref[:depth].astype(f32)
    out_ref[...] = resid_ref[...] + total.T
    small_ref[...] = sum(
        ref[depth : depth + rows].astype(f32) + ref[depth + rows :].astype(f32) for ref in (mine_ref, far_ref)
    )


def finish_tokens(resid, mine, far):
    local, depth = resid.shape
    rows = (mine.shape[0] - depth) // 2
    vmem = pl.BlockSpec(memory_space=pltpu.VMEM)
    return pl.pallas_call(
        finish_tokens_kernel,
        in_specs=[vmem] * 3,
        out_specs=[vmem] * 2,
        out_shape=[jax.ShapeDtypeStruct(resid.shape, f32), jax.ShapeDtypeStruct((rows, local), f32)],
        compiler_params=pltpu.CompilerParams(vmem_limit_bytes=16 << 20),
        cost_estimate=cost(1),
        name="finish_tokens",
    )(resid, mine, far)


def finish_hidden_kernel(a_ref, b_ref, hidden_ref, mixer_ref):
    total = a_ref[...].astype(f32) + b_ref[...].astype(f32)
    hidden = hidden_ref.shape[1]
    hidden_ref[...] = total[:, :hidden]
    mixer_ref[...] = total[:, hidden:].T


def finish_hidden(entries, hidden):
    rows, columns = entries[0].shape
    vmem = pl.BlockSpec(memory_space=pltpu.VMEM)
    return pl.pallas_call(
        finish_hidden_kernel,
        in_specs=[vmem] * 2,
        out_specs=[vmem] * 2,
        out_shape=[
            jax.ShapeDtypeStruct((rows, hidden), f32),
            jax.ShapeDtypeStruct((columns - hidden, rows), f32),
        ],
        compiler_params=pltpu.CompilerParams(vmem_limit_bytes=60 << 20),
        cost_estimate=cost(1),
        name="finish_hidden",
    )(*entries)


def finish_qkv_kernel(a_ref, b_ref, c_ref, d_ref, query_ref, key_ref, value_ref):
    rows, width = a_ref.shape[0], query_ref.shape[1]
    low = a_ref[...].astype(f32) + b_ref[...].astype(f32)
    high = c_ref[...].astype(f32) + d_ref[...].astype(f32)
    for kind, out in enumerate((query_ref, key_ref, value_ref)):
        out[:rows] = low[:, kind * width : (kind + 1) * width]
        out[rows:] = high[:, kind * width : (kind + 1) * width]


def finish_qkv(entries):
    rows, columns = entries[0].shape
    vmem = pl.BlockSpec(memory_space=pltpu.VMEM)
    return pl.pallas_call(
        finish_qkv_kernel,
        in_specs=[vmem] * 4,
        out_specs=[vmem] * 3,
        out_shape=[jax.ShapeDtypeStruct((2 * rows, columns // 3), f32)] * 3,
        compiler_params=pltpu.CompilerParams(vmem_limit_bytes=60 << 20),
        cost_estimate=cost(1),
        name="finish_qkv",
    )(*entries)


BIAS_ROWS = (6, 7, 12)


def swap(values, mask):
    size = lax.axis_size("dp")
    return lax.ppermute(values, "dp", [(i, i ^ mask) for i in range(size)])


def cross(values, mask):
    size = lax.axis_size("tensor")
    return lax.ppermute(values, "tensor", [(i, i ^ mask) for i in range(size)])


def after(values, *others):
    return lax.optimization_barrier((values, others))[0]


def spread_shards(payload):
    return [payload] + [cross(payload, s) for s in range(1, lax.axis_size("tensor"))]


def spread_plane(parts, before=(), between=()):
    stack = after(jnp.stack(parts), *before)
    over_x, over_y = after((swap(stack, 2), swap(stack, 4)), *between)
    return stack, over_x, over_y, swap(over_x[:2], 4), swap(over_y[2:], 2)


def both_cores(held, before=()):
    first = after(held[:3], *before)
    return list(held) + [swap(entry, 1) for entry in first] + [swap(entry, 1) for entry in held[3:]]


def add_low(*entries):
    return sum(entry.astype(f32) for entry in entries).astype(bf16)


def sum_first(near, before=(), between=()):
    send_low, keep_low, send_high, keep_high = near
    send_low, send_high = after((send_low, send_high), *before)
    low, high = after((swap(send_low, 2), swap(send_high, 4)), *between)
    return (
        [add_low(keep_low[0], low[0]), add_low(keep_high[0], high[0])],
        [add_low(keep_low[1], low[1]), add_low(keep_high[1], high[1])],
    )


def sum_second(stay, send, between=()):
    low, high = after((swap(send[0], 4), swap(send[1], 2)), *between)
    return [add_low(stay[0], low), add_low(stay[1], high)]


def scatter_all(halves, axis):
    parts = []
    for half in range(2):
        blocks = []
        for i in range(PLANE):
            part, index = slot_place(i, half)
            blocks.append(halves[i % 2][2 * half + part][index])
        parts.append(jnp.stack(blocks, axis=1))
    whole = jnp.concatenate(parts, axis=axis)
    whole = whole.reshape(whole.shape[:1] + (-1,) + whole.shape[-1:])
    return lax.psum_scatter(whole, "dp", scatter_dimension=1, tiled=True)


def pair_shards(grads):
    return after(jnp.stack([grads[1], grads[3]]))


def join_shards(grads, pair, between=()):
    near = after(cross(pair, 1), *between)
    mine, other = add_low(grads[0], near[0]), add_low(grads[2], near[1])
    return mine, cross(other, 2)


def by_shard(halves):
    return [half[s] for half in halves for s in range(half.shape[0])]


def small_sum(values):
    size = lax.axis_size("dp")
    if size != PLANE:
        values = lax.psum(values, "dp")
    else:
        for mask in (1, 2, 4):
            values = values + swap(values, mask)
    return values


def body(
    tokens,
    lengths,
    query_weight,
    query_bias,
    key_weight,
    key_bias,
    value_weight,
    value_bias,
    feature_proj,
    mixer_weight,
    mixer_bias,
    first_gain,
    first_shift,
    hidden_weight,
    hidden_bias,
    output_weight,
    output_bias,
    second_gain,
    second_shift,
    cotangent,
):
    depth = tokens.shape[1]
    shards = lax.axis_size("tensor")
    place = lax.axis_index("tensor").astype(jnp.int32)
    plane = (lax.axis_index("dp") % PLANE).astype(jnp.int32)
    width = query_weight.shape[1]
    hidden = hidden_weight.shape[1]
    mixer_rows = mixer_weight.shape[0] // (PLANE // 2)
    own = jnp.stack([plane, place])
    slot_of = plane[None] if lax.axis_size("dp") == PLANE else jnp.zeros((1,), jnp.int32)

    def row(vector):
        return vector.reshape(1, -1)

    def blocks(turned):
        return turned.reshape(PLANE, turned.shape[0] // PLANE, turned.shape[1])

    own_xt, payload, payload_out = pack(
        own, tokens, hidden_bias.reshape(-1, 128), hidden_weight, mixer_weight, output_weight
    )
    parts = spread_shards(payload)
    weights = (query_weight.T, key_weight.T, value_weight.T)
    qkv_weight = prepare(after(weights, payload))
    xt = lax.all_gather(after(own_xt, qkv_weight), "tensor", axis=0, tiled=False)
    rows = payload.shape[0] - 16
    around = spread_plane([part[:rows] for part in parts])
    parts_out = spread_shards(after(payload_out, *parts))
    around = around[:3] + after(around[3:], *parts_out)
    held = both_cores(around, around[3:])
    *saved, p0, p1, p2, p3 = attend(
        after(xt, *around),
        weights,
        [row(query_bias), row(key_bias), row(value_bias)],
        feature_proj,
        lengths,
        place[None],
    )
    around_out = spread_plane(parts_out, around, (p0,))
    pieces = [p0] + [cross(p, s) for s, p in ((1, p1), (2, p2), (3, p3))]
    held_out = both_cores(around_out, pieces)
    normed, inverse, turned, mixed, acts, slopes = ffn_up(
        own, tokens, pieces, row(mixer_bias), row(first_gain), row(first_shift), parts, held, mixer_rows
    )
    acts_far, turned_far, mixed_far = swap(acts, 1), swap(turned, 1), swap(mixed, 1)
    held_out = after(held_out, turned_far, mixed_far)
    vectors = [row(v) for v in (first_gain, first_shift, output_bias, second_gain, second_shift)]
    layer_out, grad_resid, b0, b1, b2, b3, grad_ffn, grad_pre, grad_branch, sums = ffn_down(
        own, normed, inverse, acts, slopes, cotangent, vectors, held, held_out, mixer_rows
    )
    back = [b0] + [cross(b, s) for s, b in ((1, b1), (2, b2), (3, b3))]
    output_work = (blocks(grad_ffn), blocks(swap(grad_ffn, 1)), acts, acts_far)
    hidden_work = (
        blocks(turned),
        blocks(turned_far),
        grad_pre,
        swap(grad_pre, 1),
        blocks(grad_branch),
        blocks(swap(grad_branch, 1)),
        mixed,
        mixed_far,
    )
    fast = lax.axis_size("dp") == PLANE
    if fast:
        near_output = output_grad(slot_of, *output_work)
        near_output = after(near_output, hidden_work)
        near_hidden = hidden_grad(slot_of, *hidden_work)
        back = after(back, near_output, near_hidden)
    grad_qkv, send, keep = attend_back(
        saved, back, feature_proj, qkv_weight, sums, lengths, place[None]
    )
    far = cross(send, 1)
    if fast:
        even, odd = qkv_grad(slot_of, PLANE, xt, grad_qkv)
        stay_output, send_output = sum_first(near_output, between=(even,))
        stay_hidden, send_hidden = sum_first(near_hidden, between=send_output)
        near_qkv = join_cores(even, after(swap(odd, 1), send_hidden))
        mine, other = fold(depth, keep, after(far, near_qkv))
        far = cross(other, 2)
        grad_output = by_shard(sum_second(stay_output, send_output, between=(other,)))
        pair_output = pair_shards(grad_output)
        grad_hidden = by_shard(sum_second(stay_hidden, send_hidden, between=(pair_output,)))
        pair_hidden = pair_shards(grad_hidden)
        stay_qkv, send_qkv = sum_first(near_qkv, between=(pair_hidden,))
        grad_output = join_shards(grad_output, pair_output, send_qkv)
        low, high = swap(send_qkv[0], 4), swap(send_qkv[1], 2)
        grad_weights = finish_qkv([entry[0] for entry in (stay_qkv[0], low, stay_qkv[1], high)])
        grad_hidden = join_shards(grad_hidden, pair_hidden, grad_weights)
    else:
        zero, one = jnp.zeros((1,), jnp.int32), jnp.ones((1,), jnp.int32)
        mine, other = fold(depth, keep, far)
        far = cross(other, 2)
        grad_output = scatter_all([output_grad(slot, *output_work) for slot in (zero, one)], 0)
        grad_output = by_shard([0.5 * grad_output])
        grad_output = join_shards(grad_output, pair_shards(grad_output))
        grad_hidden = scatter_all([hidden_grad(slot, *hidden_work) for slot in (zero, one)], 0)
        grad_hidden = by_shard([0.5 * grad_hidden])
        grad_hidden = join_shards(grad_hidden, pair_shards(grad_hidden))
        grad_weight = scatter_all(
            [
                [entry[half, part] for half in range(2) for part in range(2)]
                for entry in qkv_grad(zero, PLANE, xt, grad_qkv)
            ],
            2,
        )[0].astype(f32)
        grad_weights = [grad_weight[:, kind * width : (kind + 1) * width] for kind in range(3)]
    tokens_grad, small = finish_tokens(grad_resid, mine, far)
    small = small_sum(small)
    small = after(small.reshape(-1, 16, small.shape[1]).transpose(1, 0, 2).reshape(16, -1))
    grad_output = sum(entry.astype(f32) for entry in grad_output).T
    grad_hidden, grad_mixer = finish_hidden(grad_hidden, hidden)
    return (
        layer_out,
        tokens_grad,
        grad_weights[0],
        small[6],
        grad_weights[1],
        small[7],
        grad_weights[2],
        small[12],
        grad_mixer,
        small[5],
        small[3],
        small[4],
        grad_hidden,
        small[8 : 8 + shards].reshape(-1),
        grad_output,
        small[2],
        small[0],
        small[1],
    )


def solution(mesh):
    placed = (
        P(("dp", "tensor"), None),
        P("dp", None),
        P(None, "tensor"),
        P("tensor"),
        P(None, "tensor"),
        P("tensor"),
        P(None, "tensor"),
        P("tensor"),
        P("tensor", None, None),
        P("tensor", None),
        P(),
        P(),
        P(),
        P(None, "tensor"),
        P("tensor"),
        P("tensor", None),
        P(),
        P(),
        P(),
        P(("dp", "tensor"), None),
    )
    return jax.shard_map(
        body,
        mesh=mesh,
        in_specs=placed,
        out_specs=(
            P(("dp", "tensor"), None),
            P(("dp", "tensor"), None),
            P("dp", "tensor"),
            P(),
            P("dp", "tensor"),
            P(),
            P("dp", "tensor"),
            P(),
            P("tensor", "dp"),
            P(),
            P(),
            P(),
            P("dp", "tensor"),
            P(),
            P("tensor", "dp"),
            P(),
            P(),
            P(),
        ),
        check_vma=False,
    )
```

```python
import functools
import math

import jax
import jax.numpy as jnp
from jax import lax
from jax.experimental import pallas as pl
from jax.experimental.pallas import tpu as pltpu
from jax.sharding import PartitionSpec as P

HEAD_DIM = 64
FEAT = 256
PLANE = 8
COST_RATE = 9e9

eps = 1e-06
bf16 = jnp.bfloat16
f32 = jnp.float32


def dot(left, right):
    return jnp.dot(left, right, preferred_element_type=f32)


def dot_rows(left, right):
    return lax.dot_general(left, right, (((0,), (0,)), ((), ())), preferred_element_type=f32)


def dot_cols(left, right):
    return lax.dot_general(left, right, (((1,), (1,)), ((), ())), preferred_element_type=f32)


def cost(micros):
    return pl.CostEstimate(flops=int(micros * COST_RATE), transcendentals=0, bytes_accessed=0)


def pack_kernel(
    own_ref, bias_ref, tokens_ref, hidden_ref, mixer_ref, output_ref, first_ref, second_ref, turned_ref, held_ref, sems
):
    rows, columns = second_ref.shape
    chip = lax.shift_right_logical(own_ref[0], 1)
    core = lax.bitwise_and(own_ref[0], 1)
    mixer_rows = mixer_ref.shape[0] // (PLANE // 2)

    def copy(source, height, target, sem):
        begin = pl.multiple_of(chip * height, 16)
        return pltpu.make_async_copy(
            source.at[pl.ds(begin, height), lanes(core, columns)], target, sem
        )

    copies = [
        copy(hidden_ref, rows, first_ref.at[0:rows], sems.at[0]),
        copy(mixer_ref, mixer_rows, first_ref.at[rows : rows + mixer_rows], sems.at[1]),
        copy(output_ref, rows, second_ref, sems.at[2]),
    ]
    fetch = pltpu.make_async_copy(tokens_ref, held_ref, sems.at[3])
    start_all([copies])
    fetch.start()
    wide = jnp.concatenate([bias_ref[...], jnp.zeros((16 - bias_ref.shape[0], 128), f32)], axis=0)
    for index in range(3):
        part = wide.astype(bf16)
        wide = wide - part.astype(f32)
        first_ref[rows + mixer_rows :, index * 128 : (index + 1) * 128] = part
    fetch.wait()
    turned_ref[...] = held_ref[...].T
    wait_all(copies)


def pack(own, tokens, hidden_bias, hidden_weight, mixer_weight, output_weight):
    local, depth = tokens.shape
    chips = PLANE // 2
    columns = depth // 2
    rows = depth // chips
    first_rows = rows + mixer_weight.shape[0] // chips + 16
    vmem = pl.BlockSpec(memory_space=pltpu.VMEM)
    return pl.pallas_call(
        pack_kernel,
        in_specs=[pl.BlockSpec(memory_space=pltpu.SMEM), vmem] + [pl.BlockSpec(memory_space=pltpu.HBM)] * 4,
        out_specs=[vmem] * 3,
        out_shape=[
            jax.ShapeDtypeStruct((first_rows, columns), bf16),
            jax.ShapeDtypeStruct((rows, columns), bf16),
            jax.ShapeDtypeStruct((depth, local), bf16),
        ],
        scratch_shapes=[pltpu.VMEM((local, depth), bf16), pltpu.SemaphoreType.DMA((4,))],
        compiler_params=pltpu.CompilerParams(vmem_limit_bytes=60 << 20),
        cost_estimate=cost(3),
        name="pack",
    )(own, hidden_bias, tokens, hidden_weight, mixer_weight, output_weight)


def unpack_bias(entries):
    wide = entries.astype(f32)
    wide = wide[:, :128] + wide[:, 128:256] + wide[:, 256:384]
    return jnp.concatenate([wide[index : index + 1] for index in range(6)], axis=1)


def prepare_kernel(query_ref, key_ref, value_ref, joined_ref):
    joined_ref[...] = jnp.concatenate([query_ref[...].T, key_ref[...].T, value_ref[...].T], axis=1)


def prepare(weights):
    width, depth = weights[0].shape
    vmem = pl.BlockSpec(memory_space=pltpu.VMEM)
    return pl.pallas_call(
        prepare_kernel,
        in_specs=[vmem] * 3,
        out_specs=vmem,
        out_shape=jax.ShapeDtypeStruct((depth, 3 * width), bf16),
        compiler_params=pltpu.CompilerParams(vmem_limit_bytes=8 << 20),
        cost_estimate=cost(4),
        name="prepare",
    )(*weights)


def lanes(index, size):
    return pl.ds(pl.multiple_of(index * size, size), size)


def segments(lengths_ref, count, shape):
    places = lax.broadcasted_iota(jnp.int32, shape, len(shape) - 1)
    seg = jnp.zeros(shape, jnp.int32)
    end = jnp.int32(0)
    for s in range(count):
        end = end + lengths_ref[0, s]
        seg = seg + (places >= end).astype(jnp.int32)
    return seg


def masked_copies(seg, entries, count):
    zero = jnp.zeros_like(entries)
    return [jnp.where(seg == s, entries, zero) for s in range(count)]


def one_hot_rows(seg, count):
    rows = lax.broadcasted_iota(jnp.int32, (8, seg.shape[1]), 0)
    return jnp.where((rows == seg) & (rows < count), 1.0, 0.0).astype(f32)


def masked_sum(seg, wide, count):
    height = HEAD_DIM
    total = jnp.zeros((height, wide.shape[1]), f32)
    for s in range(count):
        total = total + jnp.where(seg == s, wide[s * height : (s + 1) * height], 0.0)
    return total


def feature_rows(vectors, proj_t):
    scale = HEAD_DIM ** (-0.25)
    widened = vectors.astype(f32)
    square = (0.5 * scale * scale) * jnp.sum(widened * widened, axis=0, keepdims=True)
    return (jnp.exp(scale * dot(proj_t, vectors) - square) * (1.0 / math.sqrt(FEAT))).astype(bf16)


def attend_kernel(
    count,
    lengths_ref,
    place_ref,
    x0_ref,
    x1_ref,
    x2_ref,
    x3_ref,
    query_weight_ref,
    key_weight_ref,
    value_weight_ref,
    query_bias_ref,
    key_bias_ref,
    value_bias_ref,
    proj_ref,
    qkv_ref,
    qf_ref,
    kf_ref,
    state_ref,
    out_ref,
    den_ref,
    p0_ref,
    p1_ref,
    p2_ref,
    p3_ref,
    mixed_ref,
):
    h = pl.program_id(0)
    tokens = (x0_ref, x1_ref, x2_ref, x3_ref)
    shards, local = len(tokens), x0_ref.shape[1]
    heads = pl.num_programs(0)
    width = query_weight_ref.shape[0]
    spread_rows = count * HEAD_DIM

    @pl.when(h == 0)
    def _():
        for kind, (weight, bias) in enumerate(
            (
                (query_weight_ref, query_bias_ref),
                (key_weight_ref, key_bias_ref),
                (value_weight_ref, value_bias_ref),
            )
        ):
            column = jnp.broadcast_to(bias[...], (8, width)).T[:, 0:1]
            for s in range(shards):
                qkv_ref[kind * width : (kind + 1) * width, lanes(lax.bitwise_xor(place_ref[0], s), local)] = (
                    dot(weight[...], tokens[s][...]) + column
                ).astype(bf16)

    def rows(kind):
        begin = pl.multiple_of(kind * width + h * HEAD_DIM, HEAD_DIM)
        return qkv_ref[pl.ds(begin, HEAD_DIM), :]

    seg = segments(lengths_ref, count, (1, shards * local))
    hot = one_hot_rows(seg, count)
    proj_t = proj_ref[0].T
    q_feat = feature_rows(rows(0), proj_t)
    k_feat = feature_rows(rows(1), proj_t)
    qf_ref[0] = q_feat
    kf_ref[0] = k_feat
    wide = jnp.concatenate(
        masked_copies(seg, rows(2), count) + [jnp.concatenate([hot, hot], axis=0).astype(bf16)], axis=0
    )
    state = dot_cols(wide, k_feat)
    sums = state[spread_rows : spread_rows + 8]
    high = sums.astype(bf16).astype(f32)
    state_ref[0, :spread_rows] = state[:spread_rows].astype(bf16)
    state_ref[0, spread_rows : spread_rows + 16] = jnp.concatenate([high, high], axis=0).astype(bf16)
    state_ref[0, spread_rows + 16 :] = jnp.concatenate(
        [sums - high, jnp.zeros_like(high)], axis=0
    ).astype(bf16)
    through = dot(state_ref[0], q_feat)
    scores = through[spread_rows : spread_rows + 8] + through[spread_rows + 16 : spread_rows + 24]
    den = jnp.sum(hot * scores, axis=0, keepdims=True) + (seg >= count).astype(f32)
    out = masked_sum(seg, through, count) / den
    out_ref[...] = out
    den_ref[0] = jnp.broadcast_to(den, den_ref.shape[1:])
    mixed_ref[pl.ds(pl.multiple_of(h * HEAD_DIM, HEAD_DIM), HEAD_DIM), :] = out.astype(bf16)

    @pl.when(h == heads - 1)
    def _():
        for s, piece in enumerate((p0_ref, p1_ref, p2_ref, p3_ref)):
            piece[...] = mixed_ref[:, lanes(lax.bitwise_xor(place_ref[0], s), local)]


def attend(tokens, weights, biases, proj, lengths, place):
    shards, local, depth = len(tokens), tokens[0].shape[1], weights[0].shape[1]
    heads, head_dim, feat = proj.shape
    total = shards * local
    count = lengths.shape[1] - 1
    width = heads * head_dim
    state_rows = count * head_dim + 32
    smem = pl.BlockSpec(memory_space=pltpu.SMEM)

    def whole(*shape):
        return pl.BlockSpec(shape, lambda h: (0,) * len(shape))

    def per_head(*shape):
        return pl.BlockSpec((1,) + shape, lambda h: (h,) + (0,) * len(shape))

    return pl.pallas_call(
        functools.partial(attend_kernel, count),
        grid=(heads,),
        in_specs=[
            smem,
            smem,
        ]
        + [whole(depth, local)] * shards
        + [whole(width, depth)] * 3
        + [whole(1, width)] * 3
        + [per_head(head_dim, feat)],
        out_specs=[
            whole(3 * width, total),
            per_head(feat, total),
            per_head(feat, total),
            per_head(state_rows, feat),
            pl.BlockSpec((head_dim, total), lambda h: (h, 0)),
            per_head(8, total),
        ]
        + [whole(width, local)] * shards,
        out_shape=[
            jax.ShapeDtypeStruct((3 * width, total), bf16),
            jax.ShapeDtypeStruct((heads, feat, total), bf16),
            jax.ShapeDtypeStruct((heads, feat, total), bf16),
            jax.ShapeDtypeStruct((heads, state_rows, feat), bf16),
            jax.ShapeDtypeStruct((width, total), f32),
            jax.ShapeDtypeStruct((heads, 8, total), f32),
        ]
        + [jax.ShapeDtypeStruct((width, local), bf16)] * shards,
        scratch_shapes=[pltpu.VMEM((width, total), bf16)],
        compiler_params=pltpu.CompilerParams(vmem_limit_bytes=30 << 20),
        cost_estimate=cost(8),
        name="attend",
    )(lengths, place, *tokens, *weights, *biases, proj)


def feature_back_rows(grad_feat, feat, vectors, proj_w):
    scale = HEAD_DIM ** (-0.25)
    grad_proj = grad_feat * feat.astype(f32)
    pulled = scale * dot(proj_w, grad_proj.astype(bf16))
    return pulled - (scale * scale) * vectors.astype(f32) * jnp.sum(grad_proj, axis=0, keepdims=True)


def attend_back_kernel(
    count,
    lengths_ref,
    place_ref,
    qkv_ref,
    qf_ref,
    kf_ref,
    state_ref,
    out_ref,
    den_ref,
    g0_ref,
    g1_ref,
    g2_ref,
    g3_ref,
    proj_ref,
    weight_ref,
    sums_ref,
    grad_ref,
    send_ref,
    keep_ref,
    heads_ref,
    small_ref,
):
    h = pl.program_id(0)
    width, local = g0_ref.shape
    shards = grad_ref.shape[1] // local
    depth = weight_ref.shape[0]
    heads = pl.num_programs(0)
    spread_rows = count * HEAD_DIM

    @pl.when(h == 0)
    def _():
        for s, piece in enumerate((g0_ref, g1_ref, g2_ref, g3_ref)):
            heads_ref[:, lanes(lax.bitwise_xor(place_ref[0], s), local)] = piece[...]

    def at(kind):
        return pl.ds(pl.multiple_of(kind * width + h * HEAD_DIM, HEAD_DIM), HEAD_DIM)

    seg = segments(lengths_ref, count, (1, shards * local))
    hot = one_hot_rows(seg, count)
    query, key, value = qkv_ref[at(0), :], qkv_ref[at(1), :], qkv_ref[at(2), :]
    q_feat, k_feat = qf_ref[0], kf_ref[0]
    grad_head = heads_ref[pl.ds(pl.multiple_of(h * HEAD_DIM, HEAD_DIM), HEAD_DIM), :].astype(f32)
    den = den_ref[0, 0:1, :]
    grad_numer = (grad_head / den).astype(bf16)
    grad_den = -jnp.sum(grad_head * out_ref[...], axis=0, keepdims=True) / den
    marked = hot * grad_den
    high = marked.astype(bf16).astype(f32)
    low = marked - high
    numer_wide = jnp.concatenate(
        masked_copies(seg, grad_numer, count)
        + [
            jnp.concatenate([high, low], axis=0).astype(bf16),
            jnp.concatenate([high, jnp.zeros_like(high)], axis=0).astype(bf16),
        ],
        axis=0,
    )
    grad_state = dot_cols(numer_wide[: spread_rows + 16], q_feat)
    sums = grad_state[spread_rows : spread_rows + 8] + grad_state[spread_rows + 8 : spread_rows + 16]
    sums_high = sums.astype(bf16).astype(f32)
    grad_state = jnp.concatenate(
        [
            grad_state[:spread_rows].astype(bf16),
            jnp.concatenate([sums_high, sums - sums_high], axis=0).astype(bf16),
        ],
        axis=0,
    )
    value_wide = jnp.concatenate(
        masked_copies(seg, value, count) + [jnp.concatenate([hot, hot], axis=0).astype(bf16)], axis=0
    )
    proj_w = proj_ref[0]
    grad_qfeat = dot_rows(state_ref[0], numer_wide)
    grad_ref[at(0), :] = feature_back_rows(grad_qfeat, q_feat, query, proj_w).astype(bf16)
    grad_kfeat = dot_rows(grad_state, value_wide)
    grad_ref[at(1), :] = feature_back_rows(grad_kfeat, k_feat, key, proj_w).astype(bf16)
    grad_ref[at(2), :] = masked_sum(seg, dot(grad_state[:spread_rows], k_feat), count).astype(bf16)

    @pl.when(h == heads - 1)
    def _():
        small_ref[...] = sums_ref[...]
        totals = dot_cols(jnp.ones((8, shards * local), bf16), grad_ref[...])
        for t in range(shards):

            @pl.when(place_ref[0] == t)
            def _():
                for kind, row in enumerate(BIAS_ROWS):
                    small_ref[row : row + 1, t * width : (t + 1) * width] = totals[
                        0:1, kind * width : (kind + 1) * width
                    ]

        small = jnp.concatenate(
            [small_ref[:, begin : begin + local] for begin in range(0, depth, local)], axis=0
        )
        rows = small.shape[0]
        high = small.astype(bf16)
        low = (small - high.astype(f32)).astype(bf16)
        for s in range(shards):
            out = (keep_ref, send_ref)[s % 2].at[s // 2]
            out[:depth] = dot(
                weight_ref[...], grad_ref[:, lanes(lax.bitwise_xor(place_ref[0], s), local)]
            ).astype(bf16)
            out[depth : depth + rows] = high
            out[depth + rows :] = low


def attend_back(saved, pieces, proj, weight, sums, lengths, place):
    qkv, qf, kf, state, out, den = saved
    heads, feat, total = qf.shape
    width, local = pieces[0].shape
    shards = total // local
    depth = weight.shape[0]
    count = lengths.shape[1] - 1
    state_rows = state.shape[1]
    extra = 2 * sums.shape[0] * (depth // local)
    smem = pl.BlockSpec(memory_space=pltpu.SMEM)

    def whole(*shape):
        return pl.BlockSpec(shape, lambda h: (0,) * len(shape))

    def per_head(*shape):
        return pl.BlockSpec((1,) + shape, lambda h: (h,) + (0,) * len(shape))

    return pl.pallas_call(
        functools.partial(attend_back_kernel, count),
        grid=(heads,),
        in_specs=[
            smem,
            smem,
            whole(3 * width, total),
            per_head(feat, total),
            per_head(feat, total),
            per_head(state_rows, feat),
            pl.BlockSpec((HEAD_DIM, total), lambda h: (h, 0)),
            per_head(8, total),
        ]
        + [whole(width, local)] * shards
        + [per_head(HEAD_DIM, feat), whole(depth, 3 * width), whole(*sums.shape)],
        out_specs=[
            whole(3 * width, total),
            whole(shards // 2, depth + extra, local),
            whole(shards // 2, depth + extra, local),
        ],
        out_shape=[
            jax.ShapeDtypeStruct((3 * width, total), bf16),
            jax.ShapeDtypeStruct((shards // 2, depth + extra, local), bf16),
            jax.ShapeDtypeStruct((shards // 2, depth + extra, local), bf16),
        ],
        scratch_shapes=[pltpu.VMEM((width, total), bf16), pltpu.VMEM(sums.shape, f32)],
        compiler_params=pltpu.CompilerParams(vmem_limit_bytes=28 << 20),
        cost_estimate=cost(9),
        name="attend_back",
    )(lengths, place, qkv, qf, kf, state, out, den, *pieces, proj, weight, sums)


def slot_place(slot, half):
    k = slot // 2
    if half == 0:
        return 1 - k % 2, k // 2
    return 1 - k // 2, k % 2


def pick_blocks(own, turned_ref):
    slots = turned_ref.shape[0]
    return jnp.concatenate([turned_ref[lax.bitwise_xor(own, slot)] for slot in range(0, slots, 2)], axis=0)


def emit_slots(entries, outs, begin=0):
    height = outs[0].shape[2]
    count = entries.shape[1]
    for half in range(2):

        @pl.when(pl.program_id(0) // 2 == half)
        def _():
            for k in range(PLANE // 2):
                part, index = slot_place(2 * k, half)
                outs[2 * half + part][index, 0, :, begin : begin + count] = entries[k * height : (k + 1) * height]


def slot_outputs(shards, height, count):
    low = pl.BlockSpec((2, 1, height, count), lambda s: (0, jnp.minimum(s, 1), 0, 0))
    high = pl.BlockSpec((2, 1, height, count), lambda s: (0, jnp.maximum(s - 2, 0), 0, 0))
    shape = jax.ShapeDtypeStruct((2, shards // 2, height, count), bf16)
    return [low, low, high, high], [shape] * 4


def output_grad_kernel(own_ref, turned_ref, turned_far_ref, act_ref, act_far_ref, *outs):
    own = own_ref[0]
    grads = dot(pick_blocks(own, turned_ref), act_ref[0]) + dot(pick_blocks(own, turned_far_ref), act_far_ref[0])
    emit_slots(grads.astype(bf16), outs)


def output_grad(own, turned, turned_far, acts, acts_far):
    shards, rows, hidden = acts.shape
    slots, height, _ = turned.shape
    specs, shapes = slot_outputs(shards, height, hidden)
    whole = pl.BlockSpec((slots, height, rows), lambda s: (0, 0, 0))
    by_shard = pl.BlockSpec((1, rows, hidden), lambda s: (s, 0, 0))
    return pl.pallas_call(
        output_grad_kernel,
        grid=(shards,),
        in_specs=[pl.BlockSpec(memory_space=pltpu.SMEM), whole, whole, by_shard, by_shard],
        out_specs=specs,
        out_shape=shapes,
        compiler_params=pltpu.CompilerParams(vmem_limit_bytes=16 << 20),
        cost_estimate=cost(4),
        name="output_grad",
    )(own, turned, turned_far, acts, acts_far)


def hidden_grad_kernel(
    own_ref,
    first_ref,
    first_far_ref,
    grad_pre_ref,
    grad_pre_far_ref,
    branch_ref,
    branch_far_ref,
    mixed_ref,
    mixed_far_ref,
    *outs,
):
    own = own_ref[0]
    hidden = grad_pre_ref.shape[2]
    grads = dot(pick_blocks(own, first_ref), grad_pre_ref[0]) + dot(
        pick_blocks(own, first_far_ref), grad_pre_far_ref[0]
    )
    emit_slots(grads.astype(bf16), outs)
    grads = dot_cols(pick_blocks(own, branch_ref), mixed_ref[0]) + dot_cols(
        pick_blocks(own, branch_far_ref), mixed_far_ref[0]
    )
    emit_slots(grads.astype(bf16), outs, hidden)


def hidden_grad(own, first, first_far, grad_pre, grad_pre_far, branch, branch_far, mixed, mixed_far):
    shards, rows, hidden = grad_pre.shape
    slots, height, _ = first.shape
    width = mixed.shape[1]
    specs, shapes = slot_outputs(shards, height, hidden + width)
    whole = pl.BlockSpec((slots, height, rows), lambda s: (0, 0, 0))
    by_shard = pl.BlockSpec((1, rows, hidden), lambda s: (s, 0, 0))
    piece = pl.BlockSpec((1, width, rows), lambda s: (s, 0, 0))
    return pl.pallas_call(
        hidden_grad_kernel,
        grid=(shards,),
        in_specs=[
            pl.BlockSpec(memory_space=pltpu.SMEM),
            whole,
            whole,
            by_shard,
            by_shard,
            whole,
            whole,
            piece,
            piece,
        ],
        out_specs=specs,
        out_shape=shapes,
        compiler_params=pltpu.CompilerParams(vmem_limit_bytes=16 << 20),
        cost_estimate=cost(5),
        name="hidden_grad",
    )(own, first, first_far, grad_pre, grad_pre_far, branch, branch_far, mixed, mixed_far)


def qkv_grad_kernel(own_ref, place_ref, x0_ref, x1_ref, x2_ref, x3_ref, grad_ref, even_ref, odd_ref, hold_ref):
    local = x0_ref.shape[1]
    depth = hold_ref.shape[0] * hold_ref.shape[1]
    grads = sum(
        dot_cols(block[:depth], grad_ref[:, lanes(lax.bitwise_xor(place_ref[0], s), local)])
        for s, block in enumerate((x0_ref, x1_ref, x2_ref, x3_ref))
    )
    hold_ref[...] = grads.astype(bf16).reshape(hold_ref.shape)
    rows = even_ref.shape[4]
    for slot in range(hold_ref.shape[0]):
        target = odd_ref if slot % 2 else even_ref
        block = hold_ref[lax.bitwise_xor(own_ref[0], slot)]
        for half in range(2):
            target[(half,) + slot_place(slot, half) + (0,)] = block[half * rows : (half + 1) * rows]


def qkv_grad(own, place, slots, depth, tokens, grads):
    count = grads.shape[0]
    vmem = pl.BlockSpec(memory_space=pltpu.VMEM)
    shape = jax.ShapeDtypeStruct((2, 2, slots // 4, 1, depth // slots // 2, count), bf16)
    return pl.pallas_call(
        qkv_grad_kernel,
        in_specs=[pl.BlockSpec(memory_space=pltpu.SMEM)] * 2 + [vmem] * (len(tokens) + 1),
        out_specs=[vmem, vmem],
        out_shape=[shape, shape],
        scratch_shapes=[pltpu.VMEM((slots, depth // slots, count), bf16)],
        compiler_params=pltpu.CompilerParams(vmem_limit_bytes=16 << 20),
        cost_estimate=cost(2),
        name="qkv_grad",
    )(own, place, *tokens, grads)


def norm_rows(resid):
    center = resid - jnp.mean(resid, axis=-1, keepdims=True)
    inverse = lax.rsqrt(jnp.mean(center * center, axis=-1, keepdims=True) + eps)
    return center * inverse, inverse


HELD = [(0, (0, 1, 2, 3)), (2, (0, 1, 2, 3)), (4, (0, 1, 2, 3)), (6, (0, 1)), (6, (2, 3))]
HELD = HELD + [(mask ^ 1, shards) for mask, shards in HELD]


def place_copies(own, held, begin, rows, target, sems):
    columns = held[0].shape[2]
    copies = []
    for index, (piece, (mask, shards)) in enumerate(zip(held, HELD)):
        source = lax.bitwise_xor(own, mask)
        chip = lax.shift_right_logical(source, 1)
        core = lax.bitwise_and(source, 1)
        copies.append(
            pltpu.make_async_copy(
                piece.at[:, pl.ds(begin, rows), :],
                target.at[shards[0] : shards[-1] + 1, chip, :, lanes(core, columns)],
                sems.at[index],
            )
        )
    return copies


def start_all(copies):
    for entries in copies:
        for copy in entries:
            copy.start()


def wait_all(entries):
    for copy in entries:
        copy.wait()


def ffn_up_kernel(
    own_ref,
    tokens_ref,
    p0_ref,
    p1_ref,
    p2_ref,
    p3_ref,
    mixer_bias_ref,
    gain_ref,
    shift_ref,
    *refs,
):
    held, refs = refs[: len(HELD)], refs[len(HELD) :]
    parts, refs = refs[:4], refs[4:]
    (
        normed_ref,
        inverse_ref,
        turned_ref,
        mixed_ref,
        act_ref,
        slope_ref,
        mixer_ref,
        hidden_ref,
        bias_ref,
        mixer_sem,
        hidden_sem,
        bias_sem,
    ) = refs
    own = own_ref[0]
    shards, chips, mixer_rows, depth = mixer_ref.shape
    hidden_rows = hidden_ref.shape[2]
    mixer_copies = place_copies(own, held, hidden_rows, mixer_rows, mixer_ref, mixer_sem)
    hidden_copies = place_copies(own, held, 0, hidden_rows, hidden_ref, hidden_sem)
    bias_rows = parts[0].shape[0] - 16
    bias_copies = [
        pltpu.make_async_copy(part.at[bias_rows : bias_rows + 16], bias_ref.at[s], bias_sem.at[s])
        for s, part in enumerate(parts)
    ]
    start_all([mixer_copies, bias_copies, hidden_copies])
    resid = tokens_ref[...].astype(f32) + mixer_bias_ref[...]
    for s, piece in enumerate((p0_ref, p1_ref, p2_ref, p3_ref)):
        mixed_ref[s] = piece[...]
        if s == 0:
            wait_all(mixer_copies)
        resid = resid + dot_rows(piece[...], mixer_ref[s].reshape(chips * mixer_rows, depth))
    normed, inverse = norm_rows(resid)
    normed_ref[...] = normed
    inverse_ref[...] = jnp.broadcast_to(inverse, inverse_ref.shape)
    first_low = (normed * gain_ref[...] + shift_ref[...]).astype(bf16)
    turned_ref[...] = first_low.T
    for s in range(shards):
        if s == 0:
            wait_all(hidden_copies + bias_copies)
        bias = unpack_bias(bias_ref[s])
        pre = dot(first_low, hidden_ref[s].reshape(chips * hidden_rows, hidden_ref.shape[3])) + bias
        phi = 0.5 * (1.0 + lax.erf(pre * math.sqrt(0.5)))
        act_ref[s] = (pre * phi).astype(bf16)
        slope_ref[s] = (
            phi + pre * jnp.exp(-0.5 * pre * pre) * (1.0 / math.sqrt(2.0 * math.pi))
        ).astype(bf16)


def ffn_up(own, tokens, pieces, mixer_bias, gain, shift_by, parts, held, mixer_rows):
    rows, depth = tokens.shape
    shards = len(pieces)
    chips = PLANE // 2
    hidden = 2 * held[0].shape[2]
    hidden_rows = held[0].shape[1] - mixer_rows
    vmem = pl.BlockSpec(memory_space=pltpu.VMEM)
    return pl.pallas_call(
        ffn_up_kernel,
        in_specs=[pl.BlockSpec(memory_space=pltpu.SMEM)]
        + [vmem] * (1 + shards + 3)
        + [pl.BlockSpec(memory_space=pl.ANY)] * (len(HELD) + shards),
        out_specs=[vmem] * 6,
        out_shape=[
            jax.ShapeDtypeStruct((rows, depth), f32),
            jax.ShapeDtypeStruct((rows, 128), f32),
            jax.ShapeDtypeStruct((depth, rows), bf16),
            jax.ShapeDtypeStruct((shards,) + pieces[0].shape, bf16),
            jax.ShapeDtypeStruct((shards, rows, hidden), bf16),
            jax.ShapeDtypeStruct((shards, rows, hidden), bf16),
        ],
        scratch_shapes=[
            pltpu.VMEM((shards, chips, mixer_rows, depth), bf16),
            pltpu.VMEM((shards, chips, hidden_rows, hidden), bf16),
            pltpu.VMEM((shards, 16, held[0].shape[2]), bf16),
            pltpu.SemaphoreType.DMA((len(HELD),)),
            pltpu.SemaphoreType.DMA((len(HELD),)),
            pltpu.SemaphoreType.DMA((shards,)),
        ],
        compiler_params=pltpu.CompilerParams(vmem_limit_bytes=28 << 20),
        cost_estimate=cost(8),
        name="ffn_up",
    )(own, tokens, *pieces, mixer_bias, gain, shift_by, *held, *parts)


def norm_rows_back(scaled, normed, inverse):
    return inverse * (
        scaled
        - jnp.mean(scaled, axis=-1, keepdims=True)
        - normed * jnp.mean(scaled * normed, axis=-1, keepdims=True)
    )


def column_sum(entries):
    return jnp.sum(entries, axis=0, keepdims=True)


def ffn_down_kernel(
    own_ref,
    normed_ref,
    inverse_ref,
    act_ref,
    slope_ref,
    cotangent_ref,
    first_gain_ref,
    first_shift_ref,
    output_bias_ref,
    gain_ref,
    shift_ref,
    *refs,
):
    held, refs = refs[: len(HELD)], refs[len(HELD) :]
    held_out, refs = refs[: len(HELD)], refs[len(HELD) :]
    (
        layer_ref,
        resid_ref,
        b0_ref,
        b1_ref,
        b2_ref,
        b3_ref,
        grad_ffn_ref,
        grad_pre_ref,
        grad_branch_ref,
        sums_ref,
        mixer_ref,
        hidden_ref,
        output_ref,
        mixer_sem,
        hidden_sem,
        output_sem,
    ) = refs
    own, place = own_ref[0], own_ref[1]
    shards, chips, mixer_rows, depth = mixer_ref.shape
    hidden_rows = hidden_ref.shape[2]
    hidden = hidden_ref.shape[3]
    output_copies = place_copies(own, held_out, 0, output_ref.shape[2], output_ref, output_sem)
    hidden_copies = place_copies(own, held, 0, hidden_rows, hidden_ref, hidden_sem)
    mixer_copies = place_copies(own, held, hidden_rows, mixer_rows, mixer_ref, mixer_sem)
    start_all([output_copies, hidden_copies, mixer_copies])
    normed_one = normed_ref[...]
    resid = normed_one * first_gain_ref[...] + first_shift_ref[...] + output_bias_ref[...]
    wait_all(output_copies)
    for s in range(shards):
        resid = resid + dot(act_ref[s], output_ref[s].reshape(hidden, depth))
    normed, inverse = norm_rows(resid)
    layer_ref[...] = (normed * gain_ref[...] + shift_ref[...]).astype(bf16)
    grad_out = cotangent_ref[...].astype(f32)
    sums_ref[0:1] = column_sum(grad_out * normed)
    sums_ref[1:2] = column_sum(grad_out)
    grad_two = norm_rows_back(grad_out * gain_ref[...], normed, inverse)
    grad_ffn = grad_two.astype(bf16)
    grad_ffn_ref[...] = grad_ffn.T
    sums_ref[2:3] = column_sum(grad_ffn.astype(f32))
    grad_first = grad_two
    for s in range(shards):
        grad_pre = (
            dot_cols(grad_ffn, output_ref[s].reshape(hidden, depth)) * slope_ref[s].astype(f32)
        ).astype(bf16)
        grad_pre_ref[s] = grad_pre
        sums_ref[pl.ds(8 + lax.bitwise_xor(place, s), 1)] = column_sum(grad_pre.astype(f32))
        if s == 0:
            wait_all(hidden_copies)
        grad_first = grad_first + dot_cols(grad_pre, hidden_ref[s].reshape(depth, hidden))
    sums_ref[3:4] = column_sum(grad_first * normed_one)
    sums_ref[4:5] = column_sum(grad_first)
    grad_one = norm_rows_back(grad_first * first_gain_ref[...], normed_one, inverse_ref[:, 0:1])
    resid_ref[...] = grad_one
    grad_branch = grad_one.astype(bf16)
    branch_turned = grad_branch.T
    grad_branch_ref[...] = branch_turned
    sums_ref[5:6] = column_sum(grad_branch.astype(f32))
    sums_ref[6:8] = jnp.zeros((2, depth), f32)
    sums_ref[8 + shards :] = jnp.zeros((8 - shards, depth), f32)
    for s, back in enumerate((b0_ref, b1_ref, b2_ref, b3_ref)):
        if s == 0:
            wait_all(mixer_copies)
        back[...] = dot(mixer_ref[s].reshape(chips * mixer_rows, depth), branch_turned).astype(bf16)


def ffn_down(own, normed, inverse, acts, slopes, cotangent, vectors, held, held_out, mixer_rows):
    rows, depth = normed.shape
    shards, _, hidden = acts.shape
    chips = PLANE // 2
    hidden_rows = held[0].shape[1] - mixer_rows
    output_rows = held_out[0].shape[1]
    vmem = pl.BlockSpec(memory_space=pltpu.VMEM)
    width = chips * mixer_rows
    return pl.pallas_call(
        ffn_down_kernel,
        in_specs=[pl.BlockSpec(memory_space=pltpu.SMEM)]
        + [vmem] * 10
        + [pl.BlockSpec(memory_space=pl.ANY)] * (2 * len(HELD)),
        out_specs=[vmem] * (6 + shards),
        out_shape=[
            jax.ShapeDtypeStruct((rows, depth), bf16),
            jax.ShapeDtypeStruct((rows, depth), f32),
        ]
        + [jax.ShapeDtypeStruct((width, rows), bf16)] * shards
        + [
            jax.ShapeDtypeStruct((depth, rows), bf16),
            jax.ShapeDtypeStruct((shards, rows, hidden), bf16),
            jax.ShapeDtypeStruct((depth, rows), bf16),
            jax.ShapeDtypeStruct((16, depth), f32),
        ],
        scratch_shapes=[
            pltpu.VMEM((shards, chips, mixer_rows, depth), bf16),
            pltpu.VMEM((shards, chips, hidden_rows, hidden), bf16),
            pltpu.VMEM((shards, chips, output_rows, depth), bf16),
            pltpu.SemaphoreType.DMA((len(HELD),)),
            pltpu.SemaphoreType.DMA((len(HELD),)),
            pltpu.SemaphoreType.DMA((len(HELD),)),
        ],
        compiler_params=pltpu.CompilerParams(vmem_limit_bytes=36 << 20),
        cost_estimate=cost(15),
        name="ffn_down",
    )(own, normed, inverse, acts, slopes, cotangent, *vectors, *held, *held_out)


def fold_kernel(depth, keep_ref, far_ref, mine_ref, other_ref):
    rows = (keep_ref.shape[1] - depth) // 2
    for s, out in enumerate((mine_ref, other_ref)):
        out[:depth] = (keep_ref[s, :depth].astype(f32) + far_ref[s, :depth].astype(f32)).astype(bf16)
        small = sum(
            ref[s, depth : depth + rows].astype(f32) + ref[s, depth + rows :].astype(f32) for ref in (keep_ref, far_ref)
        )
        high = small.astype(bf16)
        out[depth : depth + rows] = high
        out[depth + rows :] = (small - high.astype(f32)).astype(bf16)


def fold(depth, keep, far):
    vmem = pl.BlockSpec(memory_space=pltpu.VMEM)
    return pl.pallas_call(
        functools.partial(fold_kernel, depth),
        in_specs=[vmem] * 2,
        out_specs=[vmem] * 2,
        out_shape=[jax.ShapeDtypeStruct(keep.shape[1:], bf16)] * 2,
        compiler_params=pltpu.CompilerParams(vmem_limit_bytes=8 << 20),
        cost_estimate=cost(2),
        name="fold",
    )(keep, far)


def join_cores_kernel(near_ref, far_ref, *outs):
    for half in range(2):
        for part in range(2):
            outs[2 * half + part][...] = (
                near_ref[half, part].astype(f32) + far_ref[half, part].astype(f32)
            ).astype(bf16)


def join_cores(near, far):
    vmem = pl.BlockSpec(memory_space=pltpu.VMEM)
    return pl.pallas_call(
        join_cores_kernel,
        in_specs=[vmem] * 2,
        out_specs=[vmem] * 4,
        out_shape=[jax.ShapeDtypeStruct(near.shape[2:], bf16)] * 4,
        compiler_params=pltpu.CompilerParams(vmem_limit_bytes=8 << 20),
        cost_estimate=cost(2),
        name="join_cores",
    )(near, far)


def finish_tokens_kernel(resid_ref, mine_ref, far_ref, out_ref, small_ref):
    depth = resid_ref.shape[1]
    rows = small_ref.shape[0]
    total = mine_ref[:depth].astype(f32) + far_ref[:depth].astype(f32)
    out_ref[...] = resid_ref[...] + total.T
    small_ref[...] = sum(
        ref[depth : depth + rows].astype(f32) + ref[depth + rows :].astype(f32) for ref in (mine_ref, far_ref)
    )


def finish_tokens(resid, mine, far):
    local, depth = resid.shape
    rows = (mine.shape[0] - depth) // 2
    vmem = pl.BlockSpec(memory_space=pltpu.VMEM)
    return pl.pallas_call(
        finish_tokens_kernel,
        in_specs=[vmem] * 3,
        out_specs=[vmem] * 2,
        out_shape=[jax.ShapeDtypeStruct(resid.shape, f32), jax.ShapeDtypeStruct((rows, local), f32)],
        compiler_params=pltpu.CompilerParams(vmem_limit_bytes=8 << 20),
        cost_estimate=cost(1),
        name="finish_tokens",
    )(resid, mine, far)


def finish_hidden_kernel(a_ref, b_ref, hidden_ref, mixer_ref):
    total = a_ref[...].astype(f32) + b_ref[...].astype(f32)
    hidden = hidden_ref.shape[1]
    hidden_ref[...] = total[:, :hidden]
    mixer_ref[...] = total[:, hidden:].T


def finish_hidden(entries, hidden):
    rows, columns = entries[0].shape
    vmem = pl.BlockSpec(memory_space=pltpu.VMEM)
    return pl.pallas_call(
        finish_hidden_kernel,
        in_specs=[vmem] * 2,
        out_specs=[vmem] * 2,
        out_shape=[
            jax.ShapeDtypeStruct((rows, hidden), f32),
            jax.ShapeDtypeStruct((columns - hidden, rows), f32),
        ],
        compiler_params=pltpu.CompilerParams(vmem_limit_bytes=8 << 20),
        cost_estimate=cost(1),
        name="finish_hidden",
    )(*entries)


def finish_qkv_kernel(a_ref, b_ref, c_ref, d_ref, query_ref, key_ref, value_ref):
    rows, width = a_ref.shape[0], query_ref.shape[1]
    low = a_ref[...].astype(f32) + b_ref[...].astype(f32)
    high = c_ref[...].astype(f32) + d_ref[...].astype(f32)
    for kind, out in enumerate((query_ref, key_ref, value_ref)):
        out[:rows] = low[:, kind * width : (kind + 1) * width]
        out[rows:] = high[:, kind * width : (kind + 1) * width]


def finish_qkv(entries):
    rows, columns = entries[0].shape
    vmem = pl.BlockSpec(memory_space=pltpu.VMEM)
    return pl.pallas_call(
        finish_qkv_kernel,
        in_specs=[vmem] * 4,
        out_specs=[vmem] * 3,
        out_shape=[jax.ShapeDtypeStruct((2 * rows, columns // 3), f32)] * 3,
        compiler_params=pltpu.CompilerParams(vmem_limit_bytes=8 << 20),
        cost_estimate=cost(1),
        name="finish_qkv",
    )(*entries)


BIAS_ROWS = (6, 7, 12)


def swap(values, mask):
    size = lax.axis_size("dp")
    return lax.ppermute(values, "dp", [(i, i ^ mask) for i in range(size)])


def cross(values, mask):
    size = lax.axis_size("tensor")
    return lax.ppermute(values, "tensor", [(i, i ^ mask) for i in range(size)])


def after(values, *others):
    return lax.optimization_barrier((values, others))[0]


def from_neighbours(payload):
    return cross(payload, 1), cross(payload, 2)


def all_shards(payload, near, far):
    return [payload, near, far, cross(far, 1)]


def spread_plane(stack, between=()):
    over_x, over_y = after((swap(stack, 2), swap(stack, 4)), *between)
    return [stack, over_x, over_y, swap(over_x[:2], 4), swap(over_y[2:], 2)]


def other_core(held, before=()):
    return [swap(entry, 1) for entry in after(held, *before)]


def add_low(*entries):
    return sum(entry.astype(f32) for entry in entries).astype(bf16)


def sum_first(near, before=(), between=()):
    send_low, keep_low, send_high, keep_high = near
    send_low, send_high = after((send_low, send_high), *before)
    low, high = after((swap(send_low, 2), swap(send_high, 4)), *between)
    return (
        [add_low(keep_low[0], low[0]), add_low(keep_high[0], high[0])],
        [add_low(keep_low[1], low[1]), add_low(keep_high[1], high[1])],
    )


def sum_second(stay, send, between=()):
    low, high = after((swap(send[0], 4), swap(send[1], 2)), *between)
    return [add_low(stay[0], low), add_low(stay[1], high)]


def scatter_all(halves, axis):
    parts = []
    for half in range(2):
        blocks = []
        for i in range(PLANE):
            part, index = slot_place(i, half)
            blocks.append(halves[i % 2][2 * half + part][index])
        parts.append(jnp.stack(blocks, axis=1))
    whole = jnp.concatenate(parts, axis=axis)
    whole = whole.reshape(whole.shape[:1] + (-1,) + whole.shape[-1:])
    return lax.psum_scatter(whole, "dp", scatter_dimension=1, tiled=True)


def pair_shards(grads):
    return after(jnp.stack([grads[1], grads[3]]))


def join_shards(grads, pair, between=()):
    near = after(cross(pair, 1), *between)
    mine, other = add_low(grads[0], near[0]), add_low(grads[2], near[1])
    return mine, cross(other, 2)


def by_shard(halves):
    return [half[s] for half in halves for s in range(half.shape[0])]


def small_sum(values):
    size = lax.axis_size("dp")
    if size != PLANE:
        values = lax.psum(values, "dp")
    else:
        for mask in (1, 2, 4):
            values = values + swap(values, mask)
    return values


def body(
    tokens,
    lengths,
    query_weight,
    query_bias,
    key_weight,
    key_bias,
    value_weight,
    value_bias,
    feature_proj,
    mixer_weight,
    mixer_bias,
    first_gain,
    first_shift,
    hidden_weight,
    hidden_bias,
    output_weight,
    output_bias,
    second_gain,
    second_shift,
    cotangent,
):
    depth = tokens.shape[1]
    shards = lax.axis_size("tensor")
    place = lax.axis_index("tensor").astype(jnp.int32)
    plane = (lax.axis_index("dp") % PLANE).astype(jnp.int32)
    width = query_weight.shape[1]
    hidden = hidden_weight.shape[1]
    mixer_rows = mixer_weight.shape[0] // (PLANE // 2)
    own = jnp.stack([plane, place])
    slot_of = plane[None] if lax.axis_size("dp") == PLANE else jnp.zeros((1,), jnp.int32)

    def row(vector):
        return vector.reshape(1, -1)

    def blocks(turned):
        return turned.reshape(PLANE, turned.shape[0] // PLANE, turned.shape[1])

    payload, payload_out, turned = pack(
        own, tokens, hidden_bias.reshape(-1, 128), hidden_weight, mixer_weight, output_weight
    )
    near, far = from_neighbours(payload)
    parts = all_shards(payload, near, far)
    near_out, far_out = from_neighbours(after(payload_out, far))
    parts_out = all_shards(payload_out, near_out, far_out)
    near, far = from_neighbours(after(turned, parts[3]))
    weights = [query_weight.T, key_weight.T, value_weight.T]
    qkv_weight = prepare(after(weights, payload))
    rows = payload.shape[0] - 16
    stack = jnp.stack([part[:rows] for part in parts])
    stack_far = swap(stack, 1)
    stack_out = jnp.stack(parts_out)
    around = spread_plane(stack, between=(near, far, qkv_weight, stack_far, stack_out))
    tokens_all = all_shards(turned, near, far)
    crossed = [stack_far] + other_core(around[1:3])
    tokens_all = after(tokens_all, *crossed, *around[3:])
    *saved, p0, p1, p2, p3 = attend(
        tokens_all,
        weights,
        [row(query_bias), row(key_bias), row(value_bias)],
        feature_proj,
        lengths,
        place[None],
    )
    around_out = spread_plane(stack_out, between=(p0,))
    pieces = [p0] + [cross(p, s) for s, p in ((1, p1), (2, p2), (3, p3))]
    held = around + crossed + other_core(around[3:])
    held_out = around_out + other_core(around_out[:3], pieces) + other_core(around_out[3:])
    normed, inverse, turned, mixed, acts, slopes = ffn_up(
        own, tokens, pieces, row(mixer_bias), row(first_gain), row(first_shift), parts, held, mixer_rows
    )
    acts_far, turned_far, mixed_far = swap(acts, 1), swap(turned, 1), swap(mixed, 1)
    held_out = after(held_out, turned_far, mixed_far)
    vectors = [row(v) for v in (first_gain, first_shift, output_bias, second_gain, second_shift)]
    layer_out, grad_resid, b0, b1, b2, b3, grad_ffn, grad_pre, grad_branch, sums = ffn_down(
        own, normed, inverse, acts, slopes, cotangent, vectors, held, held_out, mixer_rows
    )
    back = [b0] + [cross(b, s) for s, b in ((1, b1), (2, b2), (3, b3))]
    output_work = (blocks(grad_ffn), blocks(swap(grad_ffn, 1)), acts, acts_far)
    hidden_work = (
        blocks(turned),
        blocks(turned_far),
        grad_pre,
        swap(grad_pre, 1),
        blocks(grad_branch),
        blocks(swap(grad_branch, 1)),
        mixed,
        mixed_far,
    )
    fast = lax.axis_size("dp") == PLANE
    if fast:
        near_output = output_grad(slot_of, *output_work)
        near_output = after(near_output, hidden_work)
        near_hidden = hidden_grad(slot_of, *hidden_work)
        back = after(back, near_output, near_hidden)
    grad_qkv, send, keep = attend_back(
        saved, back, feature_proj, qkv_weight, sums, lengths, place[None]
    )
    far = cross(send, 1)
    if fast:
        even, odd = qkv_grad(slot_of, place[None], PLANE, depth, tokens_all, grad_qkv)
        stay_output, send_output = sum_first(near_output, between=(even,))
        stay_hidden, send_hidden = sum_first(near_hidden, between=send_output)
        near_qkv = join_cores(even, after(swap(odd, 1), send_hidden))
        mine, other = fold(depth, keep, after(far, near_qkv))
        far = cross(other, 2)
        grad_output = by_shard(sum_second(stay_output, send_output, between=(other,)))
        pair_output = pair_shards(grad_output)
        grad_hidden = by_shard(sum_second(stay_hidden, send_hidden, between=(pair_output,)))
        pair_hidden = pair_shards(grad_hidden)
        stay_qkv, send_qkv = sum_first(near_qkv, between=(pair_hidden,))
        grad_output = join_shards(grad_output, pair_output, send_qkv)
        low, high = swap(send_qkv[0], 4), swap(send_qkv[1], 2)
        grad_weights = finish_qkv([entry[0] for entry in (stay_qkv[0], low, stay_qkv[1], high)])
        grad_hidden = join_shards(grad_hidden, pair_hidden, grad_weights)
    else:
        zero, one = jnp.zeros((1,), jnp.int32), jnp.ones((1,), jnp.int32)
        mine, other = fold(depth, keep, far)
        far = cross(other, 2)
        grad_output = scatter_all([output_grad(slot, *output_work) for slot in (zero, one)], 0)
        grad_output = by_shard([0.5 * grad_output])
        grad_output = join_shards(grad_output, pair_shards(grad_output))
        grad_hidden = scatter_all([hidden_grad(slot, *hidden_work) for slot in (zero, one)], 0)
        grad_hidden = by_shard([0.5 * grad_hidden])
        grad_hidden = join_shards(grad_hidden, pair_shards(grad_hidden))
        grad_weight = scatter_all(
            [
                [entry[half, part] for half in range(2) for part in range(2)]
                for entry in qkv_grad(zero, place[None], PLANE, depth, tokens_all, grad_qkv)
            ],
            2,
        )[0].astype(f32)
        grad_weights = [grad_weight[:, kind * width : (kind + 1) * width] for kind in range(3)]
    tokens_grad, small = finish_tokens(grad_resid, mine, far)
    small = small_sum(small)
    small = after(small.reshape(-1, 16, small.shape[1]).transpose(1, 0, 2).reshape(16, -1))
    grad_output = sum(entry.astype(f32) for entry in grad_output).T
    grad_hidden, grad_mixer = finish_hidden(grad_hidden, hidden)
    return (
        layer_out,
        tokens_grad,
        grad_weights[0],
        small[6],
        grad_weights[1],
        small[7],
        grad_weights[2],
        small[12],
        grad_mixer,
        small[5],
        small[3],
        small[4],
        grad_hidden,
        small[8 : 8 + shards].reshape(-1),
        grad_output,
        small[2],
        small[0],
        small[1],
    )


def solution(mesh):
    placed = (
        P(("dp", "tensor"), None),
        P("dp", None),
        P(None, "tensor"),
        P("tensor"),
        P(None, "tensor"),
        P("tensor"),
        P(None, "tensor"),
        P("tensor"),
        P("tensor", None, None),
        P("tensor", None),
        P(),
        P(),
        P(),
        P(None, "tensor"),
        P("tensor"),
        P("tensor", None),
        P(),
        P(),
        P(),
        P(("dp", "tensor"), None),
    )
    return jax.shard_map(
        body,
        mesh=mesh,
        in_specs=placed,
        out_specs=(
            P(("dp", "tensor"), None),
            P(("dp", "tensor"), None),
            P("dp", "tensor"),
            P(),
            P("dp", "tensor"),
            P(),
            P("dp", "tensor"),
            P(),
            P("tensor", "dp"),
            P(),
            P(),
            P(),
            P("dp", "tensor"),
            P(),
            P("tensor", "dp"),
            P(),
            P(),
            P(),
        ),
        check_vma=False,
    )
```

```python
import functools
import math

import jax
import jax.numpy as jnp
from jax import lax
from jax.experimental import pallas as pl
from jax.experimental.pallas import tpu as pltpu
from jax.sharding import PartitionSpec as P

HEAD_DIM = 64
FEAT = 256
PLANE = 8
COST_RATE = 9e9

eps = 1e-06
bf16 = jnp.bfloat16
f32 = jnp.float32


def dot(left, right):
    return jnp.dot(left, right, preferred_element_type=f32)


def dot_rows(left, right):
    return lax.dot_general(left, right, (((0,), (0,)), ((), ())), preferred_element_type=f32)


def dot_cols(left, right):
    return lax.dot_general(left, right, (((1,), (1,)), ((), ())), preferred_element_type=f32)


def cost(micros):
    return pl.CostEstimate(flops=int(micros * COST_RATE), transcendentals=0, bytes_accessed=0)


def pack_kernel(
    own_ref, bias_ref, tokens_ref, hidden_ref, mixer_ref, output_ref, first_ref, second_ref, turned_ref, held_ref, sems
):
    rows, columns = second_ref.shape
    chip = lax.shift_right_logical(own_ref[0], 1)
    core = lax.bitwise_and(own_ref[0], 1)
    mixer_rows = mixer_ref.shape[0] // (PLANE // 2)

    def copy(source, height, target, sem):
        begin = pl.multiple_of(chip * height, 16)
        return pltpu.make_async_copy(
            source.at[pl.ds(begin, height), lanes(core, columns)], target, sem
        )

    copies = [
        copy(hidden_ref, rows, first_ref.at[0:rows], sems.at[0]),
        copy(mixer_ref, mixer_rows, first_ref.at[rows : rows + mixer_rows], sems.at[1]),
        copy(output_ref, rows, second_ref, sems.at[2]),
    ]
    fetch = pltpu.make_async_copy(tokens_ref, held_ref, sems.at[3])
    start_all([copies])
    fetch.start()
    wide = jnp.concatenate([bias_ref[...], jnp.zeros((16 - bias_ref.shape[0], 128), f32)], axis=0)
    for index in range(3):
        part = wide.astype(bf16)
        wide = wide - part.astype(f32)
        first_ref[rows + mixer_rows :, index * 128 : (index + 1) * 128] = part
    fetch.wait()
    turned_ref[...] = held_ref[...].T
    wait_all(copies)


def pack(own, tokens, hidden_bias, hidden_weight, mixer_weight, output_weight):
    local, depth = tokens.shape
    chips = PLANE // 2
    columns = depth // 2
    rows = depth // chips
    first_rows = rows + mixer_weight.shape[0] // chips + 16
    vmem = pl.BlockSpec(memory_space=pltpu.VMEM)
    return pl.pallas_call(
        pack_kernel,
        in_specs=[pl.BlockSpec(memory_space=pltpu.SMEM), vmem] + [pl.BlockSpec(memory_space=pltpu.HBM)] * 4,
        out_specs=[vmem] * 3,
        out_shape=[
            jax.ShapeDtypeStruct((first_rows, columns), bf16),
            jax.ShapeDtypeStruct((rows, columns), bf16),
            jax.ShapeDtypeStruct((depth, local), bf16),
        ],
        scratch_shapes=[pltpu.VMEM((local, depth), bf16), pltpu.SemaphoreType.DMA((4,))],
        compiler_params=pltpu.CompilerParams(vmem_limit_bytes=60 << 20),
        cost_estimate=cost(3),
        name="pack",
    )(own, hidden_bias, tokens, hidden_weight, mixer_weight, output_weight)


def unpack_bias(entries):
    wide = entries.astype(f32)
    wide = wide[:, :128] + wide[:, 128:256] + wide[:, 256:384]
    return jnp.concatenate([wide[index : index + 1] for index in range(6)], axis=1)


def prepare_kernel(query_ref, key_ref, value_ref, joined_ref):
    joined_ref[...] = jnp.concatenate([query_ref[...].T, key_ref[...].T, value_ref[...].T], axis=1)


def prepare(weights):
    width, depth = weights[0].shape
    vmem = pl.BlockSpec(memory_space=pltpu.VMEM)
    return pl.pallas_call(
        prepare_kernel,
        in_specs=[vmem] * 3,
        out_specs=vmem,
        out_shape=jax.ShapeDtypeStruct((depth, 3 * width), bf16),
        compiler_params=pltpu.CompilerParams(vmem_limit_bytes=4 << 20),
        cost_estimate=cost(4),
        name="prepare",
    )(*weights)


def lanes(index, size):
    return pl.ds(pl.multiple_of(index * size, size), size)


def segments(lengths_ref, count, shape):
    places = lax.broadcasted_iota(jnp.int32, shape, len(shape) - 1)
    seg = jnp.zeros(shape, jnp.int32)
    end = jnp.int32(0)
    for s in range(count):
        end = end + lengths_ref[0, s]
        seg = seg + (places >= end).astype(jnp.int32)
    return seg


def masked_copies(seg, entries, count):
    zero = jnp.zeros_like(entries)
    return [jnp.where(seg == s, entries, zero) for s in range(count)]


def one_hot_rows(seg, count):
    rows = lax.broadcasted_iota(jnp.int32, (8, seg.shape[1]), 0)
    return jnp.where((rows == seg) & (rows < count), 1.0, 0.0).astype(f32)


def masked_sum(seg, wide, count):
    height = HEAD_DIM
    total = jnp.zeros((height, wide.shape[1]), f32)
    for s in range(count):
        total = total + jnp.where(seg == s, wide[s * height : (s + 1) * height], 0.0)
    return total


def feature_rows(vectors, proj_t):
    scale = HEAD_DIM ** (-0.25)
    widened = vectors.astype(f32)
    square = (0.5 * scale * scale) * jnp.sum(widened * widened, axis=0, keepdims=True)
    return (jnp.exp(scale * dot(proj_t, vectors) - square) * (1.0 / math.sqrt(FEAT))).astype(bf16)


def attend_kernel(
    count,
    lengths_ref,
    place_ref,
    x0_ref,
    x1_ref,
    x2_ref,
    x3_ref,
    query_weight_ref,
    key_weight_ref,
    value_weight_ref,
    query_bias_ref,
    key_bias_ref,
    value_bias_ref,
    proj_ref,
    qkv_ref,
    qf_ref,
    kf_ref,
    state_ref,
    out_ref,
    den_ref,
    p0_ref,
    p1_ref,
    p2_ref,
    p3_ref,
    mixed_ref,
):
    h = pl.program_id(0)
    tokens = (x0_ref, x1_ref, x2_ref, x3_ref)
    shards, local = len(tokens), x0_ref.shape[1]
    heads = pl.num_programs(0)
    width = query_weight_ref.shape[0]
    spread_rows = count * HEAD_DIM

    @pl.when(h == 0)
    def _():
        for kind, (weight, bias) in enumerate(
            (
                (query_weight_ref, query_bias_ref),
                (key_weight_ref, key_bias_ref),
                (value_weight_ref, value_bias_ref),
            )
        ):
            column = jnp.broadcast_to(bias[...], (8, width)).T[:, 0:1]
            for s in range(shards):
                qkv_ref[kind * width : (kind + 1) * width, lanes(lax.bitwise_xor(place_ref[0], s), local)] = (
                    dot(weight[...], tokens[s][...]) + column
                ).astype(bf16)

    def rows(kind):
        begin = pl.multiple_of(kind * width + h * HEAD_DIM, HEAD_DIM)
        return qkv_ref[pl.ds(begin, HEAD_DIM), :]

    seg = segments(lengths_ref, count, (1, shards * local))
    hot = one_hot_rows(seg, count)
    proj_t = proj_ref[0].T
    q_feat = feature_rows(rows(0), proj_t)
    k_feat = feature_rows(rows(1), proj_t)
    qf_ref[0] = q_feat
    kf_ref[0] = k_feat
    wide = jnp.concatenate(
        masked_copies(seg, rows(2), count) + [jnp.concatenate([hot, hot], axis=0).astype(bf16)], axis=0
    )
    state = dot_cols(wide, k_feat)
    sums = state[spread_rows : spread_rows + 8]
    high = sums.astype(bf16).astype(f32)
    state_ref[0, :spread_rows] = state[:spread_rows].astype(bf16)
    state_ref[0, spread_rows : spread_rows + 16] = jnp.concatenate([high, high], axis=0).astype(bf16)
    state_ref[0, spread_rows + 16 :] = jnp.concatenate(
        [sums - high, jnp.zeros_like(high)], axis=0
    ).astype(bf16)
    through = dot(state_ref[0], q_feat)
    scores = through[spread_rows : spread_rows + 8] + through[spread_rows + 16 : spread_rows + 24]
    den = jnp.sum(hot * scores, axis=0, keepdims=True) + (seg >= count).astype(f32)
    out = masked_sum(seg, through, count) / den
    out_ref[...] = out
    den_ref[0] = jnp.broadcast_to(den, den_ref.shape[1:])
    mixed_ref[pl.ds(pl.multiple_of(h * HEAD_DIM, HEAD_DIM), HEAD_DIM), :] = out.astype(bf16)

    @pl.when(h == heads - 1)
    def _():
        for s, piece in enumerate((p0_ref, p1_ref, p2_ref, p3_ref)):
            piece[...] = mixed_ref[:, lanes(lax.bitwise_xor(place_ref[0], s), local)]


def attend(tokens, weights, biases, proj, lengths, place):
    shards, local, depth = len(tokens), tokens[0].shape[1], weights[0].shape[1]
    heads, head_dim, feat = proj.shape
    total = shards * local
    count = lengths.shape[1] - 1
    width = heads * head_dim
    state_rows = count * head_dim + 32
    smem = pl.BlockSpec(memory_space=pltpu.SMEM)

    def whole(*shape):
        return pl.BlockSpec(shape, lambda h: (0,) * len(shape))

    def per_head(*shape):
        return pl.BlockSpec((1,) + shape, lambda h: (h,) + (0,) * len(shape))

    return pl.pallas_call(
        functools.partial(attend_kernel, count),
        grid=(heads,),
        in_specs=[
            smem,
            smem,
        ]
        + [whole(depth, local)] * shards
        + [whole(width, depth)] * 3
        + [whole(1, width)] * 3
        + [per_head(head_dim, feat)],
        out_specs=[
            whole(3 * width, total),
            per_head(feat, total),
            per_head(feat, total),
            per_head(state_rows, feat),
            pl.BlockSpec((head_dim, total), lambda h: (h, 0)),
            per_head(8, total),
        ]
        + [whole(width, local)] * shards,
        out_shape=[
            jax.ShapeDtypeStruct((3 * width, total), bf16),
            jax.ShapeDtypeStruct((heads, feat, total), bf16),
            jax.ShapeDtypeStruct((heads, feat, total), bf16),
            jax.ShapeDtypeStruct((heads, state_rows, feat), bf16),
            jax.ShapeDtypeStruct((width, total), f32),
            jax.ShapeDtypeStruct((heads, 8, total), f32),
        ]
        + [jax.ShapeDtypeStruct((width, local), bf16)] * shards,
        scratch_shapes=[pltpu.VMEM((width, total), bf16)],
        compiler_params=pltpu.CompilerParams(vmem_limit_bytes=16 << 20),
        cost_estimate=cost(8),
        name="attend",
    )(lengths, place, *tokens, *weights, *biases, proj)


def feature_back_rows(grad_feat, feat, vectors, proj_w):
    scale = HEAD_DIM ** (-0.25)
    grad_proj = grad_feat * feat.astype(f32)
    pulled = scale * dot(proj_w, grad_proj.astype(bf16))
    return pulled - (scale * scale) * vectors.astype(f32) * jnp.sum(grad_proj, axis=0, keepdims=True)


def attend_back_kernel(
    count,
    lengths_ref,
    place_ref,
    qkv_ref,
    qf_ref,
    kf_ref,
    state_ref,
    out_ref,
    den_ref,
    g0_ref,
    g1_ref,
    g2_ref,
    g3_ref,
    proj_ref,
    weight_ref,
    sums_ref,
    grad_ref,
    send_ref,
    keep_ref,
    heads_ref,
    small_ref,
):
    h = pl.program_id(0)
    width, local = g0_ref.shape
    shards = grad_ref.shape[1] // local
    depth = weight_ref.shape[0]
    heads = pl.num_programs(0)
    spread_rows = count * HEAD_DIM

    @pl.when(h == 0)
    def _():
        for s, piece in enumerate((g0_ref, g1_ref, g2_ref, g3_ref)):
            heads_ref[:, lanes(lax.bitwise_xor(place_ref[0], s), local)] = piece[...]

    def at(kind):
        return pl.ds(pl.multiple_of(kind * width + h * HEAD_DIM, HEAD_DIM), HEAD_DIM)

    seg = segments(lengths_ref, count, (1, shards * local))
    hot = one_hot_rows(seg, count)
    query, key, value = qkv_ref[at(0), :], qkv_ref[at(1), :], qkv_ref[at(2), :]
    q_feat, k_feat = qf_ref[0], kf_ref[0]
    grad_head = heads_ref[pl.ds(pl.multiple_of(h * HEAD_DIM, HEAD_DIM), HEAD_DIM), :].astype(f32)
    den = den_ref[0, 0:1, :]
    grad_numer = (grad_head / den).astype(bf16)
    grad_den = -jnp.sum(grad_head * out_ref[...], axis=0, keepdims=True) / den
    marked = hot * grad_den
    high = marked.astype(bf16).astype(f32)
    low = marked - high
    numer_wide = jnp.concatenate(
        masked_copies(seg, grad_numer, count)
        + [
            jnp.concatenate([high, low], axis=0).astype(bf16),
            jnp.concatenate([high, jnp.zeros_like(high)], axis=0).astype(bf16),
        ],
        axis=0,
    )
    grad_state = dot_cols(numer_wide[: spread_rows + 16], q_feat)
    sums = grad_state[spread_rows : spread_rows + 8] + grad_state[spread_rows + 8 : spread_rows + 16]
    sums_high = sums.astype(bf16).astype(f32)
    grad_state = jnp.concatenate(
        [
            grad_state[:spread_rows].astype(bf16),
            jnp.concatenate([sums_high, sums - sums_high], axis=0).astype(bf16),
        ],
        axis=0,
    )
    value_wide = jnp.concatenate(
        masked_copies(seg, value, count) + [jnp.concatenate([hot, hot], axis=0).astype(bf16)], axis=0
    )
    proj_w = proj_ref[0]
    grad_qfeat = dot_rows(state_ref[0], numer_wide)
    grad_ref[at(0), :] = feature_back_rows(grad_qfeat, q_feat, query, proj_w).astype(bf16)
    grad_kfeat = dot_rows(grad_state, value_wide)
    grad_ref[at(1), :] = feature_back_rows(grad_kfeat, k_feat, key, proj_w).astype(bf16)
    grad_ref[at(2), :] = masked_sum(seg, dot(grad_state[:spread_rows], k_feat), count).astype(bf16)

    @pl.when(h == heads - 1)
    def _():
        small_ref[...] = sums_ref[...]
        totals = dot_cols(jnp.ones((8, shards * local), bf16), grad_ref[...])
        for t in range(shards):

            @pl.when(place_ref[0] == t)
            def _():
                for kind, row in enumerate(BIAS_ROWS):
                    small_ref[row : row + 1, t * width : (t + 1) * width] = totals[
                        0:1, kind * width : (kind + 1) * width
                    ]

        small = jnp.concatenate(
            [small_ref[:, begin : begin + local] for begin in range(0, depth, local)], axis=0
        )
        rows = small.shape[0]
        high = small.astype(bf16)
        low = (small - high.astype(f32)).astype(bf16)
        for s in range(shards):
            out = (keep_ref, send_ref)[s % 2].at[s // 2]
            out[:depth] = dot(
                weight_ref[...], grad_ref[:, lanes(lax.bitwise_xor(place_ref[0], s), local)]
            ).astype(bf16)
            out[depth : depth + rows] = high
            out[depth + rows :] = low


def attend_back(saved, pieces, proj, weight, sums, lengths, place):
    qkv, qf, kf, state, out, den = saved
    heads, feat, total = qf.shape
    width, local = pieces[0].shape
    shards = total // local
    depth = weight.shape[0]
    count = lengths.shape[1] - 1
    state_rows = state.shape[1]
    extra = 2 * sums.shape[0] * (depth // local)
    smem = pl.BlockSpec(memory_space=pltpu.SMEM)

    def whole(*shape):
        return pl.BlockSpec(shape, lambda h: (0,) * len(shape))

    def per_head(*shape):
        return pl.BlockSpec((1,) + shape, lambda h: (h,) + (0,) * len(shape))

    return pl.pallas_call(
        functools.partial(attend_back_kernel, count),
        grid=(heads,),
        in_specs=[
            smem,
            smem,
            whole(3 * width, total),
            per_head(feat, total),
            per_head(feat, total),
            per_head(state_rows, feat),
            pl.BlockSpec((HEAD_DIM, total), lambda h: (h, 0)),
            per_head(8, total),
        ]
        + [whole(width, local)] * shards
        + [per_head(HEAD_DIM, feat), whole(depth, 3 * width), whole(*sums.shape)],
        out_specs=[
            whole(3 * width, total),
            whole(shards // 2, depth + extra, local),
            whole(shards // 2, depth + extra, local),
        ],
        out_shape=[
            jax.ShapeDtypeStruct((3 * width, total), bf16),
            jax.ShapeDtypeStruct((shards // 2, depth + extra, local), bf16),
            jax.ShapeDtypeStruct((shards // 2, depth + extra, local), bf16),
        ],
        scratch_shapes=[pltpu.VMEM((width, total), bf16), pltpu.VMEM(sums.shape, f32)],
        compiler_params=pltpu.CompilerParams(vmem_limit_bytes=18 << 20),
        cost_estimate=cost(9),
        name="attend_back",
    )(lengths, place, qkv, qf, kf, state, out, den, *pieces, proj, weight, sums)


def slot_place(slot, half):
    k = slot // 2
    if half == 0:
        return 1 - k % 2, k // 2
    return 1 - k // 2, k % 2


def pick_blocks(own, turned_ref):
    slots = turned_ref.shape[0]
    return jnp.concatenate([turned_ref[lax.bitwise_xor(own, slot)] for slot in range(0, slots, 2)], axis=0)


def emit_slots(entries, outs, begin=0):
    height = outs[0].shape[2]
    count = entries.shape[1]
    for half in range(2):

        @pl.when(pl.program_id(0) // 2 == half)
        def _():
            for k in range(PLANE // 2):
                part, index = slot_place(2 * k, half)
                outs[2 * half + part][index, 0, :, begin : begin + count] = entries[k * height : (k + 1) * height]


def slot_outputs(shards, height, count):
    low = pl.BlockSpec((2, 1, height, count), lambda s: (0, jnp.minimum(s, 1), 0, 0))
    high = pl.BlockSpec((2, 1, height, count), lambda s: (0, jnp.maximum(s - 2, 0), 0, 0))
    shape = jax.ShapeDtypeStruct((2, shards // 2, height, count), bf16)
    return [low, low, high, high], [shape] * 4


def output_grad_kernel(own_ref, turned_ref, turned_far_ref, act_ref, act_far_ref, *outs):
    own = own_ref[0]
    grads = dot(pick_blocks(own, turned_ref), act_ref[0]) + dot(pick_blocks(own, turned_far_ref), act_far_ref[0])
    emit_slots(grads.astype(bf16), outs)


def output_grad(own, turned, turned_far, acts, acts_far):
    shards, rows, hidden = acts.shape
    slots, height, _ = turned.shape
    specs, shapes = slot_outputs(shards, height, hidden)
    whole = pl.BlockSpec((slots, height, rows), lambda s: (0, 0, 0))
    by_shard = pl.BlockSpec((1, rows, hidden), lambda s: (s, 0, 0))
    return pl.pallas_call(
        output_grad_kernel,
        grid=(shards,),
        in_specs=[pl.BlockSpec(memory_space=pltpu.SMEM), whole, whole, by_shard, by_shard],
        out_specs=specs,
        out_shape=shapes,
        compiler_params=pltpu.CompilerParams(vmem_limit_bytes=8 << 20),
        cost_estimate=cost(4),
        name="output_grad",
    )(own, turned, turned_far, acts, acts_far)


def hidden_grad_kernel(
    own_ref,
    first_ref,
    first_far_ref,
    grad_pre_ref,
    grad_pre_far_ref,
    branch_ref,
    branch_far_ref,
    mixed_ref,
    mixed_far_ref,
    *outs,
):
    own = own_ref[0]
    hidden = grad_pre_ref.shape[2]
    grads = dot(pick_blocks(own, first_ref), grad_pre_ref[0]) + dot(
        pick_blocks(own, first_far_ref), grad_pre_far_ref[0]
    )
    emit_slots(grads.astype(bf16), outs)
    grads = dot_cols(pick_blocks(own, branch_ref), mixed_ref[0]) + dot_cols(
        pick_blocks(own, branch_far_ref), mixed_far_ref[0]
    )
    emit_slots(grads.astype(bf16), outs, hidden)


def hidden_grad(own, first, first_far, grad_pre, grad_pre_far, branch, branch_far, mixed, mixed_far):
    shards, rows, hidden = grad_pre.shape
    slots, height, _ = first.shape
    width = mixed.shape[1]
    specs, shapes = slot_outputs(shards, height, hidden + width)
    whole = pl.BlockSpec((slots, height, rows), lambda s: (0, 0, 0))
    by_shard = pl.BlockSpec((1, rows, hidden), lambda s: (s, 0, 0))
    piece = pl.BlockSpec((1, width, rows), lambda s: (s, 0, 0))
    return pl.pallas_call(
        hidden_grad_kernel,
        grid=(shards,),
        in_specs=[
            pl.BlockSpec(memory_space=pltpu.SMEM),
            whole,
            whole,
            by_shard,
            by_shard,
            whole,
            whole,
            piece,
            piece,
        ],
        out_specs=specs,
        out_shape=shapes,
        compiler_params=pltpu.CompilerParams(vmem_limit_bytes=10 << 20),
        cost_estimate=cost(5),
        name="hidden_grad",
    )(own, first, first_far, grad_pre, grad_pre_far, branch, branch_far, mixed, mixed_far)


def qkv_grad_kernel(own_ref, place_ref, x0_ref, x1_ref, x2_ref, x3_ref, grad_ref, even_ref, odd_ref, hold_ref):
    local = x0_ref.shape[1]
    depth = hold_ref.shape[0] * hold_ref.shape[1]
    grads = sum(
        dot_cols(block[:depth], grad_ref[:, lanes(lax.bitwise_xor(place_ref[0], s), local)])
        for s, block in enumerate((x0_ref, x1_ref, x2_ref, x3_ref))
    )
    hold_ref[...] = grads.astype(bf16).reshape(hold_ref.shape)
    rows = even_ref.shape[4]
    for slot in range(hold_ref.shape[0]):
        target = odd_ref if slot % 2 else even_ref
        block = hold_ref[lax.bitwise_xor(own_ref[0], slot)]
        for half in range(2):
            target[(half,) + slot_place(slot, half) + (0,)] = block[half * rows : (half + 1) * rows]


def qkv_grad(own, place, slots, depth, tokens, grads):
    count = grads.shape[0]
    vmem = pl.BlockSpec(memory_space=pltpu.VMEM)
    shape = jax.ShapeDtypeStruct((2, 2, slots // 4, 1, depth // slots // 2, count), bf16)
    return pl.pallas_call(
        qkv_grad_kernel,
        in_specs=[pl.BlockSpec(memory_space=pltpu.SMEM)] * 2 + [vmem] * (len(tokens) + 1),
        out_specs=[vmem, vmem],
        out_shape=[shape, shape],
        scratch_shapes=[pltpu.VMEM((slots, depth // slots, count), bf16)],
        compiler_params=pltpu.CompilerParams(vmem_limit_bytes=9 << 20),
        cost_estimate=cost(2),
        name="qkv_grad",
    )(own, place, *tokens, grads)


def norm_rows(resid):
    center = resid - jnp.mean(resid, axis=-1, keepdims=True)
    inverse = lax.rsqrt(jnp.mean(center * center, axis=-1, keepdims=True) + eps)
    return center * inverse, inverse


HELD = [(0, (0, 1, 2, 3)), (2, (0, 1, 2, 3)), (4, (0, 1, 2, 3)), (6, (0, 1)), (6, (2, 3))]
HELD = HELD + [(mask ^ 1, shards) for mask, shards in HELD]


def place_copies(own, held, begin, rows, target, sems):
    columns = held[0].shape[2]
    copies = []
    for index, (piece, (mask, shards)) in enumerate(zip(held, HELD)):
        source = lax.bitwise_xor(own, mask)
        chip = lax.shift_right_logical(source, 1)
        core = lax.bitwise_and(source, 1)
        copies.append(
            pltpu.make_async_copy(
                piece.at[:, pl.ds(begin, rows), :],
                target.at[shards[0] : shards[-1] + 1, chip, :, lanes(core, columns)],
                sems.at[index],
            )
        )
    return copies


def start_all(copies):
    for entries in copies:
        for copy in entries:
            copy.start()


def wait_all(entries):
    for copy in entries:
        copy.wait()


def ffn_up_kernel(
    own_ref,
    tokens_ref,
    p0_ref,
    p1_ref,
    p2_ref,
    p3_ref,
    mixer_bias_ref,
    gain_ref,
    shift_ref,
    *refs,
):
    held, refs = refs[: len(HELD)], refs[len(HELD) :]
    parts, refs = refs[:4], refs[4:]
    (
        normed_ref,
        inverse_ref,
        turned_ref,
        mixed_ref,
        act_ref,
        slope_ref,
        mixer_ref,
        hidden_ref,
        bias_ref,
        mixer_sem,
        hidden_sem,
        bias_sem,
    ) = refs
    own = own_ref[0]
    shards, chips, mixer_rows, depth = mixer_ref.shape
    hidden_rows = hidden_ref.shape[2]
    mixer_copies = place_copies(own, held, hidden_rows, mixer_rows, mixer_ref, mixer_sem)
    hidden_copies = place_copies(own, held, 0, hidden_rows, hidden_ref, hidden_sem)
    bias_rows = parts[0].shape[0] - 16
    bias_copies = [
        pltpu.make_async_copy(part.at[bias_rows : bias_rows + 16], bias_ref.at[s], bias_sem.at[s])
        for s, part in enumerate(parts)
    ]
    start_all([mixer_copies, bias_copies, hidden_copies])
    resid = tokens_ref[...].astype(f32) + mixer_bias_ref[...]
    for s, piece in enumerate((p0_ref, p1_ref, p2_ref, p3_ref)):
        mixed_ref[s] = piece[...]
        if s == 0:
            wait_all(mixer_copies)
        resid = resid + dot_rows(piece[...], mixer_ref[s].reshape(chips * mixer_rows, depth))
    normed, inverse = norm_rows(resid)
    normed_ref[...] = normed
    inverse_ref[...] = jnp.broadcast_to(inverse, inverse_ref.shape)
    first_low = (normed * gain_ref[...] + shift_ref[...]).astype(bf16)
    turned_ref[...] = first_low.T
    for s in range(shards):
        if s == 0:
            wait_all(hidden_copies + bias_copies)
        bias = unpack_bias(bias_ref[s])
        pre = dot(first_low, hidden_ref[s].reshape(chips * hidden_rows, hidden_ref.shape[3])) + bias
        phi = 0.5 * (1.0 + lax.erf(pre * math.sqrt(0.5)))
        act_ref[s] = (pre * phi).astype(bf16)
        slope_ref[s] = (
            phi + pre * jnp.exp(-0.5 * pre * pre) * (1.0 / math.sqrt(2.0 * math.pi))
        ).astype(bf16)


def ffn_up(own, tokens, pieces, mixer_bias, gain, shift_by, parts, held, mixer_rows):
    rows, depth = tokens.shape
    shards = len(pieces)
    chips = PLANE // 2
    hidden = 2 * held[0].shape[2]
    hidden_rows = held[0].shape[1] - mixer_rows
    vmem = pl.BlockSpec(memory_space=pltpu.VMEM)
    return pl.pallas_call(
        ffn_up_kernel,
        in_specs=[pl.BlockSpec(memory_space=pltpu.SMEM)]
        + [vmem] * (1 + shards + 3)
        + [pl.BlockSpec(memory_space=pl.ANY)] * (len(HELD) + shards),
        out_specs=[vmem] * 6,
        out_shape=[
            jax.ShapeDtypeStruct((rows, depth), f32),
            jax.ShapeDtypeStruct((rows, 128), f32),
            jax.ShapeDtypeStruct((depth, rows), bf16),
            jax.ShapeDtypeStruct((shards,) + pieces[0].shape, bf16),
            jax.ShapeDtypeStruct((shards, rows, hidden), bf16),
            jax.ShapeDtypeStruct((shards, rows, hidden), bf16),
        ],
        scratch_shapes=[
            pltpu.VMEM((shards, chips, mixer_rows, depth), bf16),
            pltpu.VMEM((shards, chips, hidden_rows, hidden), bf16),
            pltpu.VMEM((shards, 16, held[0].shape[2]), bf16),
            pltpu.SemaphoreType.DMA((len(HELD),)),
            pltpu.SemaphoreType.DMA((len(HELD),)),
            pltpu.SemaphoreType.DMA((shards,)),
        ],
        compiler_params=pltpu.CompilerParams(vmem_limit_bytes=17 << 20),
        cost_estimate=cost(8),
        name="ffn_up",
    )(own, tokens, *pieces, mixer_bias, gain, shift_by, *held, *parts)


def norm_rows_back(scaled, normed, inverse):
    return inverse * (
        scaled
        - jnp.mean(scaled, axis=-1, keepdims=True)
        - normed * jnp.mean(scaled * normed, axis=-1, keepdims=True)
    )


def column_sum(entries):
    return jnp.sum(entries, axis=0, keepdims=True)


def ffn_down_kernel(
    own_ref,
    normed_ref,
    inverse_ref,
    act_ref,
    slope_ref,
    cotangent_ref,
    first_gain_ref,
    first_shift_ref,
    output_bias_ref,
    gain_ref,
    shift_ref,
    *refs,
):
    held, refs = refs[: len(HELD)], refs[len(HELD) :]
    held_out, refs = refs[: len(HELD)], refs[len(HELD) :]
    (
        layer_ref,
        resid_ref,
        b0_ref,
        b1_ref,
        b2_ref,
        b3_ref,
        grad_ffn_ref,
        grad_pre_ref,
        grad_branch_ref,
        sums_ref,
        mixer_ref,
        hidden_ref,
        output_ref,
        mixer_sem,
        hidden_sem,
        output_sem,
    ) = refs
    own, place = own_ref[0], own_ref[1]
    shards, chips, mixer_rows, depth = mixer_ref.shape
    hidden_rows = hidden_ref.shape[2]
    hidden = hidden_ref.shape[3]
    output_copies = place_copies(own, held_out, 0, output_ref.shape[2], output_ref, output_sem)
    hidden_copies = place_copies(own, held, 0, hidden_rows, hidden_ref, hidden_sem)
    mixer_copies = place_copies(own, held, hidden_rows, mixer_rows, mixer_ref, mixer_sem)
    start_all([output_copies, hidden_copies, mixer_copies])
    normed_one = normed_ref[...]
    resid = normed_one * first_gain_ref[...] + first_shift_ref[...] + output_bias_ref[...]
    wait_all(output_copies)
    for s in range(shards):
        resid = resid + dot(act_ref[s], output_ref[s].reshape(hidden, depth))
    normed, inverse = norm_rows(resid)
    layer_ref[...] = (normed * gain_ref[...] + shift_ref[...]).astype(bf16)
    grad_out = cotangent_ref[...].astype(f32)
    sums_ref[0:1] = column_sum(grad_out * normed)
    sums_ref[1:2] = column_sum(grad_out)
    grad_two = norm_rows_back(grad_out * gain_ref[...], normed, inverse)
    grad_ffn = grad_two.astype(bf16)
    grad_ffn_ref[...] = grad_ffn.T
    sums_ref[2:3] = column_sum(grad_ffn.astype(f32))
    grad_first = grad_two
    for s in range(shards):
        grad_pre = (
            dot_cols(grad_ffn, output_ref[s].reshape(hidden, depth)) * slope_ref[s].astype(f32)
        ).astype(bf16)
        grad_pre_ref[s] = grad_pre
        sums_ref[pl.ds(8 + lax.bitwise_xor(place, s), 1)] = column_sum(grad_pre.astype(f32))
        if s == 0:
            wait_all(hidden_copies)
        grad_first = grad_first + dot_cols(grad_pre, hidden_ref[s].reshape(depth, hidden))
    sums_ref[3:4] = column_sum(grad_first * normed_one)
    sums_ref[4:5] = column_sum(grad_first)
    grad_one = norm_rows_back(grad_first * first_gain_ref[...], normed_one, inverse_ref[:, 0:1])
    resid_ref[...] = grad_one
    grad_branch = grad_one.astype(bf16)
    branch_turned = grad_branch.T
    grad_branch_ref[...] = branch_turned
    sums_ref[5:6] = column_sum(grad_branch.astype(f32))
    sums_ref[6:8] = jnp.zeros((2, depth), f32)
    sums_ref[8 + shards :] = jnp.zeros((8 - shards, depth), f32)
    for s, back in enumerate((b0_ref, b1_ref, b2_ref, b3_ref)):
        if s == 0:
            wait_all(mixer_copies)
        back[...] = dot(mixer_ref[s].reshape(chips * mixer_rows, depth), branch_turned).astype(bf16)


def ffn_down(own, normed, inverse, acts, slopes, cotangent, vectors, held, held_out, mixer_rows):
    rows, depth = normed.shape
    shards, _, hidden = acts.shape
    chips = PLANE // 2
    hidden_rows = held[0].shape[1] - mixer_rows
    output_rows = held_out[0].shape[1]
    vmem = pl.BlockSpec(memory_space=pltpu.VMEM)
    width = chips * mixer_rows
    return pl.pallas_call(
        ffn_down_kernel,
        in_specs=[pl.BlockSpec(memory_space=pltpu.SMEM)]
        + [vmem] * 10
        + [pl.BlockSpec(memory_space=pl.ANY)] * (2 * len(HELD)),
        out_specs=[vmem] * (6 + shards),
        out_shape=[
            jax.ShapeDtypeStruct((rows, depth), bf16),
            jax.ShapeDtypeStruct((rows, depth), f32),
        ]
        + [jax.ShapeDtypeStruct((width, rows), bf16)] * shards
        + [
            jax.ShapeDtypeStruct((depth, rows), bf16),
            jax.ShapeDtypeStruct((shards, rows, hidden), bf16),
            jax.ShapeDtypeStruct((depth, rows), bf16),
            jax.ShapeDtypeStruct((16, depth), f32),
        ],
        scratch_shapes=[
            pltpu.VMEM((shards, chips, mixer_rows, depth), bf16),
            pltpu.VMEM((shards, chips, hidden_rows, hidden), bf16),
            pltpu.VMEM((shards, chips, output_rows, depth), bf16),
            pltpu.SemaphoreType.DMA((len(HELD),)),
            pltpu.SemaphoreType.DMA((len(HELD),)),
            pltpu.SemaphoreType.DMA((len(HELD),)),
        ],
        compiler_params=pltpu.CompilerParams(vmem_limit_bytes=24 << 20),
        cost_estimate=cost(15),
        name="ffn_down",
    )(own, normed, inverse, acts, slopes, cotangent, *vectors, *held, *held_out)


def fold_kernel(depth, keep_ref, far_ref, mine_ref, other_ref):
    rows = (keep_ref.shape[1] - depth) // 2
    for s, out in enumerate((mine_ref, other_ref)):
        out[:depth] = (keep_ref[s, :depth].astype(f32) + far_ref[s, :depth].astype(f32)).astype(bf16)
        small = sum(
            ref[s, depth : depth + rows].astype(f32) + ref[s, depth + rows :].astype(f32) for ref in (keep_ref, far_ref)
        )
        high = small.astype(bf16)
        out[depth : depth + rows] = high
        out[depth + rows :] = (small - high.astype(f32)).astype(bf16)


def fold(depth, keep, far):
    vmem = pl.BlockSpec(memory_space=pltpu.VMEM)
    return pl.pallas_call(
        functools.partial(fold_kernel, depth),
        in_specs=[vmem] * 2,
        out_specs=[vmem] * 2,
        out_shape=[jax.ShapeDtypeStruct(keep.shape[1:], bf16)] * 2,
        compiler_params=pltpu.CompilerParams(vmem_limit_bytes=6 << 20),
        cost_estimate=cost(2),
        name="fold",
    )(keep, far)


def join_cores_kernel(near_ref, far_ref, *outs):
    for half in range(2):
        for part in range(2):
            outs[2 * half + part][...] = (
                near_ref[half, part].astype(f32) + far_ref[half, part].astype(f32)
            ).astype(bf16)


def join_cores(near, far):
    vmem = pl.BlockSpec(memory_space=pltpu.VMEM)
    return pl.pallas_call(
        join_cores_kernel,
        in_specs=[vmem] * 2,
        out_specs=[vmem] * 4,
        out_shape=[jax.ShapeDtypeStruct(near.shape[2:], bf16)] * 4,
        compiler_params=pltpu.CompilerParams(vmem_limit_bytes=4 << 20),
        cost_estimate=cost(2),
        name="join_cores",
    )(near, far)


def finish_tokens_kernel(resid_ref, mine_ref, far_ref, out_ref, small_ref):
    depth = resid_ref.shape[1]
    rows = small_ref.shape[0]
    total = mine_ref[:depth].astype(f32) + far_ref[:depth].astype(f32)
    out_ref[...] = resid_ref[...] + total.T
    small_ref[...] = sum(
        ref[depth : depth + rows].astype(f32) + ref[depth + rows :].astype(f32) for ref in (mine_ref, far_ref)
    )


def finish_tokens(resid, mine, far):
    local, depth = resid.shape
    rows = (mine.shape[0] - depth) // 2
    vmem = pl.BlockSpec(memory_space=pltpu.VMEM)
    return pl.pallas_call(
        finish_tokens_kernel,
        in_specs=[vmem] * 3,
        out_specs=[vmem] * 2,
        out_shape=[jax.ShapeDtypeStruct(resid.shape, f32), jax.ShapeDtypeStruct((rows, local), f32)],
        compiler_params=pltpu.CompilerParams(vmem_limit_bytes=6 << 20),
        cost_estimate=cost(1),
        name="finish_tokens",
    )(resid, mine, far)


def finish_hidden_kernel(a_ref, b_ref, hidden_ref, mixer_ref):
    total = a_ref[...].astype(f32) + b_ref[...].astype(f32)
    hidden = hidden_ref.shape[1]
    hidden_ref[...] = total[:, :hidden]
    mixer_ref[...] = total[:, hidden:].T


def finish_hidden(entries, hidden):
    rows, columns = entries[0].shape
    vmem = pl.BlockSpec(memory_space=pltpu.VMEM)
    return pl.pallas_call(
        finish_hidden_kernel,
        in_specs=[vmem] * 2,
        out_specs=[vmem] * 2,
        out_shape=[
            jax.ShapeDtypeStruct((rows, hidden), f32),
            jax.ShapeDtypeStruct((columns - hidden, rows), f32),
        ],
        compiler_params=pltpu.CompilerParams(vmem_limit_bytes=4 << 20),
        cost_estimate=cost(1),
        name="finish_hidden",
    )(*entries)


def finish_qkv_kernel(a_ref, b_ref, c_ref, d_ref, query_ref, key_ref, value_ref):
    rows, width = a_ref.shape[0], query_ref.shape[1]
    low = a_ref[...].astype(f32) + b_ref[...].astype(f32)
    high = c_ref[...].astype(f32) + d_ref[...].astype(f32)
    for kind, out in enumerate((query_ref, key_ref, value_ref)):
        out[:rows] = low[:, kind * width : (kind + 1) * width]
        out[rows:] = high[:, kind * width : (kind + 1) * width]


def finish_qkv(entries):
    rows, columns = entries[0].shape
    vmem = pl.BlockSpec(memory_space=pltpu.VMEM)
    return pl.pallas_call(
        finish_qkv_kernel,
        in_specs=[vmem] * 4,
        out_specs=[vmem] * 3,
        out_shape=[jax.ShapeDtypeStruct((2 * rows, columns // 3), f32)] * 3,
        compiler_params=pltpu.CompilerParams(vmem_limit_bytes=3 << 20),
        cost_estimate=cost(1),
        name="finish_qkv",
    )(*entries)


BIAS_ROWS = (6, 7, 12)


def swap(values, mask):
    size = lax.axis_size("dp")
    return lax.ppermute(values, "dp", [(i, i ^ mask) for i in range(size)])


def cross(values, mask):
    size = lax.axis_size("tensor")
    return lax.ppermute(values, "tensor", [(i, i ^ mask) for i in range(size)])


def after(values, *others):
    return lax.optimization_barrier((values, others))[0]


def from_neighbours(payload):
    return cross(payload, 1), cross(payload, 2)


def all_shards(payload, near, far):
    return [payload, near, far, cross(far, 1)]


def spread_plane(stack, between=()):
    over_x, over_y = after((swap(stack, 2), swap(stack, 4)), *between)
    return [stack, over_x, over_y, swap(over_x[:2], 4), swap(over_y[2:], 2)]


def other_core(held, before=()):
    return [swap(entry, 1) for entry in after(held, *before)]


def add_low(*entries):
    return sum(entry.astype(f32) for entry in entries).astype(bf16)


def sum_first(near, before=(), between=()):
    send_low, keep_low, send_high, keep_high = near
    send_low, send_high = after((send_low, send_high), *before)
    low, high = after((swap(send_low, 2), swap(send_high, 4)), *between)
    return (
        [add_low(keep_low[0], low[0]), add_low(keep_high[0], high[0])],
        [add_low(keep_low[1], low[1]), add_low(keep_high[1], high[1])],
    )


def sum_second(stay, send, between=()):
    low, high = after((swap(send[0], 4), swap(send[1], 2)), *between)
    return [add_low(stay[0], low), add_low(stay[1], high)]


def scatter_all(halves, axis):
    parts = []
    for half in range(2):
        blocks = []
        for i in range(PLANE):
            part, index = slot_place(i, half)
            blocks.append(halves[i % 2][2 * half + part][index])
        parts.append(jnp.stack(blocks, axis=1))
    whole = jnp.concatenate(parts, axis=axis)
    whole = whole.reshape(whole.shape[:1] + (-1,) + whole.shape[-1:])
    return lax.psum_scatter(whole, "dp", scatter_dimension=1, tiled=True)


def pair_shards(grads):
    return after(jnp.stack([grads[1], grads[3]]))


def join_shards(grads, pair, between=()):
    near = after(cross(pair, 1), *between)
    mine, other = add_low(grads[0], near[0]), add_low(grads[2], near[1])
    return mine, cross(other, 2)


def by_shard(halves):
    return [half[s] for half in halves for s in range(half.shape[0])]


def small_sum(values):
    size = lax.axis_size("dp")
    if size != PLANE:
        values = lax.psum(values, "dp")
    else:
        for mask in (1, 2, 4):
            values = values + swap(values, mask)
    return values


def body(
    tokens,
    lengths,
    query_weight,
    query_bias,
    key_weight,
    key_bias,
    value_weight,
    value_bias,
    feature_proj,
    mixer_weight,
    mixer_bias,
    first_gain,
    first_shift,
    hidden_weight,
    hidden_bias,
    output_weight,
    output_bias,
    second_gain,
    second_shift,
    cotangent,
):
    depth = tokens.shape[1]
    shards = lax.axis_size("tensor")
    place = lax.axis_index("tensor").astype(jnp.int32)
    plane = (lax.axis_index("dp") % PLANE).astype(jnp.int32)
    width = query_weight.shape[1]
    hidden = hidden_weight.shape[1]
    mixer_rows = mixer_weight.shape[0] // (PLANE // 2)
    own = jnp.stack([plane, place])
    slot_of = plane[None] if lax.axis_size("dp") == PLANE else jnp.zeros((1,), jnp.int32)

    def row(vector):
        return vector.reshape(1, -1)

    def blocks(turned):
        return turned.reshape(PLANE, turned.shape[0] // PLANE, turned.shape[1])

    payload, payload_out, turned = pack(
        own, tokens, hidden_bias.reshape(-1, 128), hidden_weight, mixer_weight, output_weight
    )
    near, far = from_neighbours(payload)
    parts = all_shards(payload, near, far)
    near_out, far_out = from_neighbours(after(payload_out, far))
    parts_out = all_shards(payload_out, near_out, far_out)
    near, far = from_neighbours(after(turned, parts[3]))
    weights = [query_weight.T, key_weight.T, value_weight.T]
    qkv_weight = prepare(after(weights, payload))
    rows = payload.shape[0] - 16
    stack = jnp.stack([part[:rows] for part in parts])
    stack_far = swap(stack, 1)
    stack_out = jnp.stack(parts_out)
    around = spread_plane(stack, between=(near, far, qkv_weight, stack_far, stack_out))
    tokens_all = all_shards(turned, near, far)
    crossed = [stack_far] + other_core(around[1:3])
    tokens_all = after(tokens_all, *crossed, *around[3:])
    *saved, p0, p1, p2, p3 = attend(
        tokens_all,
        weights,
        [row(query_bias), row(key_bias), row(value_bias)],
        feature_proj,
        lengths,
        place[None],
    )
    around_out = spread_plane(stack_out, between=(p0,))
    pieces = [p0] + [cross(p, s) for s, p in ((1, p1), (2, p2), (3, p3))]
    held = around + crossed + other_core(around[3:])
    held_out = around_out + other_core(around_out[:3], pieces) + other_core(around_out[3:])
    normed, inverse, turned, mixed, acts, slopes = ffn_up(
        own, tokens, pieces, row(mixer_bias), row(first_gain), row(first_shift), parts, held, mixer_rows
    )
    acts_far, turned_far, mixed_far = swap(acts, 1), swap(turned, 1), swap(mixed, 1)
    held_out = after(held_out, turned_far, mixed_far)
    vectors = [row(v) for v in (first_gain, first_shift, output_bias, second_gain, second_shift)]
    layer_out, grad_resid, b0, b1, b2, b3, grad_ffn, grad_pre, grad_branch, sums = ffn_down(
        own, normed, inverse, acts, slopes, cotangent, vectors, held, held_out, mixer_rows
    )
    back = [b0] + [cross(b, s) for s, b in ((1, b1), (2, b2), (3, b3))]
    output_work = (blocks(grad_ffn), blocks(swap(grad_ffn, 1)), acts, acts_far)
    hidden_work = (
        blocks(turned),
        blocks(turned_far),
        grad_pre,
        swap(grad_pre, 1),
        blocks(grad_branch),
        blocks(swap(grad_branch, 1)),
        mixed,
        mixed_far,
    )
    fast = lax.axis_size("dp") == PLANE
    if fast:
        near_output = output_grad(slot_of, *output_work)
        near_output = after(near_output, hidden_work)
        near_hidden = hidden_grad(slot_of, *hidden_work)
        back = after(back, near_output, near_hidden)
    grad_qkv, send, keep = attend_back(
        saved, back, feature_proj, qkv_weight, sums, lengths, place[None]
    )
    far = cross(send, 1)
    if fast:
        even, odd = qkv_grad(slot_of, place[None], PLANE, depth, tokens_all, grad_qkv)
        stay_output, send_output = sum_first(near_output, between=(even,))
        stay_hidden, send_hidden = sum_first(near_hidden, between=send_output)
        near_qkv = join_cores(even, after(swap(odd, 1), send_hidden))
        mine, other = fold(depth, keep, after(far, near_qkv))
        far = cross(other, 2)
        grad_output = by_shard(sum_second(stay_output, send_output, between=(other,)))
        pair_output = pair_shards(grad_output)
        grad_hidden = by_shard(sum_second(stay_hidden, send_hidden, between=(pair_output,)))
        pair_hidden = pair_shards(grad_hidden)
        stay_qkv, send_qkv = sum_first(near_qkv, between=(pair_hidden,))
        grad_output = join_shards(grad_output, pair_output, send_qkv)
        low, high = swap(send_qkv[0], 4), swap(send_qkv[1], 2)
        grad_weights = finish_qkv([entry[0] for entry in (stay_qkv[0], low, stay_qkv[1], high)])
        grad_hidden = join_shards(grad_hidden, pair_hidden, grad_weights)
    else:
        zero, one = jnp.zeros((1,), jnp.int32), jnp.ones((1,), jnp.int32)
        mine, other = fold(depth, keep, far)
        far = cross(other, 2)
        grad_output = scatter_all([output_grad(slot, *output_work) for slot in (zero, one)], 0)
        grad_output = by_shard([0.5 * grad_output])
        grad_output = join_shards(grad_output, pair_shards(grad_output))
        grad_hidden = scatter_all([hidden_grad(slot, *hidden_work) for slot in (zero, one)], 0)
        grad_hidden = by_shard([0.5 * grad_hidden])
        grad_hidden = join_shards(grad_hidden, pair_shards(grad_hidden))
        grad_weight = scatter_all(
            [
                [entry[half, part] for half in range(2) for part in range(2)]
                for entry in qkv_grad(zero, place[None], PLANE, depth, tokens_all, grad_qkv)
            ],
            2,
        )[0].astype(f32)
        grad_weights = [grad_weight[:, kind * width : (kind + 1) * width] for kind in range(3)]
    tokens_grad, small = finish_tokens(grad_resid, mine, far)
    small = small_sum(small)
    small = after(small.reshape(-1, 16, small.shape[1]).transpose(1, 0, 2).reshape(16, -1))
    grad_output = sum(entry.astype(f32) for entry in grad_output).T
    grad_hidden, grad_mixer = finish_hidden(grad_hidden, hidden)
    return (
        layer_out,
        tokens_grad,
        grad_weights[0],
        small[6],
        grad_weights[1],
        small[7],
        grad_weights[2],
        small[12],
        grad_mixer,
        small[5],
        small[3],
        small[4],
        grad_hidden,
        small[8 : 8 + shards].reshape(-1),
        grad_output,
        small[2],
        small[0],
        small[1],
    )


def solution(mesh):
    placed = (
        P(("dp", "tensor"), None),
        P("dp", None),
        P(None, "tensor"),
        P("tensor"),
        P(None, "tensor"),
        P("tensor"),
        P(None, "tensor"),
        P("tensor"),
        P("tensor", None, None),
        P("tensor", None),
        P(),
        P(),
        P(),
        P(None, "tensor"),
        P("tensor"),
        P("tensor", None),
        P(),
        P(),
        P(),
        P(("dp", "tensor"), None),
    )
    return jax.shard_map(
        body,
        mesh=mesh,
        in_specs=placed,
        out_specs=(
            P(("dp", "tensor"), None),
            P(("dp", "tensor"), None),
            P("dp", "tensor"),
            P(),
            P("dp", "tensor"),
            P(),
            P("dp", "tensor"),
            P(),
            P("tensor", "dp"),
            P(),
            P(),
            P(),
            P("dp", "tensor"),
            P(),
            P("tensor", "dp"),
            P(),
            P(),
            P(),
        ),
        check_vma=False,
    )
```

```python
import functools
import math

import jax
import jax.numpy as jnp
from jax import lax
from jax.experimental import pallas as pl
from jax.experimental.pallas import tpu as pltpu
from jax.sharding import PartitionSpec as P

HEAD_DIM = 64
FEAT = 256
PLANE = 8
COST_RATE = 9e9

eps = 1e-06
bf16 = jnp.bfloat16
f32 = jnp.float32


def dot(left, right):
    return jnp.dot(left, right, preferred_element_type=f32)


def dot_rows(left, right):
    return lax.dot_general(left, right, (((0,), (0,)), ((), ())), preferred_element_type=f32)


def dot_cols(left, right):
    return lax.dot_general(left, right, (((1,), (1,)), ((), ())), preferred_element_type=f32)


def cost(micros):
    return pl.CostEstimate(flops=int(micros * COST_RATE), transcendentals=0, bytes_accessed=0)


def pack_kernel(
    own_ref, bias_ref, tokens_ref, hidden_ref, mixer_ref, output_ref, first_ref, second_ref, turned_ref, held_ref, sems
):
    rows, columns = second_ref.shape
    chip = lax.shift_right_logical(own_ref[0], 1)
    core = lax.bitwise_and(own_ref[0], 1)
    mixer_rows = mixer_ref.shape[0] // (PLANE // 2)

    def copy(source, height, target, sem):
        begin = pl.multiple_of(chip * height, 16)
        return pltpu.make_async_copy(
            source.at[pl.ds(begin, height), lanes(core, columns)], target, sem
        )

    copies = [
        copy(hidden_ref, rows, first_ref.at[0:rows], sems.at[0]),
        copy(mixer_ref, mixer_rows, first_ref.at[rows : rows + mixer_rows], sems.at[1]),
        copy(output_ref, rows, second_ref, sems.at[2]),
    ]
    fetch = pltpu.make_async_copy(tokens_ref, held_ref, sems.at[3])
    start_all([copies])
    fetch.start()
    wide = jnp.concatenate([bias_ref[...], jnp.zeros((16 - bias_ref.shape[0], 128), f32)], axis=0)
    for index in range(3):
        part = wide.astype(bf16)
        wide = wide - part.astype(f32)
        first_ref[rows + mixer_rows :, index * 128 : (index + 1) * 128] = part
    fetch.wait()
    turned_ref[...] = held_ref[...].T
    wait_all(copies)


def pack(own, tokens, hidden_bias, hidden_weight, mixer_weight, output_weight):
    local, depth = tokens.shape
    chips = PLANE // 2
    columns = depth // 2
    rows = depth // chips
    first_rows = rows + mixer_weight.shape[0] // chips + 16
    vmem = pl.BlockSpec(memory_space=pltpu.VMEM)
    return pl.pallas_call(
        pack_kernel,
        in_specs=[pl.BlockSpec(memory_space=pltpu.SMEM), vmem] + [pl.BlockSpec(memory_space=pltpu.HBM)] * 4,
        out_specs=[vmem] * 3,
        out_shape=[
            jax.ShapeDtypeStruct((first_rows, columns), bf16),
            jax.ShapeDtypeStruct((rows, columns), bf16),
            jax.ShapeDtypeStruct((depth, local), bf16),
        ],
        scratch_shapes=[pltpu.VMEM((local, depth), bf16), pltpu.SemaphoreType.DMA((4,))],
        compiler_params=pltpu.CompilerParams(vmem_limit_bytes=60 << 20),
        cost_estimate=cost(3),
        name="pack",
    )(own, hidden_bias, tokens, hidden_weight, mixer_weight, output_weight)


def unpack_bias(entries):
    wide = entries.astype(f32)
    wide = wide[:, :128] + wide[:, 128:256] + wide[:, 256:384]
    return jnp.concatenate([wide[index : index + 1] for index in range(6)], axis=1)


def prepare_kernel(query_ref, key_ref, value_ref, joined_ref):
    joined_ref[...] = jnp.concatenate([query_ref[...].T, key_ref[...].T, value_ref[...].T], axis=1)


def prepare(weights):
    width, depth = weights[0].shape
    vmem = pl.BlockSpec(memory_space=pltpu.VMEM)
    return pl.pallas_call(
        prepare_kernel,
        in_specs=[vmem] * 3,
        out_specs=vmem,
        out_shape=jax.ShapeDtypeStruct((depth, 3 * width), bf16),
        compiler_params=pltpu.CompilerParams(vmem_limit_bytes=4 << 20),
        cost_estimate=cost(4),
        name="prepare",
    )(*weights)


def lanes(index, size):
    return pl.ds(pl.multiple_of(index * size, size), size)


def segments(lengths_ref, count, shape):
    places = lax.broadcasted_iota(jnp.int32, shape, len(shape) - 1)
    seg = jnp.zeros(shape, jnp.int32)
    end = jnp.int32(0)
    for s in range(count):
        end = end + lengths_ref[0, s]
        seg = seg + (places >= end).astype(jnp.int32)
    return seg


def masked_copies(seg, entries, count):
    zero = jnp.zeros_like(entries)
    return [jnp.where(seg == s, entries, zero) for s in range(count)]


def one_hot_rows(seg, count):
    rows = lax.broadcasted_iota(jnp.int32, (8, seg.shape[1]), 0)
    return jnp.where((rows == seg) & (rows < count), 1.0, 0.0).astype(f32)


def masked_sum(seg, wide, count):
    height = HEAD_DIM
    total = jnp.zeros((height, wide.shape[1]), f32)
    for s in range(count):
        total = total + jnp.where(seg == s, wide[s * height : (s + 1) * height], 0.0)
    return total


def feature_rows(vectors, proj_t):
    scale = HEAD_DIM ** (-0.25)
    widened = vectors.astype(f32)
    square = (0.5 * scale * scale) * jnp.sum(widened * widened, axis=0, keepdims=True)
    return (jnp.exp(scale * dot(proj_t, vectors) - square) * (1.0 / math.sqrt(FEAT))).astype(bf16)


def attend_kernel(
    count,
    lengths_ref,
    place_ref,
    x0_ref,
    x1_ref,
    x2_ref,
    x3_ref,
    query_weight_ref,
    key_weight_ref,
    value_weight_ref,
    query_bias_ref,
    key_bias_ref,
    value_bias_ref,
    proj_ref,
    qkv_ref,
    qf_ref,
    kf_ref,
    state_ref,
    out_ref,
    den_ref,
    p0_ref,
    p1_ref,
    p2_ref,
    p3_ref,
    mixed_ref,
):
    h = pl.program_id(0)
    tokens = (x0_ref, x1_ref, x2_ref, x3_ref)
    shards, local = len(tokens), x0_ref.shape[1]
    heads = pl.num_programs(0)
    width = query_weight_ref.shape[0]
    spread_rows = count * HEAD_DIM

    @pl.when(h == 0)
    def _():
        for kind, (weight, bias) in enumerate(
            (
                (query_weight_ref, query_bias_ref),
                (key_weight_ref, key_bias_ref),
                (value_weight_ref, value_bias_ref),
            )
        ):
            column = jnp.broadcast_to(bias[...], (8, width)).T[:, 0:1]
            for s in range(shards):
                qkv_ref[kind * width : (kind + 1) * width, lanes(lax.bitwise_xor(place_ref[0], s), local)] = (
                    dot(weight[...], tokens[s][...]) + column
                ).astype(bf16)

    def rows(kind):
        begin = pl.multiple_of(kind * width + h * HEAD_DIM, HEAD_DIM)
        return qkv_ref[pl.ds(begin, HEAD_DIM), :]

    seg = segments(lengths_ref, count, (1, shards * local))
    hot = one_hot_rows(seg, count)
    proj_t = proj_ref[0].T
    q_feat = feature_rows(rows(0), proj_t)
    k_feat = feature_rows(rows(1), proj_t)
    qf_ref[0] = q_feat
    kf_ref[0] = k_feat
    wide = jnp.concatenate(
        masked_copies(seg, rows(2), count) + [jnp.concatenate([hot, hot], axis=0).astype(bf16)], axis=0
    )
    state = dot_cols(wide, k_feat)
    sums = state[spread_rows : spread_rows + 8]
    high = sums.astype(bf16).astype(f32)
    state_ref[0, :spread_rows] = state[:spread_rows].astype(bf16)
    state_ref[0, spread_rows : spread_rows + 16] = jnp.concatenate([high, high], axis=0).astype(bf16)
    state_ref[0, spread_rows + 16 :] = jnp.concatenate(
        [sums - high, jnp.zeros_like(high)], axis=0
    ).astype(bf16)
    through = dot(state_ref[0], q_feat)
    scores = through[spread_rows : spread_rows + 8] + through[spread_rows + 16 : spread_rows + 24]
    den = jnp.sum(hot * scores, axis=0, keepdims=True) + (seg >= count).astype(f32)
    out = masked_sum(seg, through, count) / den
    out_ref[...] = out
    den_ref[0] = jnp.broadcast_to(den, den_ref.shape[1:])
    mixed_ref[pl.ds(pl.multiple_of(h * HEAD_DIM, HEAD_DIM), HEAD_DIM), :] = out.astype(bf16)

    @pl.when(h == heads - 1)
    def _():
        for s, piece in enumerate((p0_ref, p1_ref, p2_ref, p3_ref)):
            piece[...] = mixed_ref[:, lanes(lax.bitwise_xor(place_ref[0], s), local)]


def attend(tokens, weights, biases, proj, lengths, place):
    shards, local, depth = len(tokens), tokens[0].shape[1], weights[0].shape[1]
    heads, head_dim, feat = proj.shape
    total = shards * local
    count = lengths.shape[1] - 1
    width = heads * head_dim
    state_rows = count * head_dim + 32
    smem = pl.BlockSpec(memory_space=pltpu.SMEM)

    def whole(*shape):
        return pl.BlockSpec(shape, lambda h: (0,) * len(shape))

    def per_head(*shape):
        return pl.BlockSpec((1,) + shape, lambda h: (h,) + (0,) * len(shape))

    return pl.pallas_call(
        functools.partial(attend_kernel, count),
        grid=(heads,),
        in_specs=[
            smem,
            smem,
        ]
        + [whole(depth, local)] * shards
        + [whole(width, depth)] * 3
        + [whole(1, width)] * 3
        + [per_head(head_dim, feat)],
        out_specs=[
            whole(3 * width, total),
            per_head(feat, total),
            per_head(feat, total),
            per_head(state_rows, feat),
            pl.BlockSpec((head_dim, total), lambda h: (h, 0)),
            per_head(8, total),
        ]
        + [whole(width, local)] * shards,
        out_shape=[
            jax.ShapeDtypeStruct((3 * width, total), bf16),
            jax.ShapeDtypeStruct((heads, feat, total), bf16),
            jax.ShapeDtypeStruct((heads, feat, total), bf16),
            jax.ShapeDtypeStruct((heads, state_rows, feat), bf16),
            jax.ShapeDtypeStruct((width, total), f32),
            jax.ShapeDtypeStruct((heads, 8, total), f32),
        ]
        + [jax.ShapeDtypeStruct((width, local), bf16)] * shards,
        scratch_shapes=[pltpu.VMEM((width, total), bf16)],
        compiler_params=pltpu.CompilerParams(vmem_limit_bytes=16 << 20),
        cost_estimate=cost(8),
        name="attend",
    )(lengths, place, *tokens, *weights, *biases, proj)


def feature_back_rows(grad_feat, feat, vectors, proj_w):
    scale = HEAD_DIM ** (-0.25)
    grad_proj = grad_feat * feat.astype(f32)
    pulled = scale * dot(proj_w, grad_proj.astype(bf16))
    return pulled - (scale * scale) * vectors.astype(f32) * jnp.sum(grad_proj, axis=0, keepdims=True)


def attend_back_kernel(
    count,
    lengths_ref,
    place_ref,
    qkv_ref,
    qf_ref,
    kf_ref,
    state_ref,
    out_ref,
    den_ref,
    g0_ref,
    g1_ref,
    g2_ref,
    g3_ref,
    proj_ref,
    weight_ref,
    sums_ref,
    grad_ref,
    send_ref,
    keep_ref,
    heads_ref,
    small_ref,
):
    h = pl.program_id(0)
    width, local = g0_ref.shape
    shards = grad_ref.shape[1] // local
    depth = weight_ref.shape[0]
    heads = pl.num_programs(0)
    spread_rows = count * HEAD_DIM

    @pl.when(h == 0)
    def _():
        for s, piece in enumerate((g0_ref, g1_ref, g2_ref, g3_ref)):
            heads_ref[:, lanes(lax.bitwise_xor(place_ref[0], s), local)] = piece[...]

    def at(kind):
        return pl.ds(pl.multiple_of(kind * width + h * HEAD_DIM, HEAD_DIM), HEAD_DIM)

    seg = segments(lengths_ref, count, (1, shards * local))
    hot = one_hot_rows(seg, count)
    query, key, value = qkv_ref[at(0), :], qkv_ref[at(1), :], qkv_ref[at(2), :]
    q_feat, k_feat = qf_ref[0], kf_ref[0]
    grad_head = heads_ref[pl.ds(pl.multiple_of(h * HEAD_DIM, HEAD_DIM), HEAD_DIM), :].astype(f32)
    den = den_ref[0, 0:1, :]
    grad_numer = (grad_head / den).astype(bf16)
    grad_den = -jnp.sum(grad_head * out_ref[...], axis=0, keepdims=True) / den
    marked = hot * grad_den
    high = marked.astype(bf16).astype(f32)
    low = marked - high
    numer_wide = jnp.concatenate(
        masked_copies(seg, grad_numer, count)
        + [
            jnp.concatenate([high, low], axis=0).astype(bf16),
            jnp.concatenate([high, jnp.zeros_like(high)], axis=0).astype(bf16),
        ],
        axis=0,
    )
    grad_state = dot_cols(numer_wide[: spread_rows + 16], q_feat)
    sums = grad_state[spread_rows : spread_rows + 8] + grad_state[spread_rows + 8 : spread_rows + 16]
    sums_high = sums.astype(bf16).astype(f32)
    grad_state = jnp.concatenate(
        [
            grad_state[:spread_rows].astype(bf16),
            jnp.concatenate([sums_high, sums - sums_high], axis=0).astype(bf16),
        ],
        axis=0,
    )
    value_wide = jnp.concatenate(
        masked_copies(seg, value, count) + [jnp.concatenate([hot, hot], axis=0).astype(bf16)], axis=0
    )
    proj_w = proj_ref[0]
    grad_qfeat = dot_rows(state_ref[0], numer_wide)
    grad_ref[at(0), :] = feature_back_rows(grad_qfeat, q_feat, query, proj_w).astype(bf16)
    grad_kfeat = dot_rows(grad_state, value_wide)
    grad_ref[at(1), :] = feature_back_rows(grad_kfeat, k_feat, key, proj_w).astype(bf16)
    grad_ref[at(2), :] = masked_sum(seg, dot(grad_state[:spread_rows], k_feat), count).astype(bf16)

    @pl.when(h == heads - 1)
    def _():
        small_ref[...] = sums_ref[...]
        totals = dot_cols(jnp.ones((8, shards * local), bf16), grad_ref[...])
        for t in range(shards):

            @pl.when(place_ref[0] == t)
            def _():
                for kind, row in enumerate(BIAS_ROWS):
                    small_ref[row : row + 1, t * width : (t + 1) * width] = totals[
                        0:1, kind * width : (kind + 1) * width
                    ]

        small = jnp.concatenate(
            [small_ref[:, begin : begin + local] for begin in range(0, depth, local)], axis=0
        )
        rows = small.shape[0]
        high = small.astype(bf16)
        low = (small - high.astype(f32)).astype(bf16)
        for s in range(shards):
            out = (keep_ref, send_ref)[s % 2].at[s // 2]
            out[:depth] = dot(
                weight_ref[...], grad_ref[:, lanes(lax.bitwise_xor(place_ref[0], s), local)]
            ).astype(bf16)
            out[depth : depth + rows] = high
            out[depth + rows :] = low


def attend_back(saved, pieces, proj, weight, sums, lengths, place):
    qkv, qf, kf, state, out, den = saved
    heads, feat, total = qf.shape
    width, local = pieces[0].shape
    shards = total // local
    depth = weight.shape[0]
    count = lengths.shape[1] - 1
    state_rows = state.shape[1]
    extra = 2 * sums.shape[0] * (depth // local)
    smem = pl.BlockSpec(memory_space=pltpu.SMEM)

    def whole(*shape):
        return pl.BlockSpec(shape, lambda h: (0,) * len(shape))

    def per_head(*shape):
        return pl.BlockSpec((1,) + shape, lambda h: (h,) + (0,) * len(shape))

    return pl.pallas_call(
        functools.partial(attend_back_kernel, count),
        grid=(heads,),
        in_specs=[
            smem,
            smem,
            whole(3 * width, total),
            per_head(feat, total),
            per_head(feat, total),
            per_head(state_rows, feat),
            pl.BlockSpec((HEAD_DIM, total), lambda h: (h, 0)),
            per_head(8, total),
        ]
        + [whole(width, local)] * shards
        + [per_head(HEAD_DIM, feat), whole(depth, 3 * width), whole(*sums.shape)],
        out_specs=[
            whole(3 * width, total),
            whole(shards // 2, depth + extra, local),
            whole(shards // 2, depth + extra, local),
        ],
        out_shape=[
            jax.ShapeDtypeStruct((3 * width, total), bf16),
            jax.ShapeDtypeStruct((shards // 2, depth + extra, local), bf16),
            jax.ShapeDtypeStruct((shards // 2, depth + extra, local), bf16),
        ],
        scratch_shapes=[pltpu.VMEM((width, total), bf16), pltpu.VMEM(sums.shape, f32)],
        compiler_params=pltpu.CompilerParams(vmem_limit_bytes=18 << 20),
        cost_estimate=cost(9),
        name="attend_back",
    )(lengths, place, qkv, qf, kf, state, out, den, *pieces, proj, weight, sums)


def slot_place(slot, half):
    k = slot // 2
    if half == 0:
        return 1 - k % 2, k // 2
    return 1 - k // 2, k % 2


def pick_blocks(own, turned_ref):
    slots = turned_ref.shape[0]
    return jnp.concatenate([turned_ref[lax.bitwise_xor(own, slot)] for slot in range(0, slots, 2)], axis=0)


def emit_slots(entries, outs, begin=0):
    height = outs[0].shape[2]
    count = entries.shape[1]
    for half in range(2):

        @pl.when(pl.program_id(0) // 2 == half)
        def _():
            for k in range(PLANE // 2):
                part, index = slot_place(2 * k, half)
                outs[2 * half + part][index, 0, :, begin : begin + count] = entries[k * height : (k + 1) * height]


def slot_outputs(shards, height, count):
    low = pl.BlockSpec((2, 1, height, count), lambda s: (0, jnp.minimum(s, 1), 0, 0))
    high = pl.BlockSpec((2, 1, height, count), lambda s: (0, jnp.maximum(s - 2, 0), 0, 0))
    shape = jax.ShapeDtypeStruct((2, shards // 2, height, count), bf16)
    return [low, low, high, high], [shape] * 4


def output_grad_kernel(own_ref, turned_ref, turned_far_ref, act_ref, act_far_ref, *outs):
    own = own_ref[0]
    grads = dot(pick_blocks(own, turned_ref), act_ref[0]) + dot(pick_blocks(own, turned_far_ref), act_far_ref[0])
    emit_slots(grads.astype(bf16), outs)


def output_grad(own, turned, turned_far, acts, acts_far):
    shards, rows, hidden = acts.shape
    slots, height, _ = turned.shape
    specs, shapes = slot_outputs(shards, height, hidden)
    whole = pl.BlockSpec((slots, height, rows), lambda s: (0, 0, 0))
    by_shard = pl.BlockSpec((1, rows, hidden), lambda s: (s, 0, 0))
    return pl.pallas_call(
        output_grad_kernel,
        grid=(shards,),
        in_specs=[pl.BlockSpec(memory_space=pltpu.SMEM), whole, whole, by_shard, by_shard],
        out_specs=specs,
        out_shape=shapes,
        compiler_params=pltpu.CompilerParams(vmem_limit_bytes=8 << 20),
        cost_estimate=cost(4),
        name="output_grad",
    )(own, turned, turned_far, acts, acts_far)


def hidden_grad_kernel(
    own_ref,
    first_ref,
    first_far_ref,
    grad_pre_ref,
    grad_pre_far_ref,
    branch_ref,
    branch_far_ref,
    mixed_ref,
    mixed_far_ref,
    *outs,
):
    own = own_ref[0]
    hidden = grad_pre_ref.shape[2]
    grads = dot(pick_blocks(own, first_ref), grad_pre_ref[0]) + dot(
        pick_blocks(own, first_far_ref), grad_pre_far_ref[0]
    )
    emit_slots(grads.astype(bf16), outs)
    grads = dot_cols(pick_blocks(own, branch_ref), mixed_ref[0]) + dot_cols(
        pick_blocks(own, branch_far_ref), mixed_far_ref[0]
    )
    emit_slots(grads.astype(bf16), outs, hidden)


def hidden_grad(own, first, first_far, grad_pre, grad_pre_far, branch, branch_far, mixed, mixed_far):
    shards, rows, hidden = grad_pre.shape
    slots, height, _ = first.shape
    width = mixed.shape[1]
    specs, shapes = slot_outputs(shards, height, hidden + width)
    whole = pl.BlockSpec((slots, height, rows), lambda s: (0, 0, 0))
    by_shard = pl.BlockSpec((1, rows, hidden), lambda s: (s, 0, 0))
    piece = pl.BlockSpec((1, width, rows), lambda s: (s, 0, 0))
    return pl.pallas_call(
        hidden_grad_kernel,
        grid=(shards,),
        in_specs=[
            pl.BlockSpec(memory_space=pltpu.SMEM),
            whole,
            whole,
            by_shard,
            by_shard,
            whole,
            whole,
            piece,
            piece,
        ],
        out_specs=specs,
        out_shape=shapes,
        compiler_params=pltpu.CompilerParams(vmem_limit_bytes=10 << 20),
        cost_estimate=cost(5),
        name="hidden_grad",
    )(own, first, first_far, grad_pre, grad_pre_far, branch, branch_far, mixed, mixed_far)


def qkv_grad_kernel(own_ref, place_ref, x0_ref, x1_ref, x2_ref, x3_ref, grad_ref, even_ref, odd_ref, hold_ref):
    local = x0_ref.shape[1]
    depth = hold_ref.shape[0] * hold_ref.shape[1]
    grads = sum(
        dot_cols(block[:depth], grad_ref[:, lanes(lax.bitwise_xor(place_ref[0], s), local)])
        for s, block in enumerate((x0_ref, x1_ref, x2_ref, x3_ref))
    )
    hold_ref[...] = grads.astype(bf16).reshape(hold_ref.shape)
    rows = even_ref.shape[4]
    for slot in range(hold_ref.shape[0]):
        target = odd_ref if slot % 2 else even_ref
        block = hold_ref[lax.bitwise_xor(own_ref[0], slot)]
        for half in range(2):
            target[(half,) + slot_place(slot, half) + (0,)] = block[half * rows : (half + 1) * rows]


def qkv_grad(own, place, slots, depth, tokens, grads):
    count = grads.shape[0]
    vmem = pl.BlockSpec(memory_space=pltpu.VMEM)
    shape = jax.ShapeDtypeStruct((2, 2, slots // 4, 1, depth // slots // 2, count), bf16)
    return pl.pallas_call(
        qkv_grad_kernel,
        in_specs=[pl.BlockSpec(memory_space=pltpu.SMEM)] * 2 + [vmem] * (len(tokens) + 1),
        out_specs=[vmem, vmem],
        out_shape=[shape, shape],
        scratch_shapes=[pltpu.VMEM((slots, depth // slots, count), bf16)],
        compiler_params=pltpu.CompilerParams(vmem_limit_bytes=9 << 20),
        cost_estimate=cost(2),
        name="qkv_grad",
    )(own, place, *tokens, grads)


def norm_rows(resid):
    center = resid - jnp.mean(resid, axis=-1, keepdims=True)
    inverse = lax.rsqrt(jnp.mean(center * center, axis=-1, keepdims=True) + eps)
    return center * inverse, inverse


HELD = [(0, (0, 1, 2, 3)), (2, (0, 1, 2, 3)), (4, (0, 1, 2, 3)), (6, (0, 1)), (6, (2, 3))]
HELD = HELD + [(mask ^ 1, shards) for mask, shards in HELD]


def place_copies(own, held, begin, rows, target, sems):
    columns = held[0].shape[2]
    copies = []
    for index, (piece, (mask, shards)) in enumerate(zip(held, HELD)):
        source = lax.bitwise_xor(own, mask)
        chip = lax.shift_right_logical(source, 1)
        core = lax.bitwise_and(source, 1)
        copies.append(
            pltpu.make_async_copy(
                piece.at[:, pl.ds(begin, rows), :],
                target.at[shards[0] : shards[-1] + 1, chip, :, lanes(core, columns)],
                sems.at[index],
            )
        )
    return copies


def start_all(copies):
    for entries in copies:
        for copy in entries:
            copy.start()


def wait_all(entries):
    for copy in entries:
        copy.wait()


def ffn_up_kernel(
    own_ref,
    tokens_ref,
    p0_ref,
    p1_ref,
    p2_ref,
    p3_ref,
    mixer_bias_ref,
    gain_ref,
    shift_ref,
    *refs,
):
    held, refs = refs[: len(HELD)], refs[len(HELD) :]
    parts, refs = refs[:4], refs[4:]
    (
        normed_ref,
        inverse_ref,
        turned_ref,
        mixed_ref,
        act_ref,
        slope_ref,
        mixer_ref,
        hidden_ref,
        bias_ref,
        mixer_sem,
        hidden_sem,
        bias_sem,
    ) = refs
    own = own_ref[0]
    shards, chips, mixer_rows, depth = mixer_ref.shape
    hidden_rows = hidden_ref.shape[2]
    mixer_copies = place_copies(own, held, hidden_rows, mixer_rows, mixer_ref, mixer_sem)
    hidden_copies = place_copies(own, held, 0, hidden_rows, hidden_ref, hidden_sem)
    bias_rows = parts[0].shape[0] - 16
    bias_copies = [
        pltpu.make_async_copy(part.at[bias_rows : bias_rows + 16], bias_ref.at[s], bias_sem.at[s])
        for s, part in enumerate(parts)
    ]
    start_all([mixer_copies, bias_copies, hidden_copies])
    resid = tokens_ref[...].astype(f32) + mixer_bias_ref[...]
    for s, piece in enumerate((p0_ref, p1_ref, p2_ref, p3_ref)):
        mixed_ref[s] = piece[...]
        if s == 0:
            wait_all(mixer_copies)
        resid = resid + dot_rows(piece[...], mixer_ref[s].reshape(chips * mixer_rows, depth))
    normed, inverse = norm_rows(resid)
    normed_ref[...] = normed
    inverse_ref[...] = jnp.broadcast_to(inverse, inverse_ref.shape)
    first_low = (normed * gain_ref[...] + shift_ref[...]).astype(bf16)
    turned_ref[...] = first_low.T
    for s in range(shards):
        if s == 0:
            wait_all(hidden_copies + bias_copies)
        bias = unpack_bias(bias_ref[s])
        pre = dot(first_low, hidden_ref[s].reshape(chips * hidden_rows, hidden_ref.shape[3])) + bias
        phi = 0.5 * (1.0 + lax.erf(pre * math.sqrt(0.5)))
        act_ref[s] = (pre * phi).astype(bf16)
        slope_ref[s] = (
            phi + pre * jnp.exp(-0.5 * pre * pre) * (1.0 / math.sqrt(2.0 * math.pi))
        ).astype(bf16)


def ffn_up(own, tokens, pieces, mixer_bias, gain, shift_by, parts, held, mixer_rows):
    rows, depth = tokens.shape
    shards = len(pieces)
    chips = PLANE // 2
    hidden = 2 * held[0].shape[2]
    hidden_rows = held[0].shape[1] - mixer_rows
    vmem = pl.BlockSpec(memory_space=pltpu.VMEM)
    return pl.pallas_call(
        ffn_up_kernel,
        in_specs=[pl.BlockSpec(memory_space=pltpu.SMEM)]
        + [vmem] * (1 + shards + 3)
        + [pl.BlockSpec(memory_space=pl.ANY)] * (len(HELD) + shards),
        out_specs=[vmem] * 6,
        out_shape=[
            jax.ShapeDtypeStruct((rows, depth), f32),
            jax.ShapeDtypeStruct((rows, 128), f32),
            jax.ShapeDtypeStruct((depth, rows), bf16),
            jax.ShapeDtypeStruct((shards,) + pieces[0].shape, bf16),
            jax.ShapeDtypeStruct((shards, rows, hidden), bf16),
            jax.ShapeDtypeStruct((shards, rows, hidden), bf16),
        ],
        scratch_shapes=[
            pltpu.VMEM((shards, chips, mixer_rows, depth), bf16),
            pltpu.VMEM((shards, chips, hidden_rows, hidden), bf16),
            pltpu.VMEM((shards, 16, held[0].shape[2]), bf16),
            pltpu.SemaphoreType.DMA((len(HELD),)),
            pltpu.SemaphoreType.DMA((len(HELD),)),
            pltpu.SemaphoreType.DMA((shards,)),
        ],
        compiler_params=pltpu.CompilerParams(vmem_limit_bytes=17 << 20),
        cost_estimate=cost(8),
        name="ffn_up",
    )(own, tokens, *pieces, mixer_bias, gain, shift_by, *held, *parts)


def norm_rows_back(scaled, normed, inverse):
    return inverse * (
        scaled
        - jnp.mean(scaled, axis=-1, keepdims=True)
        - normed * jnp.mean(scaled * normed, axis=-1, keepdims=True)
    )


def column_sum(entries):
    return jnp.sum(entries, axis=0, keepdims=True)


def ffn_down_kernel(
    own_ref,
    normed_ref,
    inverse_ref,
    act_ref,
    slope_ref,
    cotangent_ref,
    first_gain_ref,
    first_shift_ref,
    output_bias_ref,
    gain_ref,
    shift_ref,
    *refs,
):
    held, refs = refs[: len(HELD)], refs[len(HELD) :]
    held_out, refs = refs[: len(HELD)], refs[len(HELD) :]
    (
        layer_ref,
        resid_ref,
        b0_ref,
        b1_ref,
        b2_ref,
        b3_ref,
        grad_ffn_ref,
        grad_pre_ref,
        grad_branch_ref,
        sums_ref,
        mixer_ref,
        hidden_ref,
        output_ref,
        mixer_sem,
        hidden_sem,
        output_sem,
    ) = refs
    own, place = own_ref[0], own_ref[1]
    shards, chips, mixer_rows, depth = mixer_ref.shape
    hidden_rows = hidden_ref.shape[2]
    hidden = hidden_ref.shape[3]
    output_copies = place_copies(own, held_out, 0, output_ref.shape[2], output_ref, output_sem)
    hidden_copies = place_copies(own, held, 0, hidden_rows, hidden_ref, hidden_sem)
    mixer_copies = place_copies(own, held, hidden_rows, mixer_rows, mixer_ref, mixer_sem)
    start_all([output_copies, hidden_copies, mixer_copies])
    normed_one = normed_ref[...]
    resid = normed_one * first_gain_ref[...] + first_shift_ref[...] + output_bias_ref[...]
    wait_all(output_copies)
    for s in range(shards):
        resid = resid + dot(act_ref[s], output_ref[s].reshape(hidden, depth))
    normed, inverse = norm_rows(resid)
    layer_ref[...] = (normed * gain_ref[...] + shift_ref[...]).astype(bf16)
    grad_out = cotangent_ref[...].astype(f32)
    sums_ref[0:1] = column_sum(grad_out * normed)
    sums_ref[1:2] = column_sum(grad_out)
    grad_two = norm_rows_back(grad_out * gain_ref[...], normed, inverse)
    grad_ffn = grad_two.astype(bf16)
    grad_ffn_ref[...] = grad_ffn.T
    sums_ref[2:3] = column_sum(grad_ffn.astype(f32))
    grad_first = grad_two
    for s in range(shards):
        grad_pre = (
            dot_cols(grad_ffn, output_ref[s].reshape(hidden, depth)) * slope_ref[s].astype(f32)
        ).astype(bf16)
        grad_pre_ref[s] = grad_pre
        sums_ref[pl.ds(8 + lax.bitwise_xor(place, s), 1)] = column_sum(grad_pre.astype(f32))
        if s == 0:
            wait_all(hidden_copies)
        grad_first = grad_first + dot_cols(grad_pre, hidden_ref[s].reshape(depth, hidden))
    sums_ref[3:4] = column_sum(grad_first * normed_one)
    sums_ref[4:5] = column_sum(grad_first)
    grad_one = norm_rows_back(grad_first * first_gain_ref[...], normed_one, inverse_ref[:, 0:1])
    resid_ref[...] = grad_one
    grad_branch = grad_one.astype(bf16)
    branch_turned = grad_branch.T
    grad_branch_ref[...] = branch_turned
    sums_ref[5:6] = column_sum(grad_branch.astype(f32))
    sums_ref[6:8] = jnp.zeros((2, depth), f32)
    sums_ref[8 + shards :] = jnp.zeros((8 - shards, depth), f32)
    for s, back in enumerate((b0_ref, b1_ref, b2_ref, b3_ref)):
        if s == 0:
            wait_all(mixer_copies)
        back[...] = dot(mixer_ref[s].reshape(chips * mixer_rows, depth), branch_turned).astype(bf16)


def ffn_down(own, normed, inverse, acts, slopes, cotangent, vectors, held, held_out, mixer_rows):
    rows, depth = normed.shape
    shards, _, hidden = acts.shape
    chips = PLANE // 2
    hidden_rows = held[0].shape[1] - mixer_rows
    output_rows = held_out[0].shape[1]
    vmem = pl.BlockSpec(memory_space=pltpu.VMEM)
    width = chips * mixer_rows
    return pl.pallas_call(
        ffn_down_kernel,
        in_specs=[pl.BlockSpec(memory_space=pltpu.SMEM)]
        + [vmem] * 10
        + [pl.BlockSpec(memory_space=pl.ANY)] * (2 * len(HELD)),
        out_specs=[vmem] * (6 + shards),
        out_shape=[
            jax.ShapeDtypeStruct((rows, depth), bf16),
            jax.ShapeDtypeStruct((rows, depth), f32),
        ]
        + [jax.ShapeDtypeStruct((width, rows), bf16)] * shards
        + [
            jax.ShapeDtypeStruct((depth, rows), bf16),
            jax.ShapeDtypeStruct((shards, rows, hidden), bf16),
            jax.ShapeDtypeStruct((depth, rows), bf16),
            jax.ShapeDtypeStruct((16, depth), f32),
        ],
        scratch_shapes=[
            pltpu.VMEM((shards, chips, mixer_rows, depth), bf16),
            pltpu.VMEM((shards, chips, hidden_rows, hidden), bf16),
            pltpu.VMEM((shards, chips, output_rows, depth), bf16),
            pltpu.SemaphoreType.DMA((len(HELD),)),
            pltpu.SemaphoreType.DMA((len(HELD),)),
            pltpu.SemaphoreType.DMA((len(HELD),)),
        ],
        compiler_params=pltpu.CompilerParams(vmem_limit_bytes=24 << 20),
        cost_estimate=cost(15),
        name="ffn_down",
    )(own, normed, inverse, acts, slopes, cotangent, *vectors, *held, *held_out)


def fold_kernel(depth, keep_ref, far_ref, mine_ref, other_ref):
    rows = (keep_ref.shape[1] - depth) // 2
    for s, out in enumerate((mine_ref, other_ref)):
        out[:depth] = (keep_ref[s, :depth].astype(f32) + far_ref[s, :depth].astype(f32)).astype(bf16)
        small = sum(
            ref[s, depth : depth + rows].astype(f32) + ref[s, depth + rows :].astype(f32) for ref in (keep_ref, far_ref)
        )
        high = small.astype(bf16)
        out[depth : depth + rows] = high
        out[depth + rows :] = (small - high.astype(f32)).astype(bf16)


def fold(depth, keep, far):
    vmem = pl.BlockSpec(memory_space=pltpu.VMEM)
    return pl.pallas_call(
        functools.partial(fold_kernel, depth),
        in_specs=[vmem] * 2,
        out_specs=[vmem] * 2,
        out_shape=[jax.ShapeDtypeStruct(keep.shape[1:], bf16)] * 2,
        compiler_params=pltpu.CompilerParams(vmem_limit_bytes=6 << 20),
        cost_estimate=cost(0),
        name="fold",
    )(keep, far)


def join_cores_kernel(near_ref, far_ref, *outs):
    for half in range(2):
        for part in range(2):
            outs[2 * half + part][...] = (
                near_ref[half, part].astype(f32) + far_ref[half, part].astype(f32)
            ).astype(bf16)


def join_cores(near, far):
    vmem = pl.BlockSpec(memory_space=pltpu.VMEM)
    return pl.pallas_call(
        join_cores_kernel,
        in_specs=[vmem] * 2,
        out_specs=[vmem] * 4,
        out_shape=[jax.ShapeDtypeStruct(near.shape[2:], bf16)] * 4,
        compiler_params=pltpu.CompilerParams(vmem_limit_bytes=4 << 20),
        cost_estimate=cost(0),
        name="join_cores",
    )(near, far)


def finish_tokens_kernel(resid_ref, mine_ref, far_ref, out_ref, small_ref):
    depth = resid_ref.shape[1]
    rows = small_ref.shape[0]
    total = mine_ref[:depth].astype(f32) + far_ref[:depth].astype(f32)
    out_ref[...] = resid_ref[...] + total.T
    small_ref[...] = sum(
        ref[depth : depth + rows].astype(f32) + ref[depth + rows :].astype(f32) for ref in (mine_ref, far_ref)
    )


def finish_tokens(resid, mine, far):
    local, depth = resid.shape
    rows = (mine.shape[0] - depth) // 2
    vmem = pl.BlockSpec(memory_space=pltpu.VMEM)
    return pl.pallas_call(
        finish_tokens_kernel,
        in_specs=[vmem] * 3,
        out_specs=[vmem] * 2,
        out_shape=[jax.ShapeDtypeStruct(resid.shape, f32), jax.ShapeDtypeStruct((rows, local), f32)],
        compiler_params=pltpu.CompilerParams(vmem_limit_bytes=6 << 20),
        cost_estimate=cost(0),
        name="finish_tokens",
    )(resid, mine, far)


def finish_hidden_kernel(a_ref, b_ref, hidden_ref, mixer_ref):
    total = a_ref[...].astype(f32) + b_ref[...].astype(f32)
    hidden = hidden_ref.shape[1]
    hidden_ref[...] = total[:, :hidden]
    mixer_ref[...] = total[:, hidden:].T


def finish_hidden(entries, hidden):
    rows, columns = entries[0].shape
    vmem = pl.BlockSpec(memory_space=pltpu.VMEM)
    return pl.pallas_call(
        finish_hidden_kernel,
        in_specs=[vmem] * 2,
        out_specs=[vmem] * 2,
        out_shape=[
            jax.ShapeDtypeStruct((rows, hidden), f32),
            jax.ShapeDtypeStruct((columns - hidden, rows), f32),
        ],
        compiler_params=pltpu.CompilerParams(vmem_limit_bytes=4 << 20),
        cost_estimate=cost(0),
        name="finish_hidden",
    )(*entries)


def finish_qkv_kernel(a_ref, b_ref, c_ref, d_ref, query_ref, key_ref, value_ref):
    rows, width = a_ref.shape[0], query_ref.shape[1]
    low = a_ref[...].astype(f32) + b_ref[...].astype(f32)
    high = c_ref[...].astype(f32) + d_ref[...].astype(f32)
    for kind, out in enumerate((query_ref, key_ref, value_ref)):
        out[:rows] = low[:, kind * width : (kind + 1) * width]
        out[rows:] = high[:, kind * width : (kind + 1) * width]


def finish_qkv(entries):
    rows, columns = entries[0].shape
    vmem = pl.BlockSpec(memory_space=pltpu.VMEM)
    return pl.pallas_call(
        finish_qkv_kernel,
        in_specs=[vmem] * 4,
        out_specs=[vmem] * 3,
        out_shape=[jax.ShapeDtypeStruct((2 * rows, columns // 3), f32)] * 3,
        compiler_params=pltpu.CompilerParams(vmem_limit_bytes=3 << 20),
        cost_estimate=cost(0),
        name="finish_qkv",
    )(*entries)


BIAS_ROWS = (6, 7, 12)


def swap(values, mask):
    size = lax.axis_size("dp")
    return lax.ppermute(values, "dp", [(i, i ^ mask) for i in range(size)])


def cross(values, mask):
    size = lax.axis_size("tensor")
    return lax.ppermute(values, "tensor", [(i, i ^ mask) for i in range(size)])


def after(values, *others):
    return lax.optimization_barrier((values, others))[0]


def from_neighbours(payload):
    return cross(payload, 1), cross(payload, 2)


def all_shards(payload, near, far):
    return [payload, near, far, cross(far, 1)]


def spread_plane(stack, between=()):
    over_x, over_y = after((swap(stack, 2), swap(stack, 4)), *between)
    return [stack, over_x, over_y, swap(over_x[:2], 4), swap(over_y[2:], 2)]


def other_core(held, before=()):
    return [swap(entry, 1) for entry in after(held, *before)]


def add_low(*entries):
    return sum(entry.astype(f32) for entry in entries).astype(bf16)


def sum_first(near, before=(), between=()):
    send_low, keep_low, send_high, keep_high = near
    send_low, send_high = after((send_low, send_high), *before)
    low, high = after((swap(send_low, 2), swap(send_high, 4)), *between)
    return (
        [add_low(keep_low[0], low[0]), add_low(keep_high[0], high[0])],
        [add_low(keep_low[1], low[1]), add_low(keep_high[1], high[1])],
    )


def sum_second(stay, send, between=()):
    low, high = after((swap(send[0], 4), swap(send[1], 2)), *between)
    return [add_low(stay[0], low), add_low(stay[1], high)]


def scatter_all(halves, axis):
    parts = []
    for half in range(2):
        blocks = []
        for i in range(PLANE):
            part, index = slot_place(i, half)
            blocks.append(halves[i % 2][2 * half + part][index])
        parts.append(jnp.stack(blocks, axis=1))
    whole = jnp.concatenate(parts, axis=axis)
    whole = whole.reshape(whole.shape[:1] + (-1,) + whole.shape[-1:])
    return lax.psum_scatter(whole, "dp", scatter_dimension=1, tiled=True)


def pair_shards(grads):
    return after(jnp.stack([grads[1], grads[3]]))


def join_shards(grads, pair, between=()):
    near = after(cross(pair, 1), *between)
    mine, other = add_low(grads[0], near[0]), add_low(grads[2], near[1])
    return mine, cross(other, 2)


def by_shard(halves):
    return [half[s] for half in halves for s in range(half.shape[0])]


def small_sum(values):
    size = lax.axis_size("dp")
    if size != PLANE:
        values = lax.psum(values, "dp")
    else:
        for mask in (1, 2, 4):
            values = values + swap(values, mask)
    return values


def body(
    tokens,
    lengths,
    query_weight,
    query_bias,
    key_weight,
    key_bias,
    value_weight,
    value_bias,
    feature_proj,
    mixer_weight,
    mixer_bias,
    first_gain,
    first_shift,
    hidden_weight,
    hidden_bias,
    output_weight,
    output_bias,
    second_gain,
    second_shift,
    cotangent,
):
    depth = tokens.shape[1]
    shards = lax.axis_size("tensor")
    place = lax.axis_index("tensor").astype(jnp.int32)
    plane = (lax.axis_index("dp") % PLANE).astype(jnp.int32)
    width = query_weight.shape[1]
    hidden = hidden_weight.shape[1]
    mixer_rows = mixer_weight.shape[0] // (PLANE // 2)
    own = jnp.stack([plane, place])
    slot_of = plane[None] if lax.axis_size("dp") == PLANE else jnp.zeros((1,), jnp.int32)

    def row(vector):
        return vector.reshape(1, -1)

    def blocks(turned):
        return turned.reshape(PLANE, turned.shape[0] // PLANE, turned.shape[1])

    payload, payload_out, turned = pack(
        own, tokens, hidden_bias.reshape(-1, 128), hidden_weight, mixer_weight, output_weight
    )
    near, far = from_neighbours(payload)
    parts = all_shards(payload, near, far)
    near_out, far_out = from_neighbours(after(payload_out, far))
    parts_out = all_shards(payload_out, near_out, far_out)
    near, far = from_neighbours(after(turned, parts[3]))
    weights = [query_weight.T, key_weight.T, value_weight.T]
    qkv_weight = prepare(after(weights, payload))
    rows = payload.shape[0] - 16
    stack = jnp.stack([part[:rows] for part in parts])
    stack_far = swap(stack, 1)
    stack_out = jnp.stack(parts_out)
    around = spread_plane(stack, between=(near, far, qkv_weight, stack_far, stack_out))
    tokens_all = all_shards(turned, near, far)
    crossed = [stack_far] + other_core(around[1:3])
    tokens_all = after(tokens_all, *crossed, *around[3:])
    *saved, p0, p1, p2, p3 = attend(
        tokens_all,
        weights,
        [row(query_bias), row(key_bias), row(value_bias)],
        feature_proj,
        lengths,
        place[None],
    )
    around_out = spread_plane(stack_out, between=(p0,))
    pieces = [p0] + [cross(p, s) for s, p in ((1, p1), (2, p2), (3, p3))]
    held = around + crossed + other_core(around[3:])
    held_out = around_out + other_core(around_out[:3], pieces) + other_core(around_out[3:])
    normed, inverse, turned, mixed, acts, slopes = ffn_up(
        own, tokens, pieces, row(mixer_bias), row(first_gain), row(first_shift), parts, held, mixer_rows
    )
    acts_far, turned_far, mixed_far = swap(acts, 1), swap(turned, 1), swap(mixed, 1)
    held_out = after(held_out, turned_far, mixed_far)
    vectors = [row(v) for v in (first_gain, first_shift, output_bias, second_gain, second_shift)]
    layer_out, grad_resid, b0, b1, b2, b3, grad_ffn, grad_pre, grad_branch, sums = ffn_down(
        own, normed, inverse, acts, slopes, cotangent, vectors, held, held_out, mixer_rows
    )
    back = [b0] + [cross(b, s) for s, b in ((1, b1), (2, b2), (3, b3))]
    output_work = (blocks(grad_ffn), blocks(swap(grad_ffn, 1)), acts, acts_far)
    hidden_work = (
        blocks(turned),
        blocks(turned_far),
        grad_pre,
        swap(grad_pre, 1),
        blocks(grad_branch),
        blocks(swap(grad_branch, 1)),
        mixed,
        mixed_far,
    )
    fast = lax.axis_size("dp") == PLANE
    if fast:
        near_output = output_grad(slot_of, *output_work)
        near_output = after(near_output, hidden_work)
        near_hidden = hidden_grad(slot_of, *hidden_work)
        back = after(back, near_output, near_hidden)
    grad_qkv, send, keep = attend_back(
        saved, back, feature_proj, qkv_weight, sums, lengths, place[None]
    )
    far = cross(send, 1)
    if fast:
        even, odd = qkv_grad(slot_of, place[None], PLANE, depth, tokens_all, grad_qkv)
        stay_output, send_output = sum_first(near_output, between=(even,))
        stay_hidden, send_hidden = sum_first(near_hidden, between=send_output)
        near_qkv = join_cores(even, after(swap(odd, 1), send_hidden))
        mine, other = fold(depth, keep, after(far, near_qkv))
        far = cross(other, 2)
        grad_output = by_shard(sum_second(stay_output, send_output, between=(other,)))
        pair_output = pair_shards(grad_output)
        grad_hidden = by_shard(sum_second(stay_hidden, send_hidden, between=(pair_output,)))
        pair_hidden = pair_shards(grad_hidden)
        stay_qkv, send_qkv = sum_first(near_qkv, between=(pair_hidden,))
        grad_output = join_shards(grad_output, pair_output, send_qkv)
        low, high = swap(send_qkv[0], 4), swap(send_qkv[1], 2)
        grad_weights = finish_qkv([entry[0] for entry in (stay_qkv[0], low, stay_qkv[1], high)])
        grad_hidden = join_shards(grad_hidden, pair_hidden, grad_weights)
    else:
        zero, one = jnp.zeros((1,), jnp.int32), jnp.ones((1,), jnp.int32)
        mine, other = fold(depth, keep, far)
        far = cross(other, 2)
        grad_output = scatter_all([output_grad(slot, *output_work) for slot in (zero, one)], 0)
        grad_output = by_shard([0.5 * grad_output])
        grad_output = join_shards(grad_output, pair_shards(grad_output))
        grad_hidden = scatter_all([hidden_grad(slot, *hidden_work) for slot in (zero, one)], 0)
        grad_hidden = by_shard([0.5 * grad_hidden])
        grad_hidden = join_shards(grad_hidden, pair_shards(grad_hidden))
        grad_weight = scatter_all(
            [
                [entry[half, part] for half in range(2) for part in range(2)]
                for entry in qkv_grad(zero, place[None], PLANE, depth, tokens_all, grad_qkv)
            ],
            2,
        )[0].astype(f32)
        grad_weights = [grad_weight[:, kind * width : (kind + 1) * width] for kind in range(3)]
    tokens_grad, small = finish_tokens(grad_resid, mine, far)
    small = small_sum(small)
    small = after(small.reshape(-1, 16, small.shape[1]).transpose(1, 0, 2).reshape(16, -1))
    grad_output = sum(entry.astype(f32) for entry in grad_output).T
    grad_hidden, grad_mixer = finish_hidden(grad_hidden, hidden)
    return (
        layer_out,
        tokens_grad,
        grad_weights[0],
        small[6],
        grad_weights[1],
        small[7],
        grad_weights[2],
        small[12],
        grad_mixer,
        small[5],
        small[3],
        small[4],
        grad_hidden,
        small[8 : 8 + shards].reshape(-1),
        grad_output,
        small[2],
        small[0],
        small[1],
    )


def solution(mesh):
    placed = (
        P(("dp", "tensor"), None),
        P("dp", None),
        P(None, "tensor"),
        P("tensor"),
        P(None, "tensor"),
        P("tensor"),
        P(None, "tensor"),
        P("tensor"),
        P("tensor", None, None),
        P("tensor", None),
        P(),
        P(),
        P(),
        P(None, "tensor"),
        P("tensor"),
        P("tensor", None),
        P(),
        P(),
        P(),
        P(("dp", "tensor"), None),
    )
    return jax.shard_map(
        body,
        mesh=mesh,
        in_specs=placed,
        out_specs=(
            P(("dp", "tensor"), None),
            P(("dp", "tensor"), None),
            P("dp", "tensor"),
            P(),
            P("dp", "tensor"),
            P(),
            P("dp", "tensor"),
            P(),
            P("tensor", "dp"),
            P(),
            P(),
            P(),
            P("dp", "tensor"),
            P(),
            P("tensor", "dp"),
            P(),
            P(),
            P(),
        ),
        check_vma=False,
    )
```
